32 devices in a mesh: dp: 4 (over z), tp: 8 (over y, x, core).
Axes of the slice: x: 2, y: 2, z: 4, core: 2. Of those that a mesh axis runs over, the one named last changes fastest.
Arguments:
- tokens: bfloat16 [8192, 2048], P(('dp', 'tp')), may hold values from -6 to 6
- segment_ids: int32 [8, 1024], P('dp'), may hold values from 0 to 3, as said below
- prefix_lengths: int32 [8, 4], P('dp'), may hold values from 1 to 512, as said below
- positions: int32 [8, 1024], P('dp'), may hold values from 0 to 511, as said below
- norm_gains: float32 [2, 2048], replicated, may hold values from 0.5 to 1.5
- norm_offsets: float32 [2, 2048], replicated, may hold values from -1.75 to 1.75
- input_weight: bfloat16 [2048, 6144], P(None, 'tp'), may hold values from -0.125 to 0.125
- input_offset: float32 [6144], P('tp'), may hold values from -0.625 to 0.625
- output_weight: bfloat16 [2048, 2048], P('tp'), may hold values from -8 to 8
- output_offset: float32 [2048], replicated, may hold values from -3 to 3
- expand_weight: bfloat16 [2048, 2, 5472], P(None, None, 'tp'), may hold values from -0.125 to 0.125
- expand_offset: float32 [2, 5472], P(None, 'tp'), may hold values from -1.75 to 1.75
- shrink_weight: bfloat16 [5472, 2048], P('tp'), may hold values from -1.25 to 1.25
- shrink_offset: float32 [2048], replicated, may hold values from -3 to 3
- cotangent: bfloat16 [8192, 2048], P(('dp', 'tp')), may hold values from -6 to 6
Outputs:
- layer_out: float32 [8192, 2048], P(('dp', 'tp'))
- tokens_grad: float32 [8192, 2048], P(('dp', 'tp'))
- input_weight_grad: float32 [2048, 6144], P(None, 'tp')
- input_offset_grad: float32 [6144], P('tp')
- output_weight_grad: float32 [2048, 2048], P('tp')
- output_offset_grad: float32 [2048], replicated
- expand_weight_grad: float32 [2048, 2, 5472], P(None, None, 'tp')
- expand_offset_grad: float32 [2, 5472], P(None, 'tp')
- shrink_weight_grad: float32 [5472, 2048], P('tp')
- shrink_offset_grad: float32 [2048], replicated
- norm_gains_grad: float32 [2, 2048], replicated
- norm_offsets_grad: float32 [2, 2048], replicated
The draws below stay inside these ranges and needn't reach their ends.
Inputs may be any that keep to these rules, and one draw needn't show every extreme that they name: `segment_ids`: each row is one sequence of 4 packed documents: ids never fall, every document has one position or more, one document has exactly 512 positions and the others fewer. `positions`: each token's place within its document, counting from 0. `prefix_lengths`: entry k of a row belongs to document k of that sequence and is at most that document's length; some document has its whole length as prefix, some has a prefix of 1.
All inputs are finite; a program needn't handle non-finite values.
Results may differ from the reference program's by a relative error of at most 0.024.
Values may be sent and summed in bfloat16 or wider, within the bound.
A program may use at most 256 MiB of HBM per device.

```python
import jax
import jax.numpy as jnp
from jax import lax

D = 2048
HEAD_DIM = 128
FF = 5472
FF_USED = 5461
LAYERS = 24
SEQ_LEN = 1024
SEGMENTS = 4
NSEQ = 8
TOKENS = 8192


def single_plan(key):
    others = SEGMENTS - 1
    longest = SEQ_LEN // 2
    base_len = longest // (2 * others)
    spare_len = longest - others * base_len
    cut_key, slot_key, prefix_key = jax.random.split(key, 3)
    cut_points = jnp.sort(jax.random.randint(cut_key, (others - 1,), 0, spare_len + 1)).astype(jnp.int32)
    cut_edges = jnp.concatenate([jnp.zeros((1,), jnp.int32), cut_points, jnp.full((1,), spare_len, jnp.int32)])
    pieces = cut_edges[1:] - cut_edges[:-1] + base_len
    lengths = jnp.concatenate([jnp.full((1,), longest, jnp.int32), pieces])
    lengths = jnp.roll(lengths, jax.random.randint(slot_key, (), 0, SEGMENTS))
    starts = jnp.cumsum(lengths) - lengths
    places_at = lax.iota(jnp.int32, SEQ_LEN)
    segments = jnp.sum((places_at[:, None] >= starts[None, 1:]).astype(jnp.int32), axis=1)
    matches = segments[:, None] == lax.iota(jnp.int32, SEGMENTS)[None, :]
    own_start = jnp.sum(jnp.where(matches, starts[None, :], 0), axis=1)
    prefixes = jax.random.randint(prefix_key, (SEGMENTS,), 1, lengths + 1).astype(jnp.int32)
    return (segments.astype(jnp.int32), (places_at - own_start).astype(jnp.int32), prefixes, lengths.astype(jnp.int32))


def document_plan(key):
    keys_all = jax.random.split(jax.random.fold_in(key, 11), NSEQ)
    segments, places, prefixes, lengths = jax.vmap(single_plan)(keys_all)
    seq_rows = lax.iota(jnp.int32, NSEQ)[:, None]
    doc_cols = lax.iota(jnp.int32, SEGMENTS)[None, :]
    force_top = (seq_rows == 0) & (lengths == SEQ_LEN // 2)
    force_low = (seq_rows == NSEQ - 1) & (doc_cols == 0)
    prefixes = jnp.where(force_top, SEQ_LEN // 2, jnp.where(force_low, 1, prefixes)).astype(jnp.int32)
    return (segments, places, prefixes)


def draw_segment_ids(key, part):
    return document_plan(key)[0]


def draw_positions(key, part):
    return document_plan(key)[1]


def draw_prefix_lengths(key, part):
    return document_plan(key)[2]


def shard_levels(own_key, extent, cuts, low, high):
    factor_of = 1.0
    for dim, parts in cuts:
        heights = jax.random.uniform(jax.random.fold_in(jax.random.fold_in(own_key, 6), dim), (parts,), jnp.float32, low / len(cuts), high / len(cuts))
        factor_of = factor_of * jnp.repeat(jnp.exp(heights), extent[dim] // parts).reshape((-1,) + (1,) * (len(extent) - 1 - dim))
    return factor_of


def scatter_about(rng, dims, spread, limit, cuts=(), held_as=jnp.bfloat16):
    drawn = spread * jax.random.normal(rng, dims, jnp.float32)
    if cuts:
        drawn = drawn * shard_levels(rng, dims, cuts, -0.22, 0.18)
    return jnp.clip(drawn, -limit, limit).astype(held_as)


def setup_inputs(seed: int = 0) -> dict:
    seeds = jax.random.split(jax.random.key(seed), 16)
    tokens = scatter_about(seeds[0], (TOKENS, D), 1.0, 6.0, ((0, 32),))
    segment_ids = draw_segment_ids(jax.random.fold_in(seeds[15], 71), 0)
    prefix_lengths = draw_prefix_lengths(jax.random.fold_in(seeds[15], 71), 0)
    positions = draw_positions(jax.random.fold_in(seeds[15], 71), 0)
    norm_gains = jnp.clip(1.0 + 0.1 * jax.random.normal(seeds[4], (2, D), jnp.float32), 0.5, 1.5)
    norm_offsets = scatter_about(seeds[5], (2, D), 0.3, 1.75, (), jnp.float32)
    input_weight = scatter_about(seeds[6], (D, 3 * D), D ** -0.5, 0.125, ((1, 8),))
    input_offset = scatter_about(seeds[7], (3 * D,), 0.1, 0.625, ((0, 8),), jnp.float32)
    output_weight = scatter_about(seeds[8], (D, D), 1.5, 8.0, ((0, 8),))
    output_offset = scatter_about(seeds[9], (D,), 0.5, 3.0, (), jnp.float32)
    expand_weight = scatter_about(seeds[10], (D, 2, FF), D ** -0.5, 0.125, ((2, 8),))
    expand_offset = scatter_about(seeds[11], (2, FF), 0.3, 1.75, ((1, 8),), jnp.float32)
    shrink_weight = scatter_about(seeds[12], (FF, D), 0.2, 1.25, ((0, 8),))
    shrink_offset = scatter_about(seeds[13], (D,), 0.5, 3.0, (), jnp.float32)
    cotangent = scatter_about(seeds[14], (TOKENS, D), 1.0, 6.0, ((0, 32),))
    return {"tokens": tokens, "segment_ids": segment_ids, "prefix_lengths": prefix_lengths, "positions": positions, "norm_gains": norm_gains, "norm_offsets": norm_offsets, "input_weight": input_weight, "input_offset": input_offset, "output_weight": output_weight, "output_offset": output_offset, "expand_weight": expand_weight, "expand_offset": expand_offset, "shrink_weight": shrink_weight, "shrink_offset": shrink_offset, "cotangent": cotangent}


epsilon = 1e-05
rope_base = 10000.0
masked_score = -1e+30
highest = lax.Precision.HIGHEST

@jax.custom_vjp
def low(v):
    return lax.optimization_barrier(v.astype(jnp.bfloat16)).astype(jnp.float32)

@jax.custom_vjp
def low_back(v):
    return v

def low_keep(v):
    return (low(v), None)

def low_pass(kept, grad):
    return (grad,)

def back_keep(v):
    return (v, None)

def back_low(kept, grad):
    return (low(grad),)
low.defvjp(low_keep, low_pass)
low_back.defvjp(back_keep, back_low)

def layer_norm(values, gains, offsets):
    average = lax.optimization_barrier(jnp.mean(values, axis=-1, keepdims=True))
    centred = values - average
    variance = lax.optimization_barrier(jnp.mean(centred * centred, axis=-1, keepdims=True))
    return centred * lax.rsqrt(variance + epsilon) * gains + offsets

def rotary_tables(places):
    half_dim = HEAD_DIM // 2
    exponents = lax.iota(jnp.float32, half_dim) * (-2.0 / HEAD_DIM)
    rates = jnp.power(rope_base, exponents)
    angles = places.astype(jnp.float32)[..., None] * rates
    angles = jnp.concatenate([angles, angles], axis=-1)
    return (jnp.cos(angles), jnp.sin(angles))

def rotate(values, cosine, sine):
    half_dim = HEAD_DIM // 2
    turned = jnp.concatenate([-values[..., half_dim:], values[..., :half_dim]], axis=-1)
    return values * cosine + turned * sine

def gated_gelu(gate_up, keep_units):
    return jax.nn.gelu(gate_up[:, 0], approximate=False) * gate_up[:, 1] * keep_units

def visible_mask(segments, places, prefixes):
    doc_count = prefixes.shape[0]
    matches = segments[:, None] == lax.iota(jnp.int32, doc_count)[None, :]
    own_prefix = lax.optimization_barrier(jnp.sum(jnp.where(matches, prefixes[None, :], 0), axis=1))
    same_doc = segments[:, None] == segments[None, :]
    rows_at = lax.iota(jnp.int32, segments.shape[0])
    earlier = rows_at[None, :] <= rows_at[:, None]
    opened = places[None, :] < own_prefix[:, None]
    return same_doc & (earlier | opened)

def layer_block(row_block, segments, places, prefixes, norm_gains, norm_offsets, input_weight, input_offset, output_weight, output_offset, expand_weight, expand_offset, shrink_weight, shrink_offset):
    residual_scale = (2.0 * LAYERS) ** 0.5
    score_scale = HEAD_DIM ** (-0.5)
    heads_all = D // HEAD_DIM
    first_norm = layer_norm(row_block, norm_gains[0], norm_offsets[0])
    projected = low_back(jnp.dot(low(first_norm), input_weight, precision=highest) + input_offset)
    projected = projected.reshape(SEQ_LEN, heads_all, 3, HEAD_DIM)
    cosine, sine = rotary_tables(places)
    cosine = cosine[:, None, :]
    sine = sine[:, None, :]
    queries = low(rotate(projected[:, :, 0], cosine, sine))
    keys_low = low(rotate(projected[:, :, 1], cosine, sine))
    values_low = low(projected[:, :, 2])
    visible = visible_mask(segments, places, prefixes)
    scores = jnp.einsum('ihe,jhe->hij', queries, keys_low, precision=highest) * score_scale
    scores = low_back(jnp.where(visible[None], scores, masked_score))
    attend_probs = low(jax.nn.softmax(scores, axis=-1))
    mixed_heads = jnp.einsum('hij,jhe->ihe', attend_probs, values_low, precision=highest)
    mixed_heads = low(low_back(mixed_heads)).reshape(SEQ_LEN, D)
    attention = low_back(jnp.dot(mixed_heads, output_weight, precision=highest) + output_offset)
    middle = residual_scale * first_norm + attention
    second_norm = layer_norm(middle, norm_gains[1], norm_offsets[1])
    gate_up = low_back(jnp.einsum('id,dcf->icf', low(second_norm), expand_weight, precision=highest) + expand_offset)
    keep_units = (lax.iota(jnp.int32, FF) < FF_USED).astype(jnp.float32)
    hidden = low(gated_gelu(gate_up, keep_units))
    shrunk = low_back(jnp.dot(hidden, shrink_weight, precision=highest) + shrink_offset)
    return residual_scale * second_norm + shrunk

def reference(tokens, segment_ids, prefix_lengths, positions, norm_gains, norm_offsets, input_weight, input_offset, output_weight, output_offset, expand_weight, expand_offset, shrink_weight, shrink_offset, cotangent):
    params = (norm_gains, norm_offsets, input_weight.astype(jnp.float32), input_offset, output_weight.astype(jnp.float32), output_offset, expand_weight.astype(jnp.float32), expand_offset, shrink_weight.astype(jnp.float32), shrink_offset)
    seq_total = segment_ids.shape[0]
    token_rows = tokens.astype(jnp.float32).reshape(seq_total, SEQ_LEN, D)
    grad_rows = cotangent.astype(jnp.float32).reshape(seq_total, SEQ_LEN, D)

    def per_sequence(running, pieces_in):
        row_block, grad_block, segments, places, prefixes = pieces_in

        def forward(block_in, *weights):
            return layer_block(block_in, segments, places, prefixes, *weights)
        outputs, pull_back = jax.vjp(forward, row_block, *params)
        pulled = pull_back(grad_block)
        updated = tuple((summed + fresh for summed, fresh in zip(running, pulled[1:])))
        return (updated, (outputs, pulled[0]))
    empty_sums = tuple((jnp.zeros_like(weight) for weight in params))
    totals, (layer_rows, grad_tokens) = lax.scan(per_sequence, empty_sums, (token_rows, grad_rows, segment_ids, positions, prefix_lengths))
    return (layer_rows.reshape(TOKENS, D), grad_tokens.reshape(TOKENS, D), totals[2], totals[3], totals[4], totals[5], totals[6], totals[7], totals[8], totals[9], totals[0], totals[1])
```

```python
import functools

import jax
import jax.numpy as jnp
from jax import lax
from jax.experimental import pallas as pl
from jax.experimental.pallas import tpu as pltpu
from jax.sharding import PartitionSpec as P

HEAD_DIM = 128
FF_USED = 5461
LAYERS = 24
SEQ_LEN = 1024
BLOCK = 256

epsilon = 1e-05
rope_base = 10000.0
masked_score = -1e30
F32 = jnp.float32
BF16 = jnp.bfloat16
ROWS = (((1,), (1,)), ((), ()))
COLS = (((0,), (0,)), ((), ()))


def dot(left, right, dims):
    return lax.dot_general(left, right, dims, preferred_element_type=F32)


def normalize(values):
    average = jnp.mean(values, axis=-1, keepdims=True)
    centred = values - average
    variance = jnp.mean(centred * centred, axis=-1, keepdims=True)
    scale = lax.rsqrt(variance + epsilon)
    return centred * scale, scale


def normalize_back(grad, gains, hat, scale):
    pulled = grad * gains
    grad_in = scale * (
        pulled
        - jnp.mean(pulled, axis=-1, keepdims=True)
        - hat * jnp.mean(pulled * hat, axis=-1, keepdims=True)
    )
    return grad_in, jnp.sum(grad * hat, axis=0), jnp.sum(grad, axis=0)


def rotary_tables(places):
    half_dim = HEAD_DIM // 2
    exponents = lax.iota(F32, half_dim) * (-2.0 / HEAD_DIM)
    rates = jnp.power(rope_base, exponents)
    angles = places.astype(F32)[..., None] * rates
    cosine, sine = jnp.cos(angles), jnp.sin(angles)
    return jnp.concatenate([cosine, cosine], -1), jnp.concatenate([-sine, sine], -1)


def line_steps(part, count, axis):
    here = lax.axis_index(axis)
    half = count // 2
    for k in range(half - 1):
        got = yield part, [(k, k + 1), (count - 1 - k, count - 2 - k)]
        part = (part.astype(F32) + got.astype(F32)).astype(BF16)
    if count > 1:
        got = yield part, [(half - 1, half), (half, half - 1)]
        part = (part.astype(F32) + got.astype(F32)).astype(BF16)
    for k in range(half - 1):
        got = yield part, [(half - 1 - k, half - 2 - k), (half + k, half + k + 1)]
        outer = (here == half - 2 - k) | (here == half + k + 1)
        part = jnp.where(outer, got, part)
    return part


class Line:
    def __init__(self, count, axis):
        self.count, self.axis = count, axis
        self.waiting, self.moving, self.sums, self.marks = [], [], {}, []

    def add(self, name, part):
        self.waiting.append((name, part.astype(BF16)))

    def turn(self, *inputs):
        sends = []
        if self.waiting:
            name, part = self.waiting.pop(0)
            self.moving.append((name, line_steps(part, self.count, self.axis), None))
        for name, steps, got in self.moving:
            try:
                part, pairs = steps.send(got)
                sends.append((name, steps, part, pairs))
            except StopIteration as done:
                self.sums[name] = done.value
        parts = [part for _, _, part, _ in sends]
        inputs, parts, _ = lax.optimization_barrier((inputs, parts, self.marks))
        self.moving = [
            (name, steps, lax.ppermute(part, self.axis, pairs))
            for (name, steps, _, pairs), part in zip(sends, parts)
        ]
        self.marks = [got for _, _, got in self.moving]
        return inputs

    def made(self, *values):
        self.marks.extend(values)


def swap_sum(values, count, axis):
    bit = 1
    while bit < count:
        values = values + lax.ppermute(values, axis, [(i, i ^ bit) for i in range(count)])
        bit *= 2
    return values


def turned(values, cosine, sine):
    return values * cosine + pltpu.roll(values, HEAD_DIM // 2, 1) * sine


def attend_forward_kernel(bounds, projected, cosine, sine, low, high, packed, mixed, peaks, values_t):
    seq = pl.program_id(0)
    score_scale = HEAD_DIM ** (-0.5)
    packed[:, :HEAD_DIM] = turned(projected[:, :HEAD_DIM], cosine[...], sine[...]).astype(BF16)
    packed[:, HEAD_DIM : 2 * HEAD_DIM] = turned(
        projected[:, HEAD_DIM : 2 * HEAD_DIM], cosine[...], sine[...]
    ).astype(BF16)
    packed[:, 2 * HEAD_DIM :] = projected[:, 2 * HEAD_DIM :].astype(BF16)
    for b in range(SEQ_LEN // BLOCK):
        values_t[b] = projected[b * BLOCK : (b + 1) * BLOCK, 2 * HEAD_DIM :].T.astype(BF16)

    def queries_block(b, _):
        start = pl.multiple_of(b * BLOCK, BLOCK)
        queries = packed[pl.ds(start, BLOCK), :HEAD_DIM]
        first = low[0, 0, pl.ds(start, BLOCK)][None, :]
        last = high[0, 0, pl.ds(start, BLOCK)][None, :]

        def keys_block(j, carry):
            peak, total, gathered = carry
            keys = packed[pl.ds(pl.multiple_of(j * BLOCK, BLOCK), BLOCK), HEAD_DIM : 2 * HEAD_DIM]
            scores = dot(keys, queries, ROWS) * score_scale
            place = lax.broadcasted_iota(jnp.int32, (BLOCK, BLOCK), 0) + j * BLOCK
            scores = jnp.where((place >= first) & (place <= last), scores, masked_score)
            new_peak = jnp.maximum(peak, jnp.max(scores, axis=0, keepdims=True))
            shifted = jnp.exp(scores - new_peak)
            fade = jnp.exp(peak - new_peak)
            total = total * fade + jnp.sum(shifted, axis=0, keepdims=True)
            gathered = gathered * fade + jnp.dot(
                values_t[j], shifted.astype(BF16), preferred_element_type=F32
            )
            return new_peak, total, gathered

        peak, total, gathered = lax.fori_loop(
            bounds[seq, b, 0],
            bounds[seq, b, 1],
            keys_block,
            (
                jnp.full((1, BLOCK), masked_score, F32),
                jnp.zeros((1, BLOCK), F32),
                jnp.zeros((HEAD_DIM, BLOCK), F32),
            ),
        )
        mixed[pl.ds(start, BLOCK), :] = (gathered / total).T.astype(BF16)
        peaks[0, 0, 0, pl.ds(start, BLOCK)] = (peak + jnp.log(total))[0]
        return 0

    lax.fori_loop(0, SEQ_LEN // BLOCK, queries_block, 0)


def attend_forward(projected, cosine, sine, low, high, bounds):
    seq_count, heads = cosine.shape[0], projected.shape[1] // (3 * HEAD_DIM)
    rows = seq_count * SEQ_LEN
    per_head = pl.BlockSpec((SEQ_LEN, 3 * HEAD_DIM), lambda s, h, *_: (s, h))
    table = pl.BlockSpec((None, SEQ_LEN, HEAD_DIM), lambda s, h, *_: (s, 0, 0))
    line = pl.BlockSpec((1, 1, SEQ_LEN), lambda s, h, *_: (s, 0, 0))
    return pl.pallas_call(
        attend_forward_kernel,
        grid_spec=pltpu.PrefetchScalarGridSpec(
            num_scalar_prefetch=1,
            grid=(seq_count, heads),
            in_specs=[per_head, table, table, line, line],
            out_specs=[
                per_head,
                pl.BlockSpec((SEQ_LEN, HEAD_DIM), lambda s, h, *_: (s, h)),
                pl.BlockSpec((1, 1, 1, SEQ_LEN), lambda s, h, *_: (s, h, 0, 0)),
            ],
            scratch_shapes=[pltpu.VMEM((SEQ_LEN // BLOCK, HEAD_DIM, BLOCK), BF16)],
        ),
        out_shape=[
            jax.ShapeDtypeStruct(projected.shape, BF16),
            jax.ShapeDtypeStruct((rows, heads * HEAD_DIM), BF16),
            jax.ShapeDtypeStruct((seq_count, heads, 1, SEQ_LEN), F32),
        ],
        compiler_params=pltpu.CompilerParams(vmem_limit_bytes=40 << 20),
        cost_estimate=pl.CostEstimate(
            flops=4 * rows * SEQ_LEN * HEAD_DIM * heads,
            bytes_accessed=rows * heads * HEAD_DIM * 20,
            transcendentals=rows * SEQ_LEN * heads,
        ),
        name="attend_forward",
    )(bounds, projected, cosine, sine, low[:, None], high[:, None])


def attend_backward_kernel(
    bounds, packed, mixed, grad_mixed, peaks, cosine, sine, low, high, grad, keys_t, inner, grad_queries_t, grad_keys, grad_values
):
    seq = pl.program_id(0)
    score_scale = HEAD_DIM ** (-0.5)
    for b in range(SEQ_LEN // BLOCK):
        part = slice(b * BLOCK, (b + 1) * BLOCK)
        keys_t[b] = packed[part, HEAD_DIM : 2 * HEAD_DIM].astype(F32).T.astype(BF16)
        both = grad_mixed[part, :].astype(F32) * mixed[part, :].astype(F32)
        inner[b] = jnp.sum(both.T, axis=0, keepdims=True)
    grad_keys[...] = jnp.zeros_like(grad_keys)
    grad_values[...] = jnp.zeros_like(grad_values)

    def queries_block(b, _):
        start = pl.multiple_of(b * BLOCK, BLOCK)
        queries = packed[pl.ds(start, BLOCK), :HEAD_DIM]
        pulled = grad_mixed[pl.ds(start, BLOCK), :]
        first = low[0, 0, pl.ds(start, BLOCK)][None, :]
        last = high[0, 0, pl.ds(start, BLOCK)][None, :]
        peak = peaks[0, 0, 0, pl.ds(start, BLOCK)][None, :]
        inner_sum = inner[b]

        def keys_block(j, total):
            part = pl.ds(pl.multiple_of(j * BLOCK, BLOCK), BLOCK)
            keys = packed[part, HEAD_DIM : 2 * HEAD_DIM]
            values = packed[part, 2 * HEAD_DIM :]
            scores = dot(keys, queries, ROWS) * score_scale
            place = lax.broadcasted_iota(jnp.int32, (BLOCK, BLOCK), 0) + j * BLOCK
            scores = jnp.where((place >= first) & (place <= last), scores, masked_score)
            probs = jnp.exp(scores - peak)
            grad_probs = dot(values, pulled, ROWS)
            grad_scores = (probs * (grad_probs - inner_sum)).astype(BF16)
            grad_values[part, :] += jnp.dot(probs.astype(BF16), pulled, preferred_element_type=F32)
            grad_keys[part, :] += jnp.dot(grad_scores, queries, preferred_element_type=F32)
            return total + jnp.dot(keys_t[j], grad_scores, preferred_element_type=F32)

        total = lax.fori_loop(
            bounds[seq, b, 0], bounds[seq, b, 1], keys_block, jnp.zeros((HEAD_DIM, BLOCK), F32)
        )
        grad_queries = total.T * score_scale
        rows = pl.ds(start, BLOCK)
        grad[rows, :HEAD_DIM] = turned(grad_queries, cosine[rows, :], -sine[rows, :]).astype(BF16)
        return 0

    lax.fori_loop(0, SEQ_LEN // BLOCK, queries_block, 0)
    grad[:, HEAD_DIM : 2 * HEAD_DIM] = turned(
        grad_keys[...] * score_scale, cosine[...], -sine[...]
    ).astype(BF16)
    grad[:, 2 * HEAD_DIM :] = grad_values[...].astype(BF16)


def attend_backward(packed, mixed, grad_mixed, peaks, cosine, sine, low, high, bounds):
    seq_count, heads = cosine.shape[0], packed.shape[1] // (3 * HEAD_DIM)
    rows = seq_count * SEQ_LEN
    per_head = pl.BlockSpec((SEQ_LEN, 3 * HEAD_DIM), lambda s, h, *_: (s, h))
    single = pl.BlockSpec((SEQ_LEN, HEAD_DIM), lambda s, h, *_: (s, h))
    table = pl.BlockSpec((None, SEQ_LEN, HEAD_DIM), lambda s, h, *_: (s, 0, 0))
    line = pl.BlockSpec((1, 1, SEQ_LEN), lambda s, h, *_: (s, 0, 0))
    blocks = SEQ_LEN // BLOCK
    return pl.pallas_call(
        attend_backward_kernel,
        grid_spec=pltpu.PrefetchScalarGridSpec(
            num_scalar_prefetch=1,
            grid=(seq_count, heads),
            in_specs=[
                per_head,
                single,
                single,
                pl.BlockSpec((1, 1, 1, SEQ_LEN), lambda s, h, *_: (s, h, 0, 0)),
                table,
                table,
                line,
                line,
            ],
            out_specs=per_head,
            scratch_shapes=[
                pltpu.VMEM((blocks, HEAD_DIM, BLOCK), BF16),
                pltpu.VMEM((blocks, 1, BLOCK), F32),
                pltpu.VMEM((blocks, HEAD_DIM, BLOCK), F32),
                pltpu.VMEM((SEQ_LEN, HEAD_DIM), F32),
                pltpu.VMEM((SEQ_LEN, HEAD_DIM), F32),
            ],
        ),
        out_shape=jax.ShapeDtypeStruct(packed.shape, BF16),
        compiler_params=pltpu.CompilerParams(vmem_limit_bytes=40 << 20),
        cost_estimate=pl.CostEstimate(
            flops=10 * rows * SEQ_LEN * HEAD_DIM * heads,
            bytes_accessed=rows * heads * HEAD_DIM * 20,
            transcendentals=rows * SEQ_LEN * heads,
        ),
        name="attend_backward",
    )(bounds, packed, mixed, grad_mixed, peaks, cosine, sine, low[:, None], high[:, None])


def feed_kernel(units, second, cotangent, expand, shrink, columns, hidden, grads):
    step = 176 if units % 176 == 0 else units
    for at in range(0, units, step):
        part = slice(at, at + step)
        upper = slice(units + at, units + at + step)
        gate = dot(expand[part, :], second[...], ROWS) + columns[part, 0:1]
        up = dot(expand[upper, :], second[...], ROWS) + columns[part, 1:2]
        grad_hidden = dot(shrink[part, :], cotangent[...], ROWS) * columns[part, 2:3]
        normal = 0.5 * (1.0 + lax.erf(gate * (0.5**0.5)))
        density = jnp.exp(-0.5 * gate * gate) * (0.5 / jnp.pi) ** 0.5
        gelu = gate * normal
        hidden[part, :] = (gelu * up * columns[part, 2:3]).astype(BF16)
        grads[part, :] = (grad_hidden * up * (normal + gate * density)).astype(BF16)
        grads[upper, :] = (grad_hidden * gelu).astype(BF16)


def feed(second, cotangent, expand, shrink, columns):
    rows, width = second.shape
    units = shrink.shape[0]
    tile = 256
    tokens = pl.BlockSpec((tile, width), lambda i: (i, 0))
    whole = lambda a: pl.BlockSpec(a.shape, lambda i: (0, 0), pipeline_mode=pl.Buffered(1))
    return pl.pallas_call(
        functools.partial(feed_kernel, units),
        grid=(rows // tile,),
        in_specs=[tokens, tokens, whole(expand), whole(shrink), whole(columns)],
        out_specs=[
            pl.BlockSpec((units, tile), lambda i: (0, i)),
            pl.BlockSpec((2 * units, tile), lambda i: (0, i)),
        ],
        out_shape=[
            jax.ShapeDtypeStruct((units, rows), BF16),
            jax.ShapeDtypeStruct((2 * units, rows), BF16),
        ],
        compiler_params=pltpu.CompilerParams(vmem_limit_bytes=50 << 20),
        cost_estimate=pl.CostEstimate(
            flops=6 * rows * width * units,
            bytes_accessed=4 * rows * width + 6 * units * (rows + width),
            transcendentals=2 * rows * units,
        ),
        name="feed",
    )(second, cotangent, expand, shrink, columns)


def weave_kernel(gate, up, out):
    out[:, 0, :] = gate[...].astype(F32)
    out[:, 1, :] = up[...].astype(F32)


def weave(gate, up):
    rows, width = gate.shape
    tile = 256
    part = pl.BlockSpec((rows, tile), lambda j: (0, j))
    return pl.pallas_call(
        weave_kernel,
        grid=(width // tile,),
        in_specs=[part, part],
        out_specs=pl.BlockSpec((rows, 2, tile), lambda j: (0, 0, j)),
        out_shape=jax.ShapeDtypeStruct((rows, 2, width), F32),
        compiler_params=pltpu.CompilerParams(vmem_limit_bytes=40 << 20),
        cost_estimate=pl.CostEstimate(flops=0, bytes_accessed=12 * rows * width, transcendentals=0),
        name="weave",
    )(gate, up)


def cuts(total, pieces):
    step = -(-total // pieces)
    step = -(-step // 16) * 16
    return [(at, min(at + step, total)) for at in range(0, total, step)]


def local(
    dp,
    tp,
    tokens,
    segment_ids,
    prefix_lengths,
    positions,
    norm_gains,
    norm_offsets,
    input_weight,
    input_offset,
    output_weight,
    output_offset,
    expand_weight,
    expand_offset,
    shrink_weight,
    shrink_offset,
    cotangent,
):
    residual_scale = (2.0 * LAYERS) ** 0.5
    seq_count = segment_ids.shape[0]
    group_rows = seq_count * SEQ_LEN
    width = tokens.shape[1]
    units_used = expand_weight.shape[2]
    units = -(-units_used // 176) * 176
    heads_width = output_weight.shape[0]
    gather = lambda a: lax.all_gather(a, "tp", axis=0, tiled=True)
    scatter = lambda a: lax.psum_scatter(a, "tp", scatter_dimension=0, tiled=True).astype(F32)

    pad = ((0, units - units_used), (0, 0))
    turned_expand = jnp.transpose(expand_weight, (2, 1, 0))
    expand = jnp.concatenate(
        [jnp.pad(turned_expand[:, 0], pad), jnp.pad(turned_expand[:, 1], pad)], axis=0
    )
    shrink = jnp.pad(shrink_weight, pad)
    unit_index = lax.axis_index("tp") * units_used + lax.iota(jnp.int32, units_used)
    keep_units = (unit_index < FF_USED).astype(F32)
    columns = jnp.pad(jnp.stack([expand_offset[0], expand_offset[1], keep_units], axis=1), pad)

    row_at = lax.broadcasted_iota(jnp.int32, positions.shape, 1)
    low = row_at - positions
    matches = segment_ids[:, :, None] == lax.iota(jnp.int32, prefix_lengths.shape[1])
    own_prefix = jnp.sum(jnp.where(matches, prefix_lengths[:, None, :], 0), axis=2)
    high = jnp.maximum(row_at, low + own_prefix - 1)
    bounds = jnp.stack(
        [
            jnp.min(low.reshape(seq_count, -1, BLOCK), axis=2) // BLOCK,
            jnp.max(high.reshape(seq_count, -1, BLOCK), axis=2) // BLOCK + 1,
        ],
        axis=2,
    )
    cosine, sine = rotary_tables(positions)

    first_hat, first_scale = normalize(tokens.astype(F32))
    first_norm = first_hat * norm_gains[0] + norm_offsets[0]
    first_all = gather(first_norm.astype(BF16))
    cotangent_all = gather(cotangent)
    full_output = gather(output_weight)
    projected = jnp.dot(first_all, input_weight, preferred_element_type=F32) + input_offset
    packed, mixed, peaks = attend_forward(projected, cosine, sine, low, high, bounds)
    own_heads = lax.all_to_all(mixed, "tp", split_axis=0, concat_axis=1, tiled=True)
    attention = jnp.dot(own_heads, full_output, preferred_element_type=F32) + output_offset
    middle = residual_scale * first_norm + attention
    second_hat, second_scale = normalize(middle)
    second_norm = second_hat * norm_gains[1] + norm_offsets[1]
    second_all = gather(second_norm.astype(BF16))
    hidden, grads = feed(second_all, cotangent_all, expand, shrink, columns)

    line = Line(dp, "dp")
    mul = lambda a, b: jnp.dot(a, b, preferred_element_type=F32).astype(BF16)
    unit_cuts = cuts(units_used, 3)
    width_cuts = cuts(width, 3)
    shrink_part = [None] * 3
    expand_part = [[None] * 3, [None] * 3]
    a, b = unit_cuts[0]
    line.add("s0", mul(hidden[a:b], cotangent_all))

    hidden, cotangent_all, grads, expand = line.turn(hidden, cotangent_all, grads, expand)
    for k in (1, 2):
        a, b = unit_cuts[k]
        line.add("s%d" % k, mul(hidden[a:b], cotangent_all))
    grad_second_part = dot(grads, expand, COLS).astype(BF16)
    line.made(line.waiting[0][1], line.waiting[1][1], grad_second_part)

    grads, second_all, hidden, shrink, grad_second_part = line.turn(
        grads, second_all, hidden, shrink, grad_second_part
    )
    grad_second_sum = scatter(grad_second_part)
    for k in range(3):
        a, b = unit_cuts[k]
        line.add("g%d" % k, mul(grads[a:b], second_all))
    shrink_sum_part = dot(hidden, shrink, COLS).astype(BF16)
    line.made(shrink_sum_part, *[p for _, p in line.waiting[-3:]])

    grads, second_all, shrink_sum_part, cotangent = line.turn(
        grads, second_all, shrink_sum_part, cotangent
    )
    shrink_sum = scatter(shrink_sum_part)
    for k in range(3):
        a, b = unit_cuts[k]
        line.add("u%d" % k, mul(grads[units + a : units + b], second_all))
    expand_offset_grad = jnp.sum(grads.astype(F32), axis=1).reshape(2, units)[:, :units_used]
    grad_output = cotangent.astype(F32)
    shrink_offset_grad = jnp.sum(grad_output, axis=0)
    line.made(expand_offset_grad, shrink_offset_grad, *[p for _, p in line.waiting[-3:]])

    line.turn()

    grad_second_sum, full_output = line.turn(grad_second_sum, full_output)
    grad_second = residual_scale * grad_output + grad_second_sum
    grad_middle, second_gain_grad, second_offset_grad = normalize_back(
        grad_second, norm_gains[1], second_hat, second_scale
    )
    grad_attention = grad_middle.astype(BF16)
    output_offset_grad = jnp.sum(grad_attention.astype(F32), axis=0)
    grad_own = dot(grad_attention, full_output, ROWS).astype(BF16)
    grad_mixed = lax.all_to_all(grad_own, "tp", split_axis=1, concat_axis=0, tiled=True)
    attention_all = gather(grad_attention)
    line.made(grad_mixed, second_gain_grad, second_offset_grad, output_offset_grad)

    grad_mixed, packed, mixed = line.turn(grad_mixed, packed, mixed)
    grad_projected = attend_backward(
        packed, mixed, grad_mixed, peaks, cosine, sine, low, high, bounds
    )
    line.made(grad_projected)

    grad_projected, first_all, input_weight = line.turn(grad_projected, first_all, input_weight)
    grad_first_part = dot(grad_projected, input_weight, ROWS).astype(BF16)
    input_offset_grad = jnp.sum(grad_projected.astype(F32), axis=0)
    line.made(grad_first_part, input_offset_grad)

    grad_projected, first_all, grad_first_part = line.turn(grad_projected, first_all, grad_first_part)
    grad_first_sum = scatter(grad_first_part)
    for k in range(3):
        a, b = width_cuts[k]
        line.add("i%d" % k, dot(first_all[:, a:b], grad_projected, COLS))
    line.made(*[p for _, p in line.waiting[-3:]])

    attention_all, mixed = line.turn(attention_all, mixed)
    line.add("o", dot(mixed, attention_all, COLS))
    line.made(line.waiting[-1][1])

    shrink_sum, second_hat = line.turn(shrink_sum, second_hat)
    layer_out = (
        residual_scale * (second_hat * norm_gains[1] + norm_offsets[1]) + shrink_sum + shrink_offset
    )
    shrink_grad = jnp.concatenate([line.sums["s%d" % k] for k in range(3)]).astype(F32)
    line.made(layer_out, shrink_grad)
    while "u2" not in line.sums:
        line.turn()
    expand_grad = weave(
        jnp.concatenate([line.sums["g%d" % k] for k in range(3)]),
        jnp.concatenate([line.sums["u%d" % k] for k in range(3)]),
    )
    line.made(expand_grad)

    grad_first_sum, grad_middle = line.turn(grad_first_sum, grad_middle)
    grad_first = residual_scale * grad_middle + grad_first_sum
    tokens_grad, first_gain_grad, first_offset_grad = normalize_back(
        grad_first, norm_gains[0], first_hat, first_scale
    )
    line.made(tokens_grad, first_gain_grad, first_offset_grad)
    while line.waiting or line.moving:
        line.turn()

    whole_sums = swap_sum(
        jnp.stack(
            [
                first_gain_grad,
                second_gain_grad,
                first_offset_grad,
                second_offset_grad,
                output_offset_grad,
                shrink_offset_grad,
            ]
        ),
        tp,
        "tp",
    )
    whole_sums = swap_sum(whole_sums, dp, "dp")
    group_sums = swap_sum(
        jnp.concatenate([expand_offset_grad.reshape(-1), input_offset_grad]), dp, "dp"
    )
    return (
        layer_out,
        tokens_grad,
        jnp.concatenate([line.sums["i%d" % k] for k in range(3)]).astype(F32),
        group_sums[2 * units_used :],
        line.sums["o"].astype(F32),
        whole_sums[4],
        jnp.transpose(expand_grad, (2, 1, 0)),
        group_sums[: 2 * units_used].reshape(2, units_used),
        shrink_grad,
        whole_sums[5],
        whole_sums[0:2],
        whole_sums[2:4],
    )


def solution(mesh):
    in_specs = (
        P(("dp", "tp"), None),
        P("dp", None),
        P("dp", None),
        P("dp", None),
        P(),
        P(),
        P(None, "tp"),
        P("tp"),
        P("tp", None),
        P(),
        P(None, None, "tp"),
        P(None, "tp"),
        P("tp", None),
        P(),
        P(("dp", "tp"), None),
    )
    out_specs = (
        P(("dp", "tp"), None),
        P(("dp", "tp"), None),
        P(None, "tp"),
        P("tp"),
        P("tp", None),
        P(),
        P(None, None, "tp"),
        P(None, "tp"),
        P("tp", None),
        P(),
        P(),
        P(),
    )
    return jax.shard_map(
        functools.partial(local, mesh.shape["dp"], mesh.shape["tp"]),
        mesh=mesh,
        in_specs=in_specs,
        out_specs=out_specs,
        check_vma=False,
    )
```

```python
import functools

import jax
import jax.numpy as jnp
from jax import lax
from jax.experimental import pallas as pl
from jax.experimental.pallas import tpu as pltpu
from jax.sharding import PartitionSpec as P

HEAD_DIM = 128
FF_USED = 5461
LAYERS = 24
SEQ_LEN = 1024
BLOCK = 256

epsilon = 1e-05
rope_base = 10000.0
masked_score = -1e30
F32 = jnp.float32
BF16 = jnp.bfloat16
ROWS = (((1,), (1,)), ((), ()))
COLS = (((0,), (0,)), ((), ()))


def dot(left, right, dims):
    return lax.dot_general(left, right, dims, preferred_element_type=F32)


def normalize(values):
    average = jnp.mean(values, axis=-1, keepdims=True)
    centred = values - average
    variance = jnp.mean(centred * centred, axis=-1, keepdims=True)
    scale = lax.rsqrt(variance + epsilon)
    return centred * scale, scale


def normalize_back(grad, gains, hat, scale):
    pulled = grad * gains
    grad_in = scale * (
        pulled
        - jnp.mean(pulled, axis=-1, keepdims=True)
        - hat * jnp.mean(pulled * hat, axis=-1, keepdims=True)
    )
    return grad_in, jnp.sum(grad * hat, axis=0), jnp.sum(grad, axis=0)


def rotary_tables(places):
    half_dim = HEAD_DIM // 2
    exponents = lax.iota(F32, half_dim) * (-2.0 / HEAD_DIM)
    rates = jnp.power(rope_base, exponents)
    angles = places.astype(F32)[..., None] * rates
    cosine, sine = jnp.cos(angles), jnp.sin(angles)
    return jnp.concatenate([cosine, cosine], -1), jnp.concatenate([-sine, sine], -1)


def line_steps(part, count, axis):
    here = lax.axis_index(axis)
    half = count // 2
    for k in range(half - 1):
        got = yield part, [(k, k + 1), (count - 1 - k, count - 2 - k)]
        part = (part.astype(F32) + got.astype(F32)).astype(BF16)
    if count > 1:
        got = yield part, [(half - 1, half), (half, half - 1)]
        part = (part.astype(F32) + got.astype(F32)).astype(BF16)
    for k in range(half - 1):
        got = yield part, [(half - 1 - k, half - 2 - k), (half + k, half + k + 1)]
        outer = (here == half - 2 - k) | (here == half + k + 1)
        part = jnp.where(outer, got, part)
    return part


class Line:
    def __init__(self, count, axis):
        self.count, self.axis = count, axis
        self.waiting, self.moving, self.sums, self.marks = [], [], {}, []

    def add(self, name, part):
        self.waiting.append((name, part.astype(BF16)))

    def turn(self, *inputs):
        sends = []
        if self.waiting:
            name, part = self.waiting.pop(0)
            self.moving.append((name, line_steps(part, self.count, self.axis), None))
        for name, steps, got in self.moving:
            try:
                part, pairs = steps.send(got)
                sends.append((name, steps, part, pairs))
            except StopIteration as done:
                self.sums[name] = done.value
        parts = [part for _, _, part, _ in sends]
        inputs, parts, _ = lax.optimization_barrier((inputs, parts, self.marks))
        self.moving = [
            (name, steps, lax.ppermute(part, self.axis, pairs))
            for (name, steps, _, pairs), part in zip(sends, parts)
        ]
        self.marks = [got for _, _, got in self.moving]
        return inputs

    def made(self, *values):
        self.marks.extend(values)


def swap_sum(values, count, axis):
    bit = 1
    while bit < count:
        values = values + lax.ppermute(values, axis, [(i, i ^ bit) for i in range(count)])
        bit *= 2
    return values


def turned(values, cosine, sine):
    return values * cosine + pltpu.roll(values, HEAD_DIM // 2, 1) * sine


def attend_forward_kernel(bounds, projected, cosine, sine, low, high, packed, mixed, peaks, values_t):
    seq = pl.program_id(0)
    score_scale = HEAD_DIM ** (-0.5)
    packed[:, :HEAD_DIM] = turned(projected[:, :HEAD_DIM], cosine[...], sine[...]).astype(BF16)
    packed[:, HEAD_DIM : 2 * HEAD_DIM] = turned(
        projected[:, HEAD_DIM : 2 * HEAD_DIM], cosine[...], sine[...]
    ).astype(BF16)
    packed[:, 2 * HEAD_DIM :] = projected[:, 2 * HEAD_DIM :].astype(BF16)
    for b in range(SEQ_LEN // BLOCK):
        values_t[b] = projected[b * BLOCK : (b + 1) * BLOCK, 2 * HEAD_DIM :].T.astype(BF16)

    def queries_block(b, _):
        start = pl.multiple_of(b * BLOCK, BLOCK)
        queries = packed[pl.ds(start, BLOCK), :HEAD_DIM]
        first = low[0, 0, pl.ds(start, BLOCK)][None, :]
        last = high[0, 0, pl.ds(start, BLOCK)][None, :]

        def keys_block(j, carry):
            peak, total, gathered = carry
            keys = packed[pl.ds(pl.multiple_of(j * BLOCK, BLOCK), BLOCK), HEAD_DIM : 2 * HEAD_DIM]
            scores = dot(keys, queries, ROWS) * score_scale
            place = lax.broadcasted_iota(jnp.int32, (BLOCK, BLOCK), 0) + j * BLOCK
            scores = jnp.where((place >= first) & (place <= last), scores, masked_score)
            new_peak = jnp.maximum(peak, jnp.max(scores, axis=0, keepdims=True))
            shifted = jnp.exp(scores - new_peak)
            fade = jnp.exp(peak - new_peak)
            total = total * fade + jnp.sum(shifted, axis=0, keepdims=True)
            gathered = gathered * fade + jnp.dot(
                values_t[j], shifted.astype(BF16), preferred_element_type=F32
            )
            return new_peak, total, gathered

        peak, total, gathered = lax.fori_loop(
            bounds[seq, b, 0],
            bounds[seq, b, 1],
            keys_block,
            (
                jnp.full((1, BLOCK), masked_score, F32),
                jnp.zeros((1, BLOCK), F32),
                jnp.zeros((HEAD_DIM, BLOCK), F32),
            ),
        )
        mixed[pl.ds(start, BLOCK), :] = (gathered / total).T.astype(BF16)
        peaks[0, 0, 0, pl.ds(start, BLOCK)] = (peak + jnp.log(total))[0]
        return 0

    lax.fori_loop(0, SEQ_LEN // BLOCK, queries_block, 0)


def attend_forward(projected, cosine, sine, low, high, bounds):
    seq_count, heads = cosine.shape[0], projected.shape[1] // (3 * HEAD_DIM)
    rows = seq_count * SEQ_LEN
    per_head = pl.BlockSpec((SEQ_LEN, 3 * HEAD_DIM), lambda s, h, *_: (s, h))
    table = pl.BlockSpec((None, SEQ_LEN, HEAD_DIM), lambda s, h, *_: (s, 0, 0))
    line = pl.BlockSpec((1, 1, SEQ_LEN), lambda s, h, *_: (s, 0, 0))
    return pl.pallas_call(
        attend_forward_kernel,
        grid_spec=pltpu.PrefetchScalarGridSpec(
            num_scalar_prefetch=1,
            grid=(seq_count, heads),
            in_specs=[per_head, table, table, line, line],
            out_specs=[
                per_head,
                pl.BlockSpec((SEQ_LEN, HEAD_DIM), lambda s, h, *_: (s, h)),
                pl.BlockSpec((1, 1, 1, SEQ_LEN), lambda s, h, *_: (s, h, 0, 0)),
            ],
            scratch_shapes=[pltpu.VMEM((SEQ_LEN // BLOCK, HEAD_DIM, BLOCK), BF16)],
        ),
        out_shape=[
            jax.ShapeDtypeStruct(projected.shape, BF16),
            jax.ShapeDtypeStruct((rows, heads * HEAD_DIM), BF16),
            jax.ShapeDtypeStruct((seq_count, heads, 1, SEQ_LEN), F32),
        ],
        compiler_params=pltpu.CompilerParams(vmem_limit_bytes=40 << 20),
        cost_estimate=pl.CostEstimate(
            flops=4 * rows * SEQ_LEN * HEAD_DIM * heads,
            bytes_accessed=rows * heads * HEAD_DIM * 20,
            transcendentals=rows * SEQ_LEN * heads,
        ),
        name="attend_forward",
    )(bounds, projected, cosine, sine, low[:, None], high[:, None])


def attend_backward_kernel(
    bounds, packed, mixed, grad_mixed, peaks, cosine, sine, low, high, grad, keys_t, inner, grad_queries_t, grad_keys, grad_values
):
    seq = pl.program_id(0)
    score_scale = HEAD_DIM ** (-0.5)
    for b in range(SEQ_LEN // BLOCK):
        part = slice(b * BLOCK, (b + 1) * BLOCK)
        keys_t[b] = packed[part, HEAD_DIM : 2 * HEAD_DIM].astype(F32).T.astype(BF16)
        both = grad_mixed[part, :].astype(F32) * mixed[part, :].astype(F32)
        inner[b] = jnp.sum(both.T, axis=0, keepdims=True)
    grad_keys[...] = jnp.zeros_like(grad_keys)
    grad_values[...] = jnp.zeros_like(grad_values)

    def queries_block(b, _):
        start = pl.multiple_of(b * BLOCK, BLOCK)
        queries = packed[pl.ds(start, BLOCK), :HEAD_DIM]
        pulled = grad_mixed[pl.ds(start, BLOCK), :]
        first = low[0, 0, pl.ds(start, BLOCK)][None, :]
        last = high[0, 0, pl.ds(start, BLOCK)][None, :]
        peak = peaks[0, 0, 0, pl.ds(start, BLOCK)][None, :]
        inner_sum = inner[b]

        def keys_block(j, total):
            part = pl.ds(pl.multiple_of(j * BLOCK, BLOCK), BLOCK)
            keys = packed[part, HEAD_DIM : 2 * HEAD_DIM]
            values = packed[part, 2 * HEAD_DIM :]
            scores = dot(keys, queries, ROWS) * score_scale
            place = lax.broadcasted_iota(jnp.int32, (BLOCK, BLOCK), 0) + j * BLOCK
            scores = jnp.where((place >= first) & (place <= last), scores, masked_score)
            probs = jnp.exp(scores - peak)
            grad_probs = dot(values, pulled, ROWS)
            grad_scores = (probs * (grad_probs - inner_sum)).astype(BF16)
            grad_values[part, :] += jnp.dot(probs.astype(BF16), pulled, preferred_element_type=F32)
            grad_keys[part, :] += jnp.dot(grad_scores, queries, preferred_element_type=F32)
            return total + jnp.dot(keys_t[j], grad_scores, preferred_element_type=F32)

        total = lax.fori_loop(
            bounds[seq, b, 0], bounds[seq, b, 1], keys_block, jnp.zeros((HEAD_DIM, BLOCK), F32)
        )
        grad_queries = total.T * score_scale
        rows = pl.ds(start, BLOCK)
        grad[rows, :HEAD_DIM] = turned(grad_queries, cosine[rows, :], -sine[rows, :]).astype(BF16)
        return 0

    lax.fori_loop(0, SEQ_LEN // BLOCK, queries_block, 0)
    grad[:, HEAD_DIM : 2 * HEAD_DIM] = turned(
        grad_keys[...] * score_scale, cosine[...], -sine[...]
    ).astype(BF16)
    grad[:, 2 * HEAD_DIM :] = grad_values[...].astype(BF16)


def attend_backward(packed, mixed, grad_mixed, peaks, cosine, sine, low, high, bounds):
    seq_count, heads = cosine.shape[0], packed.shape[1] // (3 * HEAD_DIM)
    rows = seq_count * SEQ_LEN
    per_head = pl.BlockSpec((SEQ_LEN, 3 * HEAD_DIM), lambda s, h, *_: (s, h))
    single = pl.BlockSpec((SEQ_LEN, HEAD_DIM), lambda s, h, *_: (s, h))
    table = pl.BlockSpec((None, SEQ_LEN, HEAD_DIM), lambda s, h, *_: (s, 0, 0))
    line = pl.BlockSpec((1, 1, SEQ_LEN), lambda s, h, *_: (s, 0, 0))
    blocks = SEQ_LEN // BLOCK
    return pl.pallas_call(
        attend_backward_kernel,
        grid_spec=pltpu.PrefetchScalarGridSpec(
            num_scalar_prefetch=1,
            grid=(seq_count, heads),
            in_specs=[
                per_head,
                single,
                single,
                pl.BlockSpec((1, 1, 1, SEQ_LEN), lambda s, h, *_: (s, h, 0, 0)),
                table,
                table,
                line,
                line,
            ],
            out_specs=per_head,
            scratch_shapes=[
                pltpu.VMEM((blocks, HEAD_DIM, BLOCK), BF16),
                pltpu.VMEM((blocks, 1, BLOCK), F32),
                pltpu.VMEM((blocks, HEAD_DIM, BLOCK), F32),
                pltpu.VMEM((SEQ_LEN, HEAD_DIM), F32),
                pltpu.VMEM((SEQ_LEN, HEAD_DIM), F32),
            ],
        ),
        out_shape=jax.ShapeDtypeStruct(packed.shape, BF16),
        compiler_params=pltpu.CompilerParams(vmem_limit_bytes=40 << 20),
        cost_estimate=pl.CostEstimate(
            flops=10 * rows * SEQ_LEN * HEAD_DIM * heads,
            bytes_accessed=rows * heads * HEAD_DIM * 20,
            transcendentals=rows * SEQ_LEN * heads,
        ),
        name="attend_backward",
    )(bounds, packed, mixed, grad_mixed, peaks, cosine, sine, low[:, None], high[:, None])


class Ring:
    def __init__(self, count, rows, buffer, sems):
        self.chips, self.rows, self.buffer = count // 2, rows, buffer
        self.ring_send, self.ring_recv, self.core_send, self.core_recv = sems
        me = lax.axis_index("tp")
        self.core, self.chip = me % 2, me // 2
        self.spot = self.place(self.chip)
        self.way = 1 - 2 * self.core
        self.next = self.place((self.spot + self.way + self.chips) % self.chips) * 2 + self.core
        self.last = self.place((self.spot - self.way + self.chips) % self.chips) * 2 + self.core
        self.me, self.mate = me, me + self.way

    def place(self, spot):
        turn = self.chips // 2
        return spot + (spot // turn) * (self.chips - 1 + turn - 2 * spot)

    def origin(self, hop):
        return self.place((self.spot - hop * self.way + hop * self.chips) % self.chips) * 2 + self.core

    def mates_origin(self, hop):
        spot = (self.spot + hop * self.way + hop * self.chips) % self.chips
        return self.place(spot) * 2 + 1 - self.core

    def part(self, device, half):
        size = self.rows // 2
        return pl.ds(pl.multiple_of(device * self.rows + half * size, size), size)

    def copy(self, device, half, send, recv, to):
        part = self.buffer.at[self.part(device, half), :]
        return pltpu.make_async_remote_copy(
            src_ref=part,
            dst_ref=part,
            send_sem=send,
            recv_sem=recv,
            device_id={"tp": to},
            device_id_type=pl.DeviceIdType.MESH,
        )

    def greet(self):
        barrier = pltpu.get_barrier_semaphore()
        for other in (self.next, self.last, self.mate):
            pl.semaphore_signal(
                barrier, inc=1, device_id={"tp": other}, device_id_type=pl.DeviceIdType.MESH
            )
        return barrier

    def along(self, hop, half, device):
        return self.copy(device, half, self.ring_send.at[hop, half], self.ring_recv.at[hop, half], self.next)

    def across(self, hop, half, device):
        return self.copy(device, half, self.core_send.at[hop, half], self.core_recv.at[hop, half], self.mate)

    def begin(self):
        for half in range(2):
            self.along(0, half, self.me).start()
            self.across(0, half, self.me).start()

    def advance(self, hop):
        device = self.origin(hop)
        for half in range(2):
            self.along(hop - 1, half, device).wait_recv()
            if hop < self.chips - 1:
                self.along(hop, half, device).start()
            self.across(hop, half, device).start()

    def from_mate(self, hop):
        device = self.mates_origin(hop)
        for half in range(2):
            self.across(hop, half, device).wait_recv()

    def finish(self):
        for half in range(2):
            for hop in range(self.chips):
                if hop < self.chips - 1:
                    self.along(hop, half, self.me).wait_send()
                self.across(hop, half, self.me).wait_send()


def ring_sems(count):
    chips = count // 2
    return [pltpu.SemaphoreType.DMA((chips, 2))] * 4


def project_kernel(count, tokens, gains, offsets, weight, bias, projected, gathered, buffer, *rest):
    sems, out_sem = rest[:4], rest[4]
    rows = tokens.shape[0]
    ring = Ring(count, rows, buffer, sems)
    barrier = ring.greet()
    hat, _ = normalize(tokens[...].astype(F32))
    own = pl.ds(pl.multiple_of(ring.me * rows, rows), rows)
    buffer[own, :] = (hat * gains[...] + offsets[...]).astype(BF16)
    pl.semaphore_wait(barrier, 3)
    ring.begin()

    def keep(device):
        part = pl.ds(pl.multiple_of(device * rows, rows), rows)
        return pltpu.make_async_copy(buffer.at[part, :], gathered.at[part, :], out_sem.at[device])

    def work(device):
        part = pl.ds(pl.multiple_of(device * rows, rows), rows)
        keep(device).start()
        projected[part, :] = (
            jnp.dot(buffer[part, :], weight[...], preferred_element_type=F32) + bias[...]
        )

    work(ring.me)
    ring.from_mate(0)
    work(ring.mate)
    for hop in range(1, ring.chips):
        ring.advance(hop)
        work(ring.origin(hop))
        ring.from_mate(hop)
        work(ring.mates_origin(hop))
    ring.finish()
    for device in range(count):
        keep(device).wait()


def project(count, tokens, gains, offsets, weight, bias):
    rows, width = tokens.shape
    columns = weight.shape[1]
    total = rows * count
    vmem = pl.BlockSpec(memory_space=pltpu.VMEM)
    return pl.pallas_call(
        functools.partial(project_kernel, count),
        in_specs=[vmem] * 5,
        out_specs=[vmem, pl.BlockSpec(memory_space=pl.ANY)],
        out_shape=[
            jax.ShapeDtypeStruct((total, columns), F32),
            jax.ShapeDtypeStruct((total, width), BF16),
        ],
        scratch_shapes=[pltpu.VMEM((total, width), BF16)]
        + ring_sems(count)
        + [pltpu.SemaphoreType.DMA((count,))],
        compiler_params=pltpu.CompilerParams(
            collective_id=0, has_side_effects=True, vmem_limit_bytes=48 << 20
        ),
        cost_estimate=pl.CostEstimate(
            flops=2 * total * width * columns, bytes_accessed=total * width * 8, transcendentals=0
        ),
        name="project",
    )(tokens, gains, offsets, weight, bias[None])


def feed_kernel(units, second, cotangent, expand, shrink, columns, hidden, grads):
    step = 176 if units % 176 == 0 else units
    for at in range(0, units, step):
        part = slice(at, at + step)
        upper = slice(units + at, units + at + step)
        gate = dot(expand[part, :], second[...], ROWS) + columns[part, 0:1]
        up = dot(expand[upper, :], second[...], ROWS) + columns[part, 1:2]
        grad_hidden = dot(shrink[part, :], cotangent[...], ROWS) * columns[part, 2:3]
        normal = 0.5 * (1.0 + lax.erf(gate * (0.5**0.5)))
        density = jnp.exp(-0.5 * gate * gate) * (0.5 / jnp.pi) ** 0.5
        gelu = gate * normal
        hidden[part, :] = (gelu * up * columns[part, 2:3]).astype(BF16)
        grads[part, :] = (grad_hidden * up * (normal + gate * density)).astype(BF16)
        grads[upper, :] = (grad_hidden * gelu).astype(BF16)


def feed(second, cotangent, expand, shrink, columns):
    rows, width = second.shape
    units = shrink.shape[0]
    tile = 256
    tokens = pl.BlockSpec((tile, width), lambda i: (i, 0))
    whole = lambda a: pl.BlockSpec(a.shape, lambda i: (0, 0), pipeline_mode=pl.Buffered(1))
    return pl.pallas_call(
        functools.partial(feed_kernel, units),
        grid=(rows // tile,),
        in_specs=[tokens, tokens, whole(expand), whole(shrink), whole(columns)],
        out_specs=[
            pl.BlockSpec((units, tile), lambda i: (0, i)),
            pl.BlockSpec((2 * units, tile), lambda i: (0, i)),
        ],
        out_shape=[
            jax.ShapeDtypeStruct((units, rows), BF16),
            jax.ShapeDtypeStruct((2 * units, rows), BF16),
        ],
        compiler_params=pltpu.CompilerParams(vmem_limit_bytes=50 << 20),
        cost_estimate=pl.CostEstimate(
            flops=6 * rows * width * units,
            bytes_accessed=4 * rows * width + 6 * units * (rows + width),
            transcendentals=2 * rows * units,
        ),
        name="feed",
    )(second, cotangent, expand, shrink, columns)


def weave_kernel(gate, up, out):
    out[:, 0, :] = gate[...].astype(F32)
    out[:, 1, :] = up[...].astype(F32)


def weave(gate, up):
    rows, width = gate.shape
    tile = 256
    part = pl.BlockSpec((rows, tile), lambda j: (0, j))
    return pl.pallas_call(
        weave_kernel,
        grid=(width // tile,),
        in_specs=[part, part],
        out_specs=pl.BlockSpec((rows, 2, tile), lambda j: (0, 0, j)),
        out_shape=jax.ShapeDtypeStruct((rows, 2, width), F32),
        compiler_params=pltpu.CompilerParams(vmem_limit_bytes=40 << 20),
        cost_estimate=pl.CostEstimate(flops=0, bytes_accessed=12 * rows * width, transcendentals=0),
        name="weave",
    )(gate, up)


def cuts(total, pieces):
    step = -(-total // pieces)
    step = -(-step // 16) * 16
    return [(at, min(at + step, total)) for at in range(0, total, step)]


def local(
    dp,
    tp,
    tokens,
    segment_ids,
    prefix_lengths,
    positions,
    norm_gains,
    norm_offsets,
    input_weight,
    input_offset,
    output_weight,
    output_offset,
    expand_weight,
    expand_offset,
    shrink_weight,
    shrink_offset,
    cotangent,
):
    residual_scale = (2.0 * LAYERS) ** 0.5
    seq_count = segment_ids.shape[0]
    group_rows = seq_count * SEQ_LEN
    width = tokens.shape[1]
    units_used = expand_weight.shape[2]
    units = -(-units_used // 176) * 176
    heads_width = output_weight.shape[0]
    gather = lambda a: lax.all_gather(a, "tp", axis=0, tiled=True)
    scatter = lambda a: lax.psum_scatter(a, "tp", scatter_dimension=0, tiled=True).astype(F32)

    pad = ((0, units - units_used), (0, 0))
    turned_expand = jnp.transpose(expand_weight, (2, 1, 0))
    expand = jnp.concatenate(
        [jnp.pad(turned_expand[:, 0], pad), jnp.pad(turned_expand[:, 1], pad)], axis=0
    )
    shrink = jnp.pad(shrink_weight, pad)
    unit_index = lax.axis_index("tp") * units_used + lax.iota(jnp.int32, units_used)
    keep_units = (unit_index < FF_USED).astype(F32)
    columns = jnp.pad(jnp.stack([expand_offset[0], expand_offset[1], keep_units], axis=1), pad)

    row_at = lax.broadcasted_iota(jnp.int32, positions.shape, 1)
    low = row_at - positions
    matches = segment_ids[:, :, None] == lax.iota(jnp.int32, prefix_lengths.shape[1])
    own_prefix = jnp.sum(jnp.where(matches, prefix_lengths[:, None, :], 0), axis=2)
    high = jnp.maximum(row_at, low + own_prefix - 1)
    bounds = jnp.stack(
        [
            jnp.min(low.reshape(seq_count, -1, BLOCK), axis=2) // BLOCK,
            jnp.max(high.reshape(seq_count, -1, BLOCK), axis=2) // BLOCK + 1,
        ],
        axis=2,
    )
    cosine, sine = rotary_tables(positions)

    first_hat, first_scale = normalize(tokens.astype(F32))
    first_norm = first_hat * norm_gains[0] + norm_offsets[0]
    cotangent_all = gather(cotangent)
    full_output = gather(output_weight)
    projected, first_all = project(
        tp, tokens, norm_gains[:1], norm_offsets[:1], input_weight, input_offset
    )
    packed, mixed, peaks = attend_forward(projected, cosine, sine, low, high, bounds)
    own_heads = lax.all_to_all(mixed, "tp", split_axis=0, concat_axis=1, tiled=True)
    attention = jnp.dot(own_heads, full_output, preferred_element_type=F32) + output_offset
    middle = residual_scale * first_norm + attention
    second_hat, second_scale = normalize(middle)
    second_norm = second_hat * norm_gains[1] + norm_offsets[1]
    second_all = gather(second_norm.astype(BF16))
    hidden, grads = feed(second_all, cotangent_all, expand, shrink, columns)

    line = Line(dp, "dp")
    mul = lambda a, b: jnp.dot(a, b, preferred_element_type=F32).astype(BF16)
    unit_cuts = cuts(units_used, 3)
    width_cuts = cuts(width, 3)
    shrink_part = [None] * 3
    expand_part = [[None] * 3, [None] * 3]
    a, b = unit_cuts[0]
    line.add("s0", mul(hidden[a:b], cotangent_all))

    hidden, cotangent_all, grads, expand = line.turn(hidden, cotangent_all, grads, expand)
    for k in (1, 2):
        a, b = unit_cuts[k]
        line.add("s%d" % k, mul(hidden[a:b], cotangent_all))
    grad_second_part = dot(grads, expand, COLS).astype(BF16)
    line.made(line.waiting[0][1], line.waiting[1][1], grad_second_part)

    grads, second_all, hidden, shrink, grad_second_part = line.turn(
        grads, second_all, hidden, shrink, grad_second_part
    )
    grad_second_sum = scatter(grad_second_part)
    for k in range(3):
        a, b = unit_cuts[k]
        line.add("g%d" % k, mul(grads[a:b], second_all))
    shrink_sum_part = dot(hidden, shrink, COLS).astype(BF16)
    line.made(shrink_sum_part, *[p for _, p in line.waiting[-3:]])

    grads, second_all, shrink_sum_part, cotangent = line.turn(
        grads, second_all, shrink_sum_part, cotangent
    )
    shrink_sum = scatter(shrink_sum_part)
    for k in range(3):
        a, b = unit_cuts[k]
        line.add("u%d" % k, mul(grads[units + a : units + b], second_all))
    expand_offset_grad = jnp.sum(grads.astype(F32), axis=1).reshape(2, units)[:, :units_used]
    grad_output = cotangent.astype(F32)
    shrink_offset_grad = jnp.sum(grad_output, axis=0)
    line.made(expand_offset_grad, shrink_offset_grad, *[p for _, p in line.waiting[-3:]])

    line.turn()

    grad_second_sum, full_output = line.turn(grad_second_sum, full_output)
    grad_second = residual_scale * grad_output + grad_second_sum
    grad_middle, second_gain_grad, second_offset_grad = normalize_back(
        grad_second, norm_gains[1], second_hat, second_scale
    )
    grad_attention = grad_middle.astype(BF16)
    output_offset_grad = jnp.sum(grad_attention.astype(F32), axis=0)
    grad_own = dot(grad_attention, full_output, ROWS).astype(BF16)
    grad_mixed = lax.all_to_all(grad_own, "tp", split_axis=1, concat_axis=0, tiled=True)
    attention_all = gather(grad_attention)
    line.made(grad_mixed, second_gain_grad, second_offset_grad, output_offset_grad)

    grad_mixed, packed, mixed = line.turn(grad_mixed, packed, mixed)
    grad_projected = attend_backward(
        packed, mixed, grad_mixed, peaks, cosine, sine, low, high, bounds
    )
    line.made(grad_projected)

    grad_projected, first_all, input_weight = line.turn(grad_projected, first_all, input_weight)
    grad_first_part = dot(grad_projected, input_weight, ROWS).astype(BF16)
    input_offset_grad = jnp.sum(grad_projected.astype(F32), axis=0)
    line.made(grad_first_part, input_offset_grad)

    grad_projected, first_all, grad_first_part = line.turn(grad_projected, first_all, grad_first_part)
    grad_first_sum = scatter(grad_first_part)
    for k in range(3):
        a, b = width_cuts[k]
        line.add("i%d" % k, dot(first_all[:, a:b], grad_projected, COLS))
    line.made(*[p for _, p in line.waiting[-3:]])

    attention_all, mixed = line.turn(attention_all, mixed)
    line.add("o", dot(mixed, attention_all, COLS))
    line.made(line.waiting[-1][1])

    shrink_sum, second_hat = line.turn(shrink_sum, second_hat)
    layer_out = (
        residual_scale * (second_hat * norm_gains[1] + norm_offsets[1]) + shrink_sum + shrink_offset
    )
    shrink_grad = jnp.concatenate([line.sums["s%d" % k] for k in range(3)]).astype(F32)
    line.made(layer_out, shrink_grad)
    while "u2" not in line.sums:
        line.turn()
    expand_grad = weave(
        jnp.concatenate([line.sums["g%d" % k] for k in range(3)]),
        jnp.concatenate([line.sums["u%d" % k] for k in range(3)]),
    )
    line.made(expand_grad)

    grad_first_sum, grad_middle = line.turn(grad_first_sum, grad_middle)
    grad_first = residual_scale * grad_middle + grad_first_sum
    tokens_grad, first_gain_grad, first_offset_grad = normalize_back(
        grad_first, norm_gains[0], first_hat, first_scale
    )
    line.made(tokens_grad, first_gain_grad, first_offset_grad)
    while line.waiting or line.moving:
        line.turn()

    whole_sums = swap_sum(
        jnp.stack(
            [
                first_gain_grad,
                second_gain_grad,
                first_offset_grad,
                second_offset_grad,
                output_offset_grad,
                shrink_offset_grad,
            ]
        ),
        tp,
        "tp",
    )
    whole_sums = swap_sum(whole_sums, dp, "dp")
    group_sums = swap_sum(
        jnp.concatenate([expand_offset_grad.reshape(-1), input_offset_grad]), dp, "dp"
    )
    return (
        layer_out,
        tokens_grad,
        jnp.concatenate([line.sums["i%d" % k] for k in range(3)]).astype(F32),
        group_sums[2 * units_used :],
        line.sums["o"].astype(F32),
        whole_sums[4],
        jnp.transpose(expand_grad, (2, 1, 0)),
        group_sums[: 2 * units_used].reshape(2, units_used),
        shrink_grad,
        whole_sums[5],
        whole_sums[0:2],
        whole_sums[2:4],
    )


def solution(mesh):
    in_specs = (
        P(("dp", "tp"), None),
        P("dp", None),
        P("dp", None),
        P("dp", None),
        P(),
        P(),
        P(None, "tp"),
        P("tp"),
        P("tp", None),
        P(),
        P(None, None, "tp"),
        P(None, "tp"),
        P("tp", None),
        P(),
        P(("dp", "tp"), None),
    )
    out_specs = (
        P(("dp", "tp"), None),
        P(("dp", "tp"), None),
        P(None, "tp"),
        P("tp"),
        P("tp", None),
        P(),
        P(None, None, "tp"),
        P(None, "tp"),
        P("tp", None),
        P(),
        P(),
        P(),
    )
    return jax.shard_map(
        functools.partial(local, mesh.shape["dp"], mesh.shape["tp"]),
        mesh=mesh,
        in_specs=in_specs,
        out_specs=out_specs,
        check_vma=False,
    )
```

```python
import functools

import jax
import jax.numpy as jnp
from jax import lax
from jax.experimental import pallas as pl
from jax.experimental.pallas import tpu as pltpu
from jax.sharding import PartitionSpec as P

HEAD_DIM = 128
FF_USED = 5461
LAYERS = 24
SEQ_LEN = 1024
BLOCK = 256
TILE = 512
UNITS = 176

epsilon = 1e-05
rope_base = 10000.0
masked_score = -1e30
F32 = jnp.float32
BF16 = jnp.bfloat16
ROWS = (((1,), (1,)), ((), ()))
MESH = pl.DeviceIdType.MESH
COLS = (((0,), (0,)), ((), ()))


def dot(left, right, dims):
    return lax.dot_general(left, right, dims, preferred_element_type=F32)


def normalize(values):
    average = jnp.mean(values, axis=-1, keepdims=True)
    centred = values - average
    variance = jnp.mean(centred * centred, axis=-1, keepdims=True)
    scale = lax.rsqrt(variance + epsilon)
    return centred * scale, scale


def normalize_back(grad, gains, hat, scale):
    pulled = grad * gains
    grad_in = scale * (
        pulled
        - jnp.mean(pulled, axis=-1, keepdims=True)
        - hat * jnp.mean(pulled * hat, axis=-1, keepdims=True)
    )
    return grad_in, jnp.sum(grad * hat, axis=0), jnp.sum(grad, axis=0)


def rotary_tables(places):
    half_dim = HEAD_DIM // 2
    exponents = lax.iota(F32, half_dim) * (-2.0 / HEAD_DIM)
    rates = jnp.power(rope_base, exponents)
    angles = places.astype(F32)[..., None] * rates
    cosine, sine = jnp.cos(angles), jnp.sin(angles)
    return jnp.concatenate([cosine, cosine], -1), jnp.concatenate([-sine, sine], -1)


def swap_sum(values, count, axis):
    bit = 1
    while bit < count:
        values = values + lax.ppermute(values, axis, [(i, i ^ bit) for i in range(count)])
        bit *= 2
    return values


def turned(values, cosine, sine):
    return values * cosine + pltpu.roll(values, HEAD_DIM // 2, 1) * sine


def attend_forward_kernel(bounds, projected, cosine, sine, low, high, packed, mixed, peaks, values_t):
    seq = pl.program_id(0)
    score_scale = HEAD_DIM ** (-0.5)
    packed[:, :HEAD_DIM] = turned(projected[:, :HEAD_DIM], cosine[...], sine[...]).astype(BF16)
    packed[:, HEAD_DIM : 2 * HEAD_DIM] = turned(
        projected[:, HEAD_DIM : 2 * HEAD_DIM], cosine[...], sine[...]
    ).astype(BF16)
    packed[:, 2 * HEAD_DIM :] = projected[:, 2 * HEAD_DIM :].astype(BF16)
    for b in range(SEQ_LEN // BLOCK):
        values_t[b] = projected[b * BLOCK : (b + 1) * BLOCK, 2 * HEAD_DIM :].T.astype(BF16)

    def queries_block(b, _):
        start = pl.multiple_of(b * BLOCK, BLOCK)
        queries = packed[pl.ds(start, BLOCK), :HEAD_DIM]
        first = low[0, 0, pl.ds(start, BLOCK)][None, :]
        last = high[0, 0, pl.ds(start, BLOCK)][None, :]

        def keys_block(j, carry):
            peak, total, gathered = carry
            keys = packed[pl.ds(pl.multiple_of(j * BLOCK, BLOCK), BLOCK), HEAD_DIM : 2 * HEAD_DIM]
            scores = dot(keys, queries, ROWS) * score_scale
            place = lax.broadcasted_iota(jnp.int32, (BLOCK, BLOCK), 0) + j * BLOCK
            scores = jnp.where((place >= first) & (place <= last), scores, masked_score)
            new_peak = jnp.maximum(peak, jnp.max(scores, axis=0, keepdims=True))
            shifted = jnp.exp(scores - new_peak)
            fade = jnp.exp(peak - new_peak)
            total = total * fade + jnp.sum(shifted, axis=0, keepdims=True)
            gathered = gathered * fade + jnp.dot(
                values_t[j], shifted.astype(BF16), preferred_element_type=F32
            )
            return new_peak, total, gathered

        peak, total, gathered = lax.fori_loop(
            bounds[seq, b, 0],
            bounds[seq, b, 1],
            keys_block,
            (
                jnp.full((1, BLOCK), masked_score, F32),
                jnp.zeros((1, BLOCK), F32),
                jnp.zeros((HEAD_DIM, BLOCK), F32),
            ),
        )
        mixed[pl.ds(start, BLOCK), :] = (gathered / total).T.astype(BF16)
        peaks[0, 0, 0, pl.ds(start, BLOCK)] = (peak + jnp.log(total))[0]
        return 0

    lax.fori_loop(0, SEQ_LEN // BLOCK, queries_block, 0)


def attend_forward(projected, cosine, sine, low, high, bounds):
    seq_count, heads = cosine.shape[0], projected.shape[1] // (3 * HEAD_DIM)
    rows = seq_count * SEQ_LEN
    per_head = pl.BlockSpec((SEQ_LEN, 3 * HEAD_DIM), lambda s, h, *_: (s, h))
    table = pl.BlockSpec((None, SEQ_LEN, HEAD_DIM), lambda s, h, *_: (s, 0, 0))
    line = pl.BlockSpec((1, 1, SEQ_LEN), lambda s, h, *_: (s, 0, 0))
    return pl.pallas_call(
        attend_forward_kernel,
        grid_spec=pltpu.PrefetchScalarGridSpec(
            num_scalar_prefetch=1,
            grid=(seq_count, heads),
            in_specs=[per_head, table, table, line, line],
            out_specs=[
                per_head,
                pl.BlockSpec((SEQ_LEN, HEAD_DIM), lambda s, h, *_: (s, h)),
                pl.BlockSpec((1, 1, 1, SEQ_LEN), lambda s, h, *_: (s, h, 0, 0)),
            ],
            scratch_shapes=[pltpu.VMEM((SEQ_LEN // BLOCK, HEAD_DIM, BLOCK), BF16)],
        ),
        out_shape=[
            jax.ShapeDtypeStruct(projected.shape, BF16),
            jax.ShapeDtypeStruct((rows, heads * HEAD_DIM), BF16),
            jax.ShapeDtypeStruct((seq_count, heads, 1, SEQ_LEN), F32),
        ],
        compiler_params=pltpu.CompilerParams(vmem_limit_bytes=40 << 20),
        cost_estimate=pl.CostEstimate(
            flops=4 * rows * SEQ_LEN * HEAD_DIM * heads,
            bytes_accessed=rows * heads * HEAD_DIM * 20,
            transcendentals=rows * SEQ_LEN * heads,
        ),
        name="attend_forward",
    )(bounds, projected, cosine, sine, low[:, None], high[:, None])


def attend_backward_kernel(
    bounds, packed, mixed, grad_mixed, peaks, cosine, sine, low, high, grad, keys_t, inner, grad_queries_t, grad_keys, grad_values
):
    seq = pl.program_id(0)
    score_scale = HEAD_DIM ** (-0.5)
    for b in range(SEQ_LEN // BLOCK):
        part = slice(b * BLOCK, (b + 1) * BLOCK)
        keys_t[b] = packed[part, HEAD_DIM : 2 * HEAD_DIM].astype(F32).T.astype(BF16)
        both = grad_mixed[part, :].astype(F32) * mixed[part, :].astype(F32)
        inner[b] = jnp.sum(both.T, axis=0, keepdims=True)
    grad_keys[...] = jnp.zeros_like(grad_keys)
    grad_values[...] = jnp.zeros_like(grad_values)

    def queries_block(b, _):
        start = pl.multiple_of(b * BLOCK, BLOCK)
        queries = packed[pl.ds(start, BLOCK), :HEAD_DIM]
        pulled = grad_mixed[pl.ds(start, BLOCK), :]
        first = low[0, 0, pl.ds(start, BLOCK)][None, :]
        last = high[0, 0, pl.ds(start, BLOCK)][None, :]
        peak = peaks[0, 0, 0, pl.ds(start, BLOCK)][None, :]
        inner_sum = inner[b]

        def keys_block(j, total):
            part = pl.ds(pl.multiple_of(j * BLOCK, BLOCK), BLOCK)
            keys = packed[part, HEAD_DIM : 2 * HEAD_DIM]
            values = packed[part, 2 * HEAD_DIM :]
            scores = dot(keys, queries, ROWS) * score_scale
            place = lax.broadcasted_iota(jnp.int32, (BLOCK, BLOCK), 0) + j * BLOCK
            scores = jnp.where((place >= first) & (place <= last), scores, masked_score)
            probs = jnp.exp(scores - peak)
            grad_probs = dot(values, pulled, ROWS)
            grad_scores = (probs * (grad_probs - inner_sum)).astype(BF16)
            grad_values[part, :] += jnp.dot(probs.astype(BF16), pulled, preferred_element_type=F32)
            grad_keys[part, :] += jnp.dot(grad_scores, queries, preferred_element_type=F32)
            return total + jnp.dot(keys_t[j], grad_scores, preferred_element_type=F32)

        total = lax.fori_loop(
            bounds[seq, b, 0], bounds[seq, b, 1], keys_block, jnp.zeros((HEAD_DIM, BLOCK), F32)
        )
        grad_queries = total.T * score_scale
        rows = pl.ds(start, BLOCK)
        grad[rows, :HEAD_DIM] = turned(grad_queries, cosine[rows, :], -sine[rows, :]).astype(BF16)
        return 0

    lax.fori_loop(0, SEQ_LEN // BLOCK, queries_block, 0)
    grad[:, HEAD_DIM : 2 * HEAD_DIM] = turned(
        grad_keys[...] * score_scale, cosine[...], -sine[...]
    ).astype(BF16)
    grad[:, 2 * HEAD_DIM :] = grad_values[...].astype(BF16)


def attend_backward(packed, mixed, grad_mixed, peaks, cosine, sine, low, high, bounds):
    seq_count, heads = cosine.shape[0], packed.shape[1] // (3 * HEAD_DIM)
    rows = seq_count * SEQ_LEN
    per_head = pl.BlockSpec((SEQ_LEN, 3 * HEAD_DIM), lambda s, h, *_: (s, h))
    single = pl.BlockSpec((SEQ_LEN, HEAD_DIM), lambda s, h, *_: (s, h))
    table = pl.BlockSpec((None, SEQ_LEN, HEAD_DIM), lambda s, h, *_: (s, 0, 0))
    line = pl.BlockSpec((1, 1, SEQ_LEN), lambda s, h, *_: (s, 0, 0))
    blocks = SEQ_LEN // BLOCK
    return pl.pallas_call(
        attend_backward_kernel,
        grid_spec=pltpu.PrefetchScalarGridSpec(
            num_scalar_prefetch=1,
            grid=(seq_count, heads),
            in_specs=[
                per_head,
                single,
                single,
                pl.BlockSpec((1, 1, 1, SEQ_LEN), lambda s, h, *_: (s, h, 0, 0)),
                table,
                table,
                line,
                line,
            ],
            out_specs=per_head,
            scratch_shapes=[
                pltpu.VMEM((blocks, HEAD_DIM, BLOCK), BF16),
                pltpu.VMEM((blocks, 1, BLOCK), F32),
                pltpu.VMEM((blocks, HEAD_DIM, BLOCK), F32),
                pltpu.VMEM((SEQ_LEN, HEAD_DIM), F32),
                pltpu.VMEM((SEQ_LEN, HEAD_DIM), F32),
            ],
        ),
        out_shape=jax.ShapeDtypeStruct(packed.shape, BF16),
        compiler_params=pltpu.CompilerParams(vmem_limit_bytes=40 << 20),
        cost_estimate=pl.CostEstimate(
            flops=10 * rows * SEQ_LEN * HEAD_DIM * heads,
            bytes_accessed=rows * heads * HEAD_DIM * 20,
            transcendentals=rows * SEQ_LEN * heads,
        ),
        name="attend_backward",
    )(bounds, packed, mixed, grad_mixed, peaks, cosine, sine, low[:, None], high[:, None])


class Ring:
    def __init__(self, count, rows, buffer, sems):
        self.chips, self.rows, self.buffer = count // 2, rows, buffer
        self.ring_send, self.ring_recv, self.core_send, self.core_recv = sems
        me = lax.axis_index("tp")
        self.core, self.chip = me % 2, me // 2
        self.spot = self.place(self.chip)
        self.way = 1 - 2 * self.core
        self.next = self.place((self.spot + self.way + self.chips) % self.chips) * 2 + self.core
        self.last = self.place((self.spot - self.way + self.chips) % self.chips) * 2 + self.core
        self.me, self.mate = me, me + self.way

    def place(self, spot):
        turn = self.chips // 2
        return spot + (spot // turn) * (self.chips - 1 + turn - 2 * spot)

    def origin(self, hop):
        return self.place((self.spot - hop * self.way + hop * self.chips) % self.chips) * 2 + self.core

    def mates_origin(self, hop):
        spot = (self.spot + hop * self.way + hop * self.chips) % self.chips
        return self.place(spot) * 2 + 1 - self.core

    def part(self, device, half):
        size = self.rows // 2
        return pl.ds(pl.multiple_of(device * self.rows + half * size, size), size)

    def copy(self, device, half, send, recv, to):
        part = self.buffer.at[self.part(device, half), :]
        return pltpu.make_async_remote_copy(
            src_ref=part,
            dst_ref=part,
            send_sem=send,
            recv_sem=recv,
            device_id={"tp": to},
            device_id_type=MESH,
        )

    def greet(self):
        barrier = pltpu.get_barrier_semaphore()
        for other in (self.next, self.last, self.mate):
            pl.semaphore_signal(
                barrier, inc=1, device_id={"tp": other}, device_id_type=MESH
            )
        return barrier

    def along(self, hop, half, device):
        return self.copy(device, half, self.ring_send.at[hop, half], self.ring_recv.at[hop, half], self.next)

    def across(self, hop, half, device):
        return self.copy(device, half, self.core_send.at[hop, half], self.core_recv.at[hop, half], self.mate)

    def begin(self):
        for half in range(2):
            self.along(0, half, self.me).start()
            self.across(0, half, self.me).start()

    def advance(self, hop):
        device = self.origin(hop)
        for half in range(2):
            self.along(hop - 1, half, device).wait_recv()
            if hop < self.chips - 1:
                self.along(hop, half, device).start()
            self.across(hop, half, device).start()

    def from_mate(self, hop):
        device = self.mates_origin(hop)
        for half in range(2):
            self.across(hop, half, device).wait_recv()

    def finish(self):
        for half in range(2):
            for hop in range(self.chips):
                if hop < self.chips - 1:
                    self.along(hop, half, self.me).wait_send()
                self.across(hop, half, self.me).wait_send()


def ring_sems(count):
    chips = count // 2
    return [pltpu.SemaphoreType.DMA((chips, 2))] * 4


def project_kernel(count, tokens, gains, offsets, weight, bias, projected, gathered, buffer, *rest):
    sems, out_sem = rest[:4], rest[4]
    rows = tokens.shape[0]
    ring = Ring(count, rows, buffer, sems)
    barrier = ring.greet()
    hat, _ = normalize(tokens[...].astype(F32))
    own = pl.ds(pl.multiple_of(ring.me * rows, rows), rows)
    buffer[own, :] = (hat * gains[...] + offsets[...]).astype(BF16)
    pl.semaphore_wait(barrier, 3)
    ring.begin()

    def keep(device):
        part = pl.ds(pl.multiple_of(device * rows, rows), rows)
        return pltpu.make_async_copy(buffer.at[part, :], gathered.at[part, :], out_sem.at[device])

    def work(device):
        part = pl.ds(pl.multiple_of(device * rows, rows), rows)
        keep(device).start()
        projected[part, :] = (
            jnp.dot(buffer[part, :], weight[...], preferred_element_type=F32) + bias[...]
        )

    work(ring.me)
    ring.from_mate(0)
    work(ring.mate)
    for hop in range(1, ring.chips):
        ring.advance(hop)
        work(ring.origin(hop))
        ring.from_mate(hop)
        work(ring.mates_origin(hop))
    ring.finish()
    for device in range(count):
        keep(device).wait()


def project(count, tokens, gains, offsets, weight, bias):
    rows, width = tokens.shape
    columns = weight.shape[1]
    total = rows * count
    vmem = pl.BlockSpec(memory_space=pltpu.VMEM)
    return pl.pallas_call(
        functools.partial(project_kernel, count),
        in_specs=[vmem] * 5,
        out_specs=[vmem, pl.BlockSpec(memory_space=pl.ANY)],
        out_shape=[
            jax.ShapeDtypeStruct((total, columns), F32),
            jax.ShapeDtypeStruct((total, width), BF16),
        ],
        scratch_shapes=[pltpu.VMEM((total, width), BF16)]
        + ring_sems(count)
        + [pltpu.SemaphoreType.DMA((count,))],
        compiler_params=pltpu.CompilerParams(
            collective_id=0, has_side_effects=True, vmem_limit_bytes=48 << 20
        ),
        cost_estimate=pl.CostEstimate(
            flops=2 * total * width * columns, bytes_accessed=total * width * 8, transcendentals=0
        ),
        name="project",
    )(tokens, gains, offsets, weight, bias[None])


class Scatter:
    def __init__(self, ring, give, take, passing, total, sems):
        self.ring, self.give, self.take, self.passing, self.total = ring, give, take, passing, total
        self.give_send, self.give_recv, self.pass_send, self.pass_recv, self.again = sems

    def handed(self, far, half):
        size = self.ring.rows // 2
        part = pl.ds(half * size, size)
        return pltpu.make_async_remote_copy(
            src_ref=self.give.at[far % 2, part, :],
            dst_ref=self.take.at[far, part, :],
            send_sem=self.give_send.at[far, half],
            recv_sem=self.give_recv.at[far, half],
            device_id={"tp": self.ring.mate},
            device_id_type=MESH,
        )

    def passed(self, far, half):
        size = self.ring.rows // 2
        part = pl.ds(half * size, size)
        return pltpu.make_async_remote_copy(
            src_ref=self.passing.at[far, part, :],
            dst_ref=self.passing.at[far - 1, part, :],
            send_sem=self.pass_send.at[far, half],
            recv_sem=self.pass_recv.at[far - 1, half],
            device_id={"tp": self.ring.next},
            device_id_type=MESH,
        )

    def run(self, make, beside=lambda far: None):
        ring = self.ring
        chips, size = ring.chips, ring.rows // 2
        for far in reversed(range(chips)):
            if far < chips - 2:
                for half in range(2):
                    self.handed(far + 2, half).wait_send()
            make(ring.origin(far) + ring.way, self.give.at[far % 2])
            for half in range(2):
                self.handed(far, half).start()
            make(ring.origin(chips - far), self.total)
            beside(far)
            for half in range(2):
                self.handed(far, half).wait_recv()
                if far < chips - 1:
                    self.passed(far + 1, half).wait_recv()

                @pl.loop(0, size // 16)
                def _(row):
                    part = pl.ds(pl.multiple_of(half * size + row * 16, 16), 16)
                    value = self.total[part, :] + self.take[far, part, :].astype(F32)
                    if far < chips - 1:
                        value = value + self.passing[far, part, :].astype(F32)
                    if far > 0:
                        self.passing[far, part, :] = value.astype(BF16)
                    else:
                        self.total[part, :] = value

                if far > 0:
                    self.passed(far, half).start()
        for half in range(2):
            for far in range(chips):
                if far < 2:
                    self.handed(far, half).wait_send()
                if far > 0:
                    self.passed(far, half).wait_send()

    def release(self):
        for other in (self.ring.last, self.ring.mate):
            pl.semaphore_signal(self.again, inc=1, device_id={"tp": other}, device_id_type=MESH)
        pl.semaphore_wait(self.again, 2)


def scatter_space(count, rows, width):
    chips = count // 2
    return [
        pltpu.VMEM((2, rows, width), BF16),
        pltpu.VMEM((chips, rows, width), BF16),
        pltpu.VMEM((chips, rows, width), BF16),
        pltpu.VMEM((rows, width), F32),
    ]


def scatter_sems(count):
    return [pltpu.SemaphoreType.DMA((count // 2, 2))] * 4 + [pltpu.SemaphoreType.REGULAR]


SLOTS = 4
LANDINGS = 3
PIECE = 128


class Line:
    def __init__(self, count, pieces, held, came, crossed, sems):
        self.pieces, self.held, self.came, self.crossed = pieces, held, came, crossed
        (
            self.load_sem,
            self.keep_sem,
            self.in_send,
            self.in_recv,
            self.mid_send,
            self.mid_recv,
            self.out_send,
            self.out_recv,
            self.in_free,
            self.mid_free,
        ) = sems
        here = lax.axis_index("dp")
        half = count // 2
        side = here // half
        self.count, self.half = count, half
        self.inner, self.outer = here + 1 - 2 * side, here - 1 + 2 * side
        self.depth = here + side * (count - 1 - 2 * here)
        self.end, self.middle = self.depth == 0, self.depth == half - 1

    def greet(self, barrier):
        pl.semaphore_signal(barrier, inc=1, device_id={"dp": self.inner}, device_id_type=MESH)

        @pl.when(self.depth > 0)
        def _():
            pl.semaphore_signal(barrier, inc=1, device_id={"dp": self.outer}, device_id_type=MESH)

    def met(self, barrier, others):
        @pl.when(self.depth == 0)
        def _():
            pl.semaphore_wait(barrier, others + 1)

        @pl.when(self.depth > 0)
        def _():
            pl.semaphore_wait(barrier, others + 2)

    def rows(self, k):
        return self.pieces[k][0].shape[0]

    def sent(self, source, target, send, recv, to):
        return pltpu.make_async_remote_copy(
            src_ref=source,
            dst_ref=target,
            send_sem=send,
            recv_sem=recv,
            device_id={"dp": to},
            device_id_type=MESH,
        )

    def inward(self, k, source):
        landing = self.came.at[k % LANDINGS, pl.ds(0, self.rows(k)), :]
        return self.sent(source, landing, self.in_send.at[k], self.in_recv.at[k], self.inner)

    def across(self, k):
        part = pl.ds(0, self.rows(k))
        return self.sent(
            self.held.at[k % SLOTS, part, :],
            self.crossed.at[k % LANDINGS, part, :],
            self.mid_send.at[k],
            self.mid_recv.at[k],
            self.inner,
        )

    def outward(self, k, source):
        return self.sent(source, self.pieces[k][1], self.out_send.at[k], self.out_recv.at[k], self.outer)

    def slot(self, k):
        return self.held.at[k % SLOTS, pl.ds(0, self.rows(k)), :]

    def load(self, k):
        return pltpu.make_async_copy(self.pieces[k][0], self.slot(k), self.load_sem.at[k])

    def keep(self, k):
        return pltpu.make_async_copy(self.slot(k), self.pieces[k][1], self.keep_sem.at[k])

    def begin(self, k):
        @pl.when(self.end)
        def _():
            if k >= LANDINGS:
                pl.semaphore_wait(self.in_free, 1)
            self.inward(k, self.pieces[k][0]).start()

    def free(self, k):
        @pl.when(self.middle)
        def _():
            self.outward(k, self.slot(k)).wait_send()
            self.keep(k).wait()

        if self.half > 2:

            @pl.when((self.depth > 0) & (self.depth < self.half - 1))
            def _():
                self.inward(k, self.slot(k)).wait_send()

    def ready(self, k):
        if k >= SLOTS:
            self.free(k - SLOTS)

        @pl.when(self.depth > 0)
        def _():
            self.load(k).start()

    def add(self, k, other):
        slot = self.held.at[k % SLOTS]

        @pl.loop(0, self.rows(k) // 16)
        def _(row):
            part = pl.ds(pl.multiple_of(row * 16, 16), 16)
            slot[part, :] = (
                slot[part, :].astype(F32) + other[k % LANDINGS, part, :].astype(F32)
            ).astype(BF16)

    def join(self, k):
        @pl.when(self.depth > 0)
        def _():
            self.load(k).wait()
            self.inward(k, self.slot(k)).wait_recv()
            self.add(k, self.came)
            if k + LANDINGS < len(self.pieces):
                pl.semaphore_signal(
                    self.in_free, inc=1, device_id={"dp": self.outer}, device_id_type=MESH
                )

        @pl.when(self.middle)
        def _():
            if k >= LANDINGS:
                pl.semaphore_wait(self.mid_free, 1)
            self.across(k).start()

        if self.half > 2:

            @pl.when((self.depth > 0) & (self.depth < self.half - 1))
            def _():
                if k >= LANDINGS:
                    pl.semaphore_wait(self.in_free, 1)
                self.inward(k, self.slot(k)).start()

    def close(self, k):
        @pl.when(self.middle)
        def _():
            self.across(k).wait_recv()
            self.across(k).wait_send()
            self.add(k, self.crossed)
            if k + LANDINGS < len(self.pieces):
                pl.semaphore_signal(
                    self.mid_free, inc=1, device_id={"dp": self.inner}, device_id_type=MESH
                )
            self.outward(k, self.slot(k)).start()
            self.keep(k).start()

    def spread(self, k):
        @pl.when(self.depth < self.half - 1)
        def _():
            self.outward(k, self.pieces[k][1]).wait_recv()

        if self.half > 2:

            @pl.when((self.depth > 0) & (self.depth < self.half - 1))
            def _():
                self.outward(k, self.pieces[k][1]).start()

    def finish(self):
        total = len(self.pieces)
        for k in range(max(0, total - SLOTS), total):
            self.free(k)
        for k in range(total):

            @pl.when(self.end)
            def _():
                self.inward(k, self.pieces[k][0]).wait_send()

            if self.half > 2:

                @pl.when((self.depth > 0) & (self.depth < self.half - 1))
                def _():
                    self.outward(k, self.pieces[k][1]).wait_send()


def line_space(width):
    return [
        pltpu.VMEM((SLOTS, PIECE, width), BF16),
        pltpu.VMEM((LANDINGS, PIECE, width), BF16),
        pltpu.VMEM((LANDINGS, PIECE, width), BF16),
    ]


def line_sems(pieces):
    return [pltpu.SemaphoreType.DMA((pieces,))] * 8 + [pltpu.SemaphoreType.REGULAR] * 2


def piece_rows(start, total):
    return [(start + at, min(PIECE, total - at)) for at in range(0, total, PIECE)]


def middle_kernel(
    count,
    mixed,
    weight,
    tokens,
    gains,
    offsets,
    output_offset,
    gate_weight,
    up_weight,
    columns,
    hidden,
    gate_factor,
    up_factor,
    gathered,
    middle,
    buffer,
    give,
    take,
    passing,
    total,
    *rest,
):
    rows = tokens.shape[0]
    residual_scale = (2.0 * LAYERS) ** 0.5
    ring = Ring(count, rows, buffer, rest[:4])
    scatter = Scatter(ring, give, take, passing, total, rest[4:9])
    out_sem = rest[9]
    pl.semaphore_wait(ring.greet(), 3)

    def make(device, target):
        part = pl.ds(pl.multiple_of(device * rows, rows), rows)

        @pl.loop(0, weight.shape[1] // TILE)
        def _(tile):
            cut = pl.ds(pl.multiple_of(tile * TILE, TILE), TILE)
            target[:, cut] = jnp.dot(
                mixed[part, :], weight[:, cut], preferred_element_type=F32
            ).astype(target.dtype)

    scatter.run(make)
    hat, _ = normalize(tokens[...].astype(F32))
    first = hat * gains[0:1, :] + offsets[0:1, :]
    middle[...] = residual_scale * first + (total[...] + output_offset[...])
    hat, _ = normalize(middle[...])
    own = pl.ds(pl.multiple_of(ring.me * rows, rows), rows)
    buffer[own, :] = (hat * gains[1:2, :] + offsets[1:2, :]).astype(BF16)
    ring.begin()

    def keep(device):
        part = pl.ds(pl.multiple_of(device * rows, rows), rows)
        return pltpu.make_async_copy(buffer.at[part, :], gathered.at[part, :], out_sem.at[device])

    def work(device):
        part = pl.ds(pl.multiple_of(device * rows, rows), rows)
        keep(device).start()

        @pl.loop(0, columns.shape[0] // UNITS)
        def _(step):
            own = pl.ds(pl.multiple_of(step * UNITS, UNITS), UNITS)
            gate = dot(gate_weight[own, :], buffer[part, :], ROWS) + columns[own, 0:1]
            up = dot(up_weight[own, :], buffer[part, :], ROWS) + columns[own, 1:2]
            up = up * columns[own, 2:3]
            normal = 0.5 * (1.0 + lax.erf(gate * (0.5**0.5)))
            density = jnp.exp(-0.5 * gate * gate) * (0.5 / jnp.pi) ** 0.5
            gelu = gate * normal
            hidden[own, part] = (gelu * up).astype(BF16)
            gate_factor[own, part] = (up * (normal + gate * density)).astype(BF16)
            up_factor[own, part] = (gelu * columns[own, 2:3]).astype(BF16)

    work(ring.me)
    ring.from_mate(0)
    work(ring.mate)
    for hop in range(1, ring.chips):
        ring.advance(hop)
        work(ring.origin(hop))
        ring.from_mate(hop)
        work(ring.mates_origin(hop))
    ring.finish()
    for device in range(count):
        keep(device).wait()


def attention_to_feed(
    count, mixed, weight, tokens, gains, offsets, output_offset, gate_weight, up_weight, columns
):
    rows, width = tokens.shape
    units = columns.shape[0]
    total = rows * count
    vmem = pl.BlockSpec(memory_space=pltpu.VMEM)
    return pl.pallas_call(
        functools.partial(middle_kernel, count),
        in_specs=[vmem] * 9,
        out_specs=[vmem] * 3 + [pl.BlockSpec(memory_space=pl.ANY), vmem],
        out_shape=[jax.ShapeDtypeStruct((units, total), BF16)] * 3
        + [jax.ShapeDtypeStruct((total, width), BF16), jax.ShapeDtypeStruct((rows, width), F32)],
        scratch_shapes=[pltpu.VMEM((total, width), BF16)]
        + scatter_space(count, rows, width)
        + ring_sems(count)
        + scatter_sems(count)
        + [pltpu.SemaphoreType.DMA((count,))],
        compiler_params=pltpu.CompilerParams(
            collective_id=1, has_side_effects=True, vmem_limit_bytes=58 << 20
        ),
        cost_estimate=pl.CostEstimate(
            flops=4 * total * width * units,
            bytes_accessed=total * width * 8,
            transcendentals=2 * total * units,
        ),
        name="attention_to_feed",
    )(
        mixed, weight, tokens, gains, offsets, output_offset[None], gate_weight, up_weight, columns
    )


class Stage:
    def __init__(self, slots, sem):
        self.slots, self.sem, self.copies, self.waited = slots, sem, [], set()

    def settle(self, index):
        if index not in self.waited:
            self.copies[index].wait()
            self.waited.add(index)

    def emit(self, work, size, target):
        index = len(self.copies)
        if index >= 2:
            self.settle(index - 2)
        slot = self.slots.at[index % 2, pl.ds(0, size), :]

        @pl.loop(0, slot.shape[1] // TILE)
        def _(tile):
            cut = pl.ds(pl.multiple_of(tile * TILE, TILE), TILE)
            slot[:, cut] = work(cut).astype(BF16)

        copy = pltpu.make_async_copy(slot, target, self.sem.at[index])
        copy.start()
        self.copies.append(copy)
        return index

    def finish(self):
        for index in range(len(self.copies)):
            self.settle(index)


def back_kernel(
    count,
    line_count,
    used,
    hidden,
    shrink,
    gate_weight,
    up_weight,
    output_weight,
    mixed,
    middle,
    cotangent,
    gains,
    cotangent_all,
    second_all,
    gate_factor,
    up_factor,
    grad_mixed,
    grad_middle,
    sums,
    unit_sums,
    shrink_part,
    expand_part,
    output_part,
    shrink_whole,
    grads,
    buffer,
    factors,
    staged,
    *rest,
):
    rows, width = middle.shape
    units = hidden.shape[0]
    tokens = buffer.shape[0]
    sems = rest[7:]
    big_sem, factor_sem, stage_sem = sems[19:22]
    residual_scale = (2.0 * LAYERS) ** 0.5
    ring = Ring(count, rows, buffer, sems[:4])
    scatter = Scatter(ring, *rest[:4], sems[4:9])
    stage = Stage(staged, stage_sem)
    parts = piece_rows(0, used)
    pieces = [
        (shrink_part.at[pl.ds(a, n), :], shrink_whole.at[pl.ds(a, n), :]) for a, n in parts
    ]
    line = Line(line_count, pieces, *rest[4:7], sems[9:19])
    barrier = ring.greet()
    line.greet(barrier)
    load = pltpu.make_async_copy(cotangent_all, buffer, big_sem.at[0])
    load.start()

    def factor(block, slot):
        cut = pl.ds(pl.multiple_of(block * BLOCK, BLOCK), BLOCK)
        return [
            pltpu.make_async_copy(from_.at[:, cut], factors.at[slot, c], factor_sem.at[slot, c])
            for c, from_ in enumerate((gate_factor, up_factor))
        ]

    for copy in factor(0, 0):
        copy.start()
    line.met(barrier, 3)
    load.wait()

    def shrink_work(a, n):
        return lambda cut: jnp.dot(
            hidden[a : a + n, :], buffer[:, cut], preferred_element_type=F32
        )

    for k, (a, n) in enumerate(parts):
        stage.emit(shrink_work(a, n), n, pieces[k][0])
        if k > 0:
            stage.settle(k - 1)
            if k == 1:
                line.ready(0)
            if k <= LANDINGS:
                line.begin(k - 1)
    stage.settle(len(parts) - 1)

    @pl.loop(0, tokens // BLOCK)
    def _(block):
        slot = block % 2
        for copy in factor(block, slot):
            copy.wait()

        @pl.when(block + 1 < tokens // BLOCK)
        def _():
            for copy in factor(block + 1, 1 - slot):
                copy.start()

        cut = pl.ds(pl.multiple_of(block * BLOCK, BLOCK), BLOCK)

        @pl.loop(0, units // UNITS)
        def _(step):
            own = pl.ds(pl.multiple_of(step * UNITS, UNITS), UNITS)
            grad_hidden = dot(shrink[own, :], buffer[cut, :], ROWS)
            grads[0, own, cut] = (grad_hidden * factors[slot, 0, own, :].astype(F32)).astype(BF16)
            grads[1, own, cut] = (grad_hidden * factors[slot, 1, own, :].astype(F32)).astype(BF16)

    load = pltpu.make_async_copy(second_all, buffer, big_sem.at[1])
    load.start()
    acts = []
    for t in range(len(pieces) + 1):
        if t < len(pieces):
            acts.append(functools.partial(line.join, t))
            if t + 1 < len(pieces):
                acts.append(functools.partial(line.ready, t + 1))
        if t > 0:
            acts.append(functools.partial(line.close, t - 1))
        if t + LANDINGS < len(pieces):
            acts.append(functools.partial(line.begin, t + LANDINGS))
    expands = []
    for c in range(2):
        for a, n in parts:
            expands.append((c, a, n))

    def expand_work(c, a, n):
        return lambda cut: jnp.dot(
            grads[c, a : a + n, :], buffer[:, cut], preferred_element_type=F32
        )

    def emit_expands(many):
        for _ in range(min(many, len(expands))):
            c, a, n = expands.pop(0)
            stage.emit(expand_work(c, a, n), n, expand_part.at[pl.ds(c * units + a, n), :])

    def serve(many):
        for _ in range(min(many, len(acts))):
            acts.pop(0)()

    def make(device, target):
        part = pl.ds(pl.multiple_of(device * rows, rows), rows)

        @pl.loop(0, width // TILE)
        def _(tile):
            cut = pl.ds(pl.multiple_of(tile * TILE, TILE), TILE)
            target[:, cut] = (
                dot(grads[0, :, part], gate_weight[:, cut], COLS)
                + dot(grads[1, :, part], up_weight[:, cut], COLS)
            ).astype(target.dtype)

    def beside(far):
        serve(3)
        if far == ring.chips - 1:
            load.wait()
        emit_expands(-(-2 * len(parts) // (ring.chips - 1)))

    scatter.run(make, beside)
    emit_expands(len(expands))
    grad_output = cotangent[...].astype(F32)
    hat, scale = normalize(middle[...])
    grad_in, gain, offset = normalize_back(
        residual_scale * grad_output + scatter.total[...], gains[1:2, :], hat, scale
    )
    grad_middle[...] = grad_in
    scatter.release()
    own = pl.ds(pl.multiple_of(ring.me * rows, rows), rows)
    buffer[own, :] = grad_in.astype(BF16)
    ring.begin()
    sums[0:1, :] = gain[None]
    sums[1:2, :] = offset[None]
    sums[2:3, :] = jnp.sum(grad_middle[...].astype(BF16).astype(F32), axis=0, keepdims=True)
    sums[3:4, :] = jnp.sum(cotangent[...].astype(F32), axis=0, keepdims=True)
    sums[4:8, :] = jnp.zeros((4, width), F32)

    def work(device):
        part = pl.ds(pl.multiple_of(device * rows, rows), rows)
        grad_mixed[part, :] = dot(buffer[part, :], output_weight[...], ROWS).astype(BF16)

    work(ring.me)
    ring.from_mate(0)
    work(ring.mate)
    for c in range(2):
        unit_sums[c] = jnp.dot(
            grads[c], jnp.ones((tokens, 128), BF16), preferred_element_type=F32
        )
    serve(3)
    for hop in range(1, ring.chips):
        ring.advance(hop)
        work(ring.origin(hop))
        ring.from_mate(hop)
        work(ring.mates_origin(hop))
        serve(3)
    for a, n in piece_rows(0, mixed.shape[1]):
        stage.emit(
            lambda cut: dot(mixed[:, a : a + n], buffer[:, cut], COLS),
            n,
            output_part.at[pl.ds(a, n), :],
        )
    ring.finish()
    serve(len(acts))
    for k in range(len(pieces)):
        line.spread(k)
    line.finish()
    stage.finish()


def back(
    count,
    line_count,
    used,
    hidden,
    shrink,
    gate_weight,
    up_weight,
    output_weight,
    mixed,
    middle,
    cotangent,
    gains,
    cotangent_all,
    second_all,
    gate_factor,
    up_factor,
):
    rows, width = middle.shape
    units, total = hidden.shape
    heads = mixed.shape[1]
    vmem, any_ = pl.BlockSpec(memory_space=pltpu.VMEM), pl.BlockSpec(memory_space=pl.ANY)
    pieces = len(piece_rows(0, used))
    return pl.pallas_call(
        functools.partial(back_kernel, count, line_count, used),
        in_specs=[vmem] * 9 + [any_] * 4,
        out_specs=[vmem] * 4 + [any_] * 4,
        out_shape=[
            jax.ShapeDtypeStruct((total, heads), BF16),
            jax.ShapeDtypeStruct((rows, width), F32),
            jax.ShapeDtypeStruct((8, width), F32),
            jax.ShapeDtypeStruct((2, units, 128), F32),
            jax.ShapeDtypeStruct((used, width), BF16),
            jax.ShapeDtypeStruct((2 * units, width), BF16),
            jax.ShapeDtypeStruct((heads, width), BF16),
            jax.ShapeDtypeStruct((used, width), BF16),
        ],
        scratch_shapes=[
            pltpu.VMEM((2, units, total), BF16),
            pltpu.VMEM((total, width), BF16),
            pltpu.VMEM((2, 2, units, BLOCK), BF16),
            pltpu.VMEM((2, PIECE, width), BF16),
        ]
        + scatter_space(count, rows, width)
        + line_space(width)
        + ring_sems(count)
        + scatter_sems(count)
        + line_sems(pieces)
        + [
            pltpu.SemaphoreType.DMA((2,)),
            pltpu.SemaphoreType.DMA((2, 2)),
            pltpu.SemaphoreType.DMA((3 * pieces + heads // PIECE,)),
        ],
        compiler_params=pltpu.CompilerParams(
            collective_id=2, has_side_effects=True, vmem_limit_bytes=60 << 20
        ),
        cost_estimate=pl.CostEstimate(
            flops=18 * total * width * units, bytes_accessed=total * width * 8, transcendentals=0
        ),
        name="back",
    )(
        hidden,
        shrink,
        gate_weight,
        up_weight,
        output_weight,
        mixed,
        middle,
        cotangent,
        gains,
        cotangent_all,
        second_all,
        gate_factor,
        up_factor,
    )


def tail_kernel(
    count,
    line_count,
    used,
    grad_projected,
    input_weight,
    hidden,
    shrink,
    middle,
    tokens,
    grad_middle,
    gains,
    offsets,
    shrink_offset,
    first_all,
    expand_part,
    output_part,
    layer_out,
    tokens_grad,
    sums,
    input_sums,
    input_part,
    expand_whole,
    output_whole,
    input_whole,
    first,
    staged,
    *rest,
):
    rows, width = middle.shape
    units = hidden.shape[0]
    sems = rest[7:]
    big_sem, stage_sem = sems[15:17]
    residual_scale = (2.0 * LAYERS) ** 0.5
    ring = Ring(count, rows, None, [None] * 4)
    scatter = Scatter(ring, *rest[:4], sems[:5])
    stage = Stage(staged, stage_sem)
    pieces = [
        (expand_part.at[pl.ds(c * units + a, n), :], expand_whole.at[pl.ds(c * units + a, n), :])
        for c in range(2)
        for a, n in piece_rows(0, used)
    ] + [
        (output_part.at[pl.ds(a, n), :], output_whole.at[pl.ds(a, n), :])
        for a, n in piece_rows(0, output_part.shape[0])
    ]
    early = len(pieces)
    lasts = piece_rows(0, grad_projected.shape[1])
    pieces += [(input_part.at[pl.ds(a, n), :], input_whole.at[pl.ds(a, n), :]) for a, n in lasts]
    line = Line(line_count, pieces, *rest[4:7], sems[5:15])
    barrier = ring.greet()
    line.greet(barrier)
    load = pltpu.make_async_copy(first_all, first, big_sem.at[0])
    load.start()
    line.ready(0)
    line.met(barrier, 3)
    for k in range(LANDINGS):
        line.begin(k)
    turns = iter(range(len(pieces) + 1))

    def turn():
        t = next(turns, None)
        if t is None:
            return
        if t < len(pieces):
            line.join(t)
            if t + 1 < len(pieces):
                line.ready(t + 1)
        if t > 0:
            line.close(t - 1)
        if t + LANDINGS < len(pieces):
            line.begin(t + LANDINGS)

    def make(device, target):
        part = pl.ds(pl.multiple_of(device * rows, rows), rows)

        @pl.loop(0, width // TILE)
        def _(tile):
            cut = pl.ds(pl.multiple_of(tile * TILE, TILE), TILE)
            target[:, cut] = dot(grad_projected[part, :], input_weight[cut, :], ROWS).astype(
                target.dtype
            )

    scatter.run(make, lambda far: turn())
    hat, scale = normalize(tokens[...].astype(F32))
    grad_in, gain, offset = normalize_back(
        residual_scale * grad_middle[...] + scatter.total[...], gains[0:1, :], hat, scale
    )
    tokens_grad[...] = grad_in
    sums[0:1, :] = gain[None]
    sums[1:2, :] = offset[None]
    sums[2:8, :] = jnp.zeros((6, width), F32)
    scatter.release()
    load.wait()

    def input_work(a, n):
        return lambda cut: dot(grad_projected[:, a : a + n], first[:, cut], COLS)

    turn()
    for a, n in lasts:
        stage.emit(input_work(a, n), n, input_part.at[pl.ds(a, n), :])
    input_sums[...] = jnp.dot(
        jnp.ones((16, grad_projected.shape[0]), BF16),
        grad_projected[...],
        preferred_element_type=F32,
    )
    stage.finish()
    turn()

    def make_out(device, target):
        part = pl.ds(pl.multiple_of(device * rows, rows), rows)

        @pl.loop(0, width // TILE)
        def _(tile):
            cut = pl.ds(pl.multiple_of(tile * TILE, TILE), TILE)
            target[:, cut] = dot(hidden[:, part], shrink[:, cut], COLS).astype(target.dtype)

    scatter.run(make_out, lambda far: turn())
    hat, _ = normalize(middle[...])
    layer_out[...] = (
        residual_scale * (hat * gains[1:2, :] + offsets[1:2, :])
        + scatter.total[...]
        + shrink_offset[...]
    )
    for _ in range(len(pieces) + 1):
        turn()
    for k in range(len(pieces)):
        line.spread(k)
    line.finish()


def tail(
    count,
    line_count,
    used,
    grad_projected,
    input_weight,
    hidden,
    shrink,
    middle,
    tokens,
    grad_middle,
    gains,
    offsets,
    shrink_offset,
    first_all,
    expand_part,
    output_part,
):
    rows, width = middle.shape
    units, total = hidden.shape
    columns = grad_projected.shape[1]
    heads = output_part.shape[0]
    vmem, any_ = pl.BlockSpec(memory_space=pltpu.VMEM), pl.BlockSpec(memory_space=pl.ANY)
    lasts = len(piece_rows(0, columns))
    pieces = 2 * len(piece_rows(0, used)) + len(piece_rows(0, heads)) + lasts
    return pl.pallas_call(
        functools.partial(tail_kernel, count, line_count, used),
        in_specs=[vmem] * 10 + [any_] * 3,
        out_specs=[vmem] * 4 + [any_] * 4,
        out_shape=[
            jax.ShapeDtypeStruct((rows, width), F32),
            jax.ShapeDtypeStruct((rows, width), F32),
            jax.ShapeDtypeStruct((8, width), F32),
            jax.ShapeDtypeStruct((16, columns), F32),
            jax.ShapeDtypeStruct((columns, width), BF16),
            jax.ShapeDtypeStruct((2 * units, width), BF16),
            jax.ShapeDtypeStruct((heads, width), BF16),
            jax.ShapeDtypeStruct((columns, width), BF16),
        ],
        scratch_shapes=[pltpu.VMEM((total, width), BF16), pltpu.VMEM((2, PIECE, width), BF16)]
        + scatter_space(count, rows, width)
        + line_space(width)
        + scatter_sems(count)
        + line_sems(pieces)
        + [pltpu.SemaphoreType.DMA((1,)), pltpu.SemaphoreType.DMA((lasts,))],
        compiler_params=pltpu.CompilerParams(
            collective_id=3, has_side_effects=True, vmem_limit_bytes=60 << 20
        ),
        cost_estimate=pl.CostEstimate(
            flops=4 * total * width * (columns + units),
            bytes_accessed=total * width * 8,
            transcendentals=0,
        ),
        name="tail",
    )(
        grad_projected,
        input_weight,
        hidden,
        shrink,
        middle,
        tokens,
        grad_middle,
        gains,
        offsets,
        shrink_offset[None],
        first_all,
        expand_part,
        output_part,
    )


def weave_kernel(gate, up, out):
    rows = out.shape[0]
    out[:, 0, :] = gate[:rows, :].astype(F32)
    out[:, 1, :] = up[:rows, :].astype(F32)


def weave(both, rows):
    units, width = both.shape[0] // 2, both.shape[1]
    tile = 256
    return pl.pallas_call(
        weave_kernel,
        grid=(width // tile,),
        in_specs=[
            pl.BlockSpec((units, tile), lambda j: (0, j)),
            pl.BlockSpec((units, tile), lambda j: (1, j)),
        ],
        out_specs=pl.BlockSpec((rows, 2, tile), lambda j: (0, 0, j)),
        out_shape=jax.ShapeDtypeStruct((rows, 2, width), F32),
        compiler_params=pltpu.CompilerParams(vmem_limit_bytes=40 << 20),
        cost_estimate=pl.CostEstimate(flops=0, bytes_accessed=12 * rows * width, transcendentals=0),
        name="weave",
    )(both, both)


def local(
    dp,
    tp,
    tokens,
    segment_ids,
    prefix_lengths,
    positions,
    norm_gains,
    norm_offsets,
    input_weight,
    input_offset,
    output_weight,
    output_offset,
    expand_weight,
    expand_offset,
    shrink_weight,
    shrink_offset,
    cotangent,
):
    seq_count = segment_ids.shape[0]
    units_used = expand_weight.shape[2]
    units = -(-units_used // UNITS) * UNITS
    used = -(-units_used // 16) * 16

    pad = ((0, units - units_used), (0, 0))
    turned_expand = jnp.transpose(expand_weight, (2, 1, 0))
    gate_weight, up_weight = jnp.pad(turned_expand[:, 0], pad), jnp.pad(turned_expand[:, 1], pad)
    shrink = jnp.pad(shrink_weight, pad)
    unit_index = lax.axis_index("tp") * units_used + lax.iota(jnp.int32, units_used)
    keep_units = (unit_index < FF_USED).astype(F32)
    columns = jnp.pad(jnp.stack([expand_offset[0], expand_offset[1], keep_units], axis=1), pad)

    row_at = lax.broadcasted_iota(jnp.int32, positions.shape, 1)
    low = row_at - positions
    matches = segment_ids[:, :, None] == lax.iota(jnp.int32, prefix_lengths.shape[1])
    own_prefix = jnp.sum(jnp.where(matches, prefix_lengths[:, None, :], 0), axis=2)
    high = jnp.maximum(row_at, low + own_prefix - 1)
    bounds = jnp.stack(
        [
            jnp.min(low.reshape(seq_count, -1, BLOCK), axis=2) // BLOCK,
            jnp.max(high.reshape(seq_count, -1, BLOCK), axis=2) // BLOCK + 1,
        ],
        axis=2,
    )
    cosine, sine = rotary_tables(positions)

    projected, first_all = project(
        tp, tokens, norm_gains[:1], norm_offsets[:1], input_weight, input_offset
    )
    waiting, first_all = lax.optimization_barrier((cotangent, first_all))
    cotangent_all = lax.all_gather(waiting, "tp", axis=0, tiled=True)
    packed, mixed, peaks = attend_forward(projected, cosine, sine, low, high, bounds)
    hidden, gate_factor, up_factor, second_all, middle = attention_to_feed(
        tp,
        mixed,
        output_weight,
        tokens,
        norm_gains,
        norm_offsets,
        output_offset,
        gate_weight,
        up_weight,
        columns,
    )

    grad_mixed, grad_middle, sums, unit_sums, _, expand_part, output_part, shrink_whole = back(
        tp,
        dp,
        used,
        hidden,
        shrink,
        gate_weight,
        up_weight,
        output_weight,
        mixed,
        middle,
        cotangent,
        norm_gains,
        cotangent_all,
        second_all,
        gate_factor,
        up_factor,
    )
    grad_projected = attend_backward(
        packed, mixed, grad_mixed, peaks, cosine, sine, low, high, bounds
    )
    layer_out, tokens_grad, late_sums, input_sums, _, expand_whole, output_whole, input_whole = tail(
        tp,
        dp,
        used,
        grad_projected,
        input_weight,
        hidden,
        shrink,
        middle,
        tokens,
        grad_middle,
        norm_gains,
        norm_offsets,
        shrink_offset,
        first_all,
        expand_part,
        output_part,
    )

    whole_sums = swap_sum(jnp.concatenate([late_sums[:2], sums[:4]]), tp, "tp")
    whole_sums = swap_sum(whole_sums, dp, "dp")
    group_sums = swap_sum(
        jnp.concatenate([unit_sums[:, :units_used, 0].reshape(-1), input_sums[0]]), dp, "dp"
    )
    return (
        layer_out,
        tokens_grad,
        input_whole.astype(F32).T,
        group_sums[2 * units_used :],
        output_whole.astype(F32),
        whole_sums[4],
        jnp.transpose(weave(expand_whole, units_used), (2, 1, 0)),
        group_sums[: 2 * units_used].reshape(2, units_used),
        shrink_whole[:units_used].astype(F32),
        whole_sums[5],
        jnp.stack([whole_sums[0], whole_sums[2]]),
        jnp.stack([whole_sums[1], whole_sums[3]]),
    )


def solution(mesh):
    in_specs = (
        P(("dp", "tp"), None),
        P("dp", None),
        P("dp", None),
        P("dp", None),
        P(),
        P(),
        P(None, "tp"),
        P("tp"),
        P("tp", None),
        P(),
        P(None, None, "tp"),
        P(None, "tp"),
        P("tp", None),
        P(),
        P(("dp", "tp"), None),
    )
    out_specs = (
        P(("dp", "tp"), None),
        P(("dp", "tp"), None),
        P(None, "tp"),
        P("tp"),
        P("tp", None),
        P(),
        P(None, None, "tp"),
        P(None, "tp"),
        P("tp", None),
        P(),
        P(),
        P(),
    )
    return jax.shard_map(
        functools.partial(local, mesh.shape["dp"], mesh.shape["tp"]),
        mesh=mesh,
        in_specs=in_specs,
        out_specs=out_specs,
        check_vma=False,
    )
```

```python
import functools

import jax
import jax.numpy as jnp
from jax import lax
from jax.experimental import pallas as pl
from jax.experimental.pallas import tpu as pltpu
from jax.sharding import PartitionSpec as P

HEAD_DIM = 128
FF_USED = 5461
LAYERS = 24
SEQ_LEN = 1024
BLOCK = 256
TILE = 512
UNITS = 176

epsilon = 1e-05
rope_base = 10000.0
masked_score = -1e30
F32 = jnp.float32
BF16 = jnp.bfloat16
ROWS = (((1,), (1,)), ((), ()))
MESH = pl.DeviceIdType.MESH
COLS = (((0,), (0,)), ((), ()))


def dot(left, right, dims):
    return lax.dot_general(left, right, dims, preferred_element_type=F32)


def normalize(values):
    average = jnp.mean(values, axis=-1, keepdims=True)
    centred = values - average
    variance = jnp.mean(centred * centred, axis=-1, keepdims=True)
    scale = lax.rsqrt(variance + epsilon)
    return centred * scale, scale


def normalize_back(grad, gains, hat, scale):
    pulled = grad * gains
    grad_in = scale * (
        pulled
        - jnp.mean(pulled, axis=-1, keepdims=True)
        - hat * jnp.mean(pulled * hat, axis=-1, keepdims=True)
    )
    return grad_in, jnp.sum(grad * hat, axis=0), jnp.sum(grad, axis=0)


def rotary_tables(places):
    half_dim = HEAD_DIM // 2
    exponents = lax.iota(F32, half_dim) * (-2.0 / HEAD_DIM)
    rates = jnp.power(rope_base, exponents)
    angles = places.astype(F32)[..., None] * rates
    cosine, sine = jnp.cos(angles), jnp.sin(angles)
    return jnp.concatenate([cosine, cosine], -1), jnp.concatenate([-sine, sine], -1)


def turned(values, cosine, sine):
    return values * cosine + pltpu.roll(values, HEAD_DIM // 2, 1) * sine


def attend_forward_kernel(bounds, projected, cosine, sine, low, high, packed, mixed, peaks, values_t):
    seq = pl.program_id(0)
    score_scale = HEAD_DIM ** (-0.5)
    packed[:, :HEAD_DIM] = turned(projected[:, :HEAD_DIM], cosine[...], sine[...]).astype(BF16)
    packed[:, HEAD_DIM : 2 * HEAD_DIM] = turned(
        projected[:, HEAD_DIM : 2 * HEAD_DIM], cosine[...], sine[...]
    ).astype(BF16)
    packed[:, 2 * HEAD_DIM :] = projected[:, 2 * HEAD_DIM :].astype(BF16)
    for b in range(SEQ_LEN // BLOCK):
        values_t[b] = projected[b * BLOCK : (b + 1) * BLOCK, 2 * HEAD_DIM :].T.astype(BF16)

    def queries_block(b, _):
        start = pl.multiple_of(b * BLOCK, BLOCK)
        queries = packed[pl.ds(start, BLOCK), :HEAD_DIM]
        first = low[0, 0, pl.ds(start, BLOCK)][None, :]
        last = high[0, 0, pl.ds(start, BLOCK)][None, :]

        def keys_block(j, carry):
            peak, total, gathered = carry
            keys = packed[pl.ds(pl.multiple_of(j * BLOCK, BLOCK), BLOCK), HEAD_DIM : 2 * HEAD_DIM]
            scores = dot(keys, queries, ROWS) * score_scale
            place = lax.broadcasted_iota(jnp.int32, (BLOCK, BLOCK), 0) + j * BLOCK
            scores = jnp.where((place >= first) & (place <= last), scores, masked_score)
            new_peak = jnp.maximum(peak, jnp.max(scores, axis=0, keepdims=True))
            shifted = jnp.exp(scores - new_peak)
            fade = jnp.exp(peak - new_peak)
            total = total * fade + jnp.sum(shifted, axis=0, keepdims=True)
            gathered = gathered * fade + jnp.dot(
                values_t[j], shifted.astype(BF16), preferred_element_type=F32
            )
            return new_peak, total, gathered

        peak, total, gathered = lax.fori_loop(
            bounds[seq, b, 0],
            bounds[seq, b, 1],
            keys_block,
            (
                jnp.full((1, BLOCK), masked_score, F32),
                jnp.zeros((1, BLOCK), F32),
                jnp.zeros((HEAD_DIM, BLOCK), F32),
            ),
        )
        mixed[pl.ds(start, BLOCK), :] = (gathered / total).T.astype(BF16)
        peaks[0, 0, 0, pl.ds(start, BLOCK)] = (peak + jnp.log(total))[0]
        return 0

    lax.fori_loop(0, SEQ_LEN // BLOCK, queries_block, 0)


def attend_forward(projected, cosine, sine, low, high, bounds):
    seq_count, heads = cosine.shape[0], projected.shape[1] // (3 * HEAD_DIM)
    rows = seq_count * SEQ_LEN
    per_head = pl.BlockSpec((SEQ_LEN, 3 * HEAD_DIM), lambda s, h, *_: (s, h))
    table = pl.BlockSpec((None, SEQ_LEN, HEAD_DIM), lambda s, h, *_: (s, 0, 0))
    line = pl.BlockSpec((1, 1, SEQ_LEN), lambda s, h, *_: (s, 0, 0))
    return pl.pallas_call(
        attend_forward_kernel,
        grid_spec=pltpu.PrefetchScalarGridSpec(
            num_scalar_prefetch=1,
            grid=(seq_count, heads),
            in_specs=[per_head, table, table, line, line],
            out_specs=[
                per_head,
                pl.BlockSpec((SEQ_LEN, HEAD_DIM), lambda s, h, *_: (s, h)),
                pl.BlockSpec((1, 1, 1, SEQ_LEN), lambda s, h, *_: (s, h, 0, 0)),
            ],
            scratch_shapes=[pltpu.VMEM((SEQ_LEN // BLOCK, HEAD_DIM, BLOCK), BF16)],
        ),
        out_shape=[
            jax.ShapeDtypeStruct(projected.shape, BF16),
            jax.ShapeDtypeStruct((rows, heads * HEAD_DIM), BF16),
            jax.ShapeDtypeStruct((seq_count, heads, 1, SEQ_LEN), F32),
        ],
        compiler_params=pltpu.CompilerParams(vmem_limit_bytes=40 << 20),
        cost_estimate=pl.CostEstimate(
            flops=4 * rows * SEQ_LEN * HEAD_DIM * heads,
            bytes_accessed=rows * heads * HEAD_DIM * 20,
            transcendentals=rows * SEQ_LEN * heads,
        ),
        name="attend_forward",
    )(bounds, projected, cosine, sine, low[:, None], high[:, None])


def attend_back(
    packed, mixed, grad_mixed, peaks, cosine, sine, low, high, grad, keys_t, inner, grad_keys, grad_values
):
    score_scale = HEAD_DIM ** (-0.5)
    for b in range(SEQ_LEN // BLOCK):
        part = slice(b * BLOCK, (b + 1) * BLOCK)
        keys_t[b] = packed[part, HEAD_DIM : 2 * HEAD_DIM].astype(F32).T.astype(BF16)
        both = grad_mixed[part, :].astype(F32) * mixed[part, :].astype(F32)
        inner[b] = jnp.sum(both.T, axis=0, keepdims=True)
    grad_keys[...] = jnp.zeros_like(grad_keys)
    grad_values[...] = jnp.zeros_like(grad_values)

    @pl.loop(0, SEQ_LEN // BLOCK)
    def _(b):
        rows = pl.ds(pl.multiple_of(b * BLOCK, BLOCK), BLOCK)
        queries = packed[rows, :HEAD_DIM]
        pulled = grad_mixed[rows, :]
        first, last = low[:, rows], high[:, rows]
        peak = peaks[:, rows]
        inner_sum = inner[b]

        def keys_block(j, total):
            part = pl.ds(pl.multiple_of(j * BLOCK, BLOCK), BLOCK)
            keys = packed[part, HEAD_DIM : 2 * HEAD_DIM]
            values = packed[part, 2 * HEAD_DIM :]
            scores = dot(keys, queries, ROWS) * score_scale
            place = lax.broadcasted_iota(jnp.int32, (BLOCK, BLOCK), 0) + j * BLOCK
            scores = jnp.where((place >= first) & (place <= last), scores, masked_score)
            probs = jnp.exp(scores - peak)
            grad_probs = dot(values, pulled, ROWS)
            grad_scores = (probs * (grad_probs - inner_sum)).astype(BF16)
            grad_values[part, :] += jnp.dot(probs.astype(BF16), pulled, preferred_element_type=F32)
            grad_keys[part, :] += jnp.dot(grad_scores, queries, preferred_element_type=F32)
            return total + jnp.dot(keys_t[j], grad_scores, preferred_element_type=F32)

        total = lax.fori_loop(
            0, SEQ_LEN // BLOCK, keys_block, jnp.zeros((HEAD_DIM, BLOCK), F32)
        )
        grad_queries = total.T * score_scale
        grad[rows, :HEAD_DIM] = turned(grad_queries, cosine[rows, :], -sine[rows, :]).astype(BF16)

    grad[:, HEAD_DIM : 2 * HEAD_DIM] = turned(
        grad_keys[...] * score_scale, cosine[...], -sine[...]
    ).astype(BF16)
    grad[:, 2 * HEAD_DIM :] = grad_values[...].astype(BF16)


class Ring:
    def __init__(self, count, rows, buffer, sems):
        self.chips, self.rows, self.buffer = count // 2, rows, buffer
        self.ring_send, self.ring_recv, self.core_send, self.core_recv = sems
        me = lax.axis_index("tp")
        self.core, self.chip = me % 2, me // 2
        self.spot = self.place(self.chip)
        self.way = 1 - 2 * self.core
        self.next = self.place((self.spot + self.way + self.chips) % self.chips) * 2 + self.core
        self.last = self.place((self.spot - self.way + self.chips) % self.chips) * 2 + self.core
        self.me, self.mate = me, me + self.way

    def place(self, spot):
        turn = self.chips // 2
        return spot + (spot // turn) * (self.chips - 1 + turn - 2 * spot)

    def origin(self, hop):
        return self.place((self.spot - hop * self.way + hop * self.chips) % self.chips) * 2 + self.core

    def mates_origin(self, hop):
        spot = (self.spot + hop * self.way + hop * self.chips) % self.chips
        return self.place(spot) * 2 + 1 - self.core

    def part(self, device, half):
        size = self.rows // 2
        return pl.ds(pl.multiple_of(device * self.rows + half * size, size), size)

    def copy(self, device, half, send, recv, to):
        part = self.buffer.at[self.part(device, half), :]
        return pltpu.make_async_remote_copy(
            src_ref=part,
            dst_ref=part,
            send_sem=send,
            recv_sem=recv,
            device_id={"tp": to},
            device_id_type=MESH,
        )

    def greet(self):
        barrier = pltpu.get_barrier_semaphore()
        for other in (self.next, self.last, self.mate):
            pl.semaphore_signal(
                barrier, inc=1, device_id={"tp": other}, device_id_type=MESH
            )
        return barrier

    def along(self, hop, half, device):
        return self.copy(device, half, self.ring_send.at[hop, half], self.ring_recv.at[hop, half], self.next)

    def across(self, hop, half, device):
        return self.copy(device, half, self.core_send.at[hop, half], self.core_recv.at[hop, half], self.mate)

    def begin(self):
        for half in range(2):
            self.along(0, half, self.me).start()
            self.across(0, half, self.me).start()

    def advance(self, hop):
        device = self.origin(hop)
        for half in range(2):
            self.along(hop - 1, half, device).wait_recv()
            if hop < self.chips - 1:
                self.along(hop, half, device).start()
            self.across(hop, half, device).start()

    def from_mate(self, hop):
        device = self.mates_origin(hop)
        for half in range(2):
            self.across(hop, half, device).wait_recv()

    def finish(self):
        for half in range(2):
            for hop in range(self.chips):
                if hop < self.chips - 1:
                    self.along(hop, half, self.me).wait_send()
                self.across(hop, half, self.me).wait_send()


def ring_sems(count):
    chips = count // 2
    return [pltpu.SemaphoreType.DMA((chips, 2))] * 4


def project_kernel(count, tokens, gains, offsets, weight, bias, projected, gathered, buffer, *rest):
    sems, out_sem = rest[:4], rest[4]
    rows = tokens.shape[0]
    ring = Ring(count, rows, buffer, sems)
    barrier = ring.greet()
    hat, _ = normalize(tokens[...].astype(F32))
    own = pl.ds(pl.multiple_of(ring.me * rows, rows), rows)
    buffer[own, :] = (hat * gains[...] + offsets[...]).astype(BF16)
    pl.semaphore_wait(barrier, 3)
    ring.begin()

    def keep(device):
        part = pl.ds(pl.multiple_of(device * rows, rows), rows)
        return pltpu.make_async_copy(buffer.at[part, :], gathered.at[part, :], out_sem.at[device])

    def work(device):
        part = pl.ds(pl.multiple_of(device * rows, rows), rows)
        keep(device).start()
        projected[part, :] = (
            jnp.dot(buffer[part, :], weight[...], preferred_element_type=F32) + bias[...]
        )

    work(ring.me)
    ring.from_mate(0)
    work(ring.mate)
    for hop in range(1, ring.chips):
        ring.advance(hop)
        work(ring.origin(hop))
        ring.from_mate(hop)
        work(ring.mates_origin(hop))
    ring.finish()
    for device in range(count):
        keep(device).wait()


def project(count, tokens, gains, offsets, weight, bias):
    rows, width = tokens.shape
    columns = weight.shape[1]
    total = rows * count
    vmem = pl.BlockSpec(memory_space=pltpu.VMEM)
    return pl.pallas_call(
        functools.partial(project_kernel, count),
        in_specs=[vmem] * 5,
        out_specs=[vmem, pl.BlockSpec(memory_space=pl.ANY)],
        out_shape=[
            jax.ShapeDtypeStruct((total, columns), F32),
            jax.ShapeDtypeStruct((total, width), BF16),
        ],
        scratch_shapes=[pltpu.VMEM((total, width), BF16)]
        + ring_sems(count)
        + [pltpu.SemaphoreType.DMA((count,))],
        compiler_params=pltpu.CompilerParams(
            collective_id=0, has_side_effects=True, vmem_limit_bytes=48 << 20
        ),
        cost_estimate=pl.CostEstimate(
            flops=2 * total * width * columns, bytes_accessed=total * width * 8, transcendentals=0
        ),
        name="project",
    )(tokens, gains, offsets, weight, bias[None])


class Scatter:
    def __init__(self, ring, give, take, passing, total, sems):
        self.ring, self.give, self.take, self.passing, self.total = ring, give, take, passing, total
        self.give_send, self.give_recv, self.pass_send, self.pass_recv, self.again = sems

    def handed(self, far, half):
        size = self.ring.rows // 2
        part = pl.ds(half * size, size)
        return pltpu.make_async_remote_copy(
            src_ref=self.give.at[far % 2, part, :],
            dst_ref=self.take.at[far, part, :],
            send_sem=self.give_send.at[far, half],
            recv_sem=self.give_recv.at[far, half],
            device_id={"tp": self.ring.mate},
            device_id_type=MESH,
        )

    def passed(self, far, half):
        size = self.ring.rows // 2
        part = pl.ds(half * size, size)
        return pltpu.make_async_remote_copy(
            src_ref=self.passing.at[far, part, :],
            dst_ref=self.passing.at[far - 1, part, :],
            send_sem=self.pass_send.at[far, half],
            recv_sem=self.pass_recv.at[far - 1, half],
            device_id={"tp": self.ring.next},
            device_id_type=MESH,
        )

    def run(self, make, beside=lambda far: None):
        ring = self.ring
        chips, size = ring.chips, ring.rows // 2
        for far in reversed(range(chips)):
            if far < chips - 2:
                for half in range(2):
                    self.handed(far + 2, half).wait_send()
            make(ring.origin(far) + ring.way, self.give.at[far % 2])
            for half in range(2):
                self.handed(far, half).start()
            make(ring.origin(chips - far), self.total)
            beside(far)
            for half in range(2):
                self.handed(far, half).wait_recv()
                if far < chips - 1:
                    self.passed(far + 1, half).wait_recv()

                @pl.loop(0, size // 16)
                def _(row):
                    part = pl.ds(pl.multiple_of(half * size + row * 16, 16), 16)
                    value = self.total[part, :] + self.take[far, part, :].astype(F32)
                    if far < chips - 1:
                        value = value + self.passing[far, part, :].astype(F32)
                    if far > 0:
                        self.passing[far, part, :] = value.astype(BF16)
                    else:
                        self.total[part, :] = value

                if far > 0:
                    self.passed(far, half).start()
        for half in range(2):
            for far in range(chips):
                if far < 2:
                    self.handed(far, half).wait_send()
                if far > 0:
                    self.passed(far, half).wait_send()

    def release(self):
        for other in (self.ring.last, self.ring.mate):
            pl.semaphore_signal(self.again, inc=1, device_id={"tp": other}, device_id_type=MESH)
        pl.semaphore_wait(self.again, 2)


def scatter_space(count, rows, width):
    chips = count // 2
    return [
        pltpu.VMEM((2, rows, width), BF16),
        pltpu.VMEM((chips, rows, width), BF16),
        pltpu.VMEM((chips, rows, width), BF16),
        pltpu.VMEM((rows, width), F32),
    ]


def scatter_sems(count):
    return [pltpu.SemaphoreType.DMA((count // 2, 2))] * 4 + [pltpu.SemaphoreType.REGULAR]


SLOTS = 4
LANDINGS = 3
PIECE = 128
EARLY = 2


class Line:
    def __init__(self, count, pieces, held, came, crossed, sems):
        self.pieces, self.held, self.came, self.crossed = pieces, held, came, crossed
        (
            self.load_sem,
            self.keep_sem,
            self.in_send,
            self.in_recv,
            self.mid_send,
            self.mid_recv,
            self.out_send,
            self.out_recv,
            self.in_free,
            self.mid_free,
        ) = sems
        here = lax.axis_index("dp")
        half = count // 2
        side = here // half
        self.count, self.half = count, half
        self.inner, self.outer = here + 1 - 2 * side, here - 1 + 2 * side
        self.depth = here + side * (count - 1 - 2 * here)
        self.end, self.middle = self.depth == 0, self.depth == half - 1

    def greet(self, barrier):
        pl.semaphore_signal(barrier, inc=1, device_id={"dp": self.inner}, device_id_type=MESH)

        @pl.when(self.depth > 0)
        def _():
            pl.semaphore_signal(barrier, inc=1, device_id={"dp": self.outer}, device_id_type=MESH)

    def met(self, barrier, others):
        @pl.when(self.depth == 0)
        def _():
            pl.semaphore_wait(barrier, others + 1)

        @pl.when(self.depth > 0)
        def _():
            pl.semaphore_wait(barrier, others + 2)

    def rows(self, k):
        return self.pieces[k][0].shape[0]

    def sent(self, source, target, send, recv, to):
        return pltpu.make_async_remote_copy(
            src_ref=source,
            dst_ref=target,
            send_sem=send,
            recv_sem=recv,
            device_id={"dp": to},
            device_id_type=MESH,
        )

    def inward(self, k, source):
        landing = self.came.at[k % LANDINGS, pl.ds(0, self.rows(k)), :]
        return self.sent(source, landing, self.in_send.at[k], self.in_recv.at[k], self.inner)

    def across(self, k):
        part = pl.ds(0, self.rows(k))
        return self.sent(
            self.held.at[k % SLOTS, part, :],
            self.crossed.at[k % LANDINGS, part, :],
            self.mid_send.at[k],
            self.mid_recv.at[k],
            self.inner,
        )

    def outward(self, k, source):
        return self.sent(source, self.pieces[k][1], self.out_send.at[k], self.out_recv.at[k], self.outer)

    def slot(self, k):
        return self.held.at[k % SLOTS, pl.ds(0, self.rows(k)), :]

    def load(self, k):
        return pltpu.make_async_copy(self.pieces[k][0], self.slot(k), self.load_sem.at[k])

    def keep(self, k):
        return pltpu.make_async_copy(self.slot(k), self.pieces[k][1], self.keep_sem.at[k])

    def begin(self, k):
        @pl.when(self.end)
        def _():
            if k >= LANDINGS:
                pl.semaphore_wait(self.in_free, 1)
            self.inward(k, self.pieces[k][0]).start()

    def free(self, k):
        @pl.when(self.middle)
        def _():
            self.outward(k, self.slot(k)).wait_send()
            self.keep(k).wait()

        if self.half > 2:

            @pl.when((self.depth > 0) & (self.depth < self.half - 1))
            def _():
                self.inward(k, self.slot(k)).wait_send()

    def ready(self, k):
        if k >= SLOTS:
            self.free(k - SLOTS)

        @pl.when(self.depth > 0)
        def _():
            self.load(k).start()

    def add(self, k, other):
        slot = self.held.at[k % SLOTS]

        @pl.loop(0, self.rows(k) // 16)
        def _(row):
            part = pl.ds(pl.multiple_of(row * 16, 16), 16)
            slot[part, :] = (
                slot[part, :].astype(F32) + other[k % LANDINGS, part, :].astype(F32)
            ).astype(BF16)

    def join(self, k):
        @pl.when(self.depth > 0)
        def _():
            self.load(k).wait()
            self.inward(k, self.slot(k)).wait_recv()
            self.add(k, self.came)
            if k + LANDINGS < len(self.pieces):
                pl.semaphore_signal(
                    self.in_free, inc=1, device_id={"dp": self.outer}, device_id_type=MESH
                )

        @pl.when(self.middle)
        def _():
            if k >= LANDINGS:
                pl.semaphore_wait(self.mid_free, 1)
            self.across(k).start()

        if self.half > 2:

            @pl.when((self.depth > 0) & (self.depth < self.half - 1))
            def _():
                if k >= LANDINGS:
                    pl.semaphore_wait(self.in_free, 1)
                self.inward(k, self.slot(k)).start()

    def close(self, k):
        @pl.when(self.middle)
        def _():
            self.across(k).wait_recv()
            self.across(k).wait_send()
            self.add(k, self.crossed)
            if k + LANDINGS < len(self.pieces):
                pl.semaphore_signal(
                    self.mid_free, inc=1, device_id={"dp": self.inner}, device_id_type=MESH
                )
            self.outward(k, self.slot(k)).start()
            self.keep(k).start()

    def spread(self, k):
        @pl.when(self.depth < self.half - 1)
        def _():
            self.outward(k, self.pieces[k][1]).wait_recv()

        if self.half > 2:

            @pl.when((self.depth > 0) & (self.depth < self.half - 1))
            def _():
                self.outward(k, self.pieces[k][1]).start()

    def finish(self):
        total = len(self.pieces)
        for k in range(max(0, total - SLOTS), total):
            self.free(k)
        for k in range(total):

            @pl.when(self.end)
            def _():
                self.inward(k, self.pieces[k][0]).wait_send()

            if self.half > 2:

                @pl.when((self.depth > 0) & (self.depth < self.half - 1))
                def _():
                    self.outward(k, self.pieces[k][1]).wait_send()


def line_space(width):
    return [
        pltpu.VMEM((SLOTS, PIECE, width), BF16),
        pltpu.VMEM((LANDINGS, PIECE, width), BF16),
        pltpu.VMEM((LANDINGS, PIECE, width), BF16),
    ]


def line_sems(pieces):
    return [pltpu.SemaphoreType.DMA((pieces,))] * 8 + [pltpu.SemaphoreType.REGULAR] * 2


def piece_rows(start, total):
    return [(start + at, min(PIECE, total - at)) for at in range(0, total, PIECE)]


def middle_kernel(
    count,
    mixed,
    weight,
    tokens,
    gains,
    offsets,
    output_offset,
    gate_weight,
    up_weight,
    columns,
    hidden,
    gate_factor,
    up_factor,
    gathered,
    middle,
    buffer,
    give,
    take,
    passing,
    total,
    *rest,
):
    rows = tokens.shape[0]
    residual_scale = (2.0 * LAYERS) ** 0.5
    ring = Ring(count, rows, buffer, rest[:4])
    scatter = Scatter(ring, give, take, passing, total, rest[4:9])
    out_sem = rest[9]
    pl.semaphore_wait(ring.greet(), 3)

    def make(device, target):
        part = pl.ds(pl.multiple_of(device * rows, rows), rows)

        @pl.loop(0, weight.shape[1] // TILE)
        def _(tile):
            cut = pl.ds(pl.multiple_of(tile * TILE, TILE), TILE)
            target[:, cut] = jnp.dot(
                mixed[part, :], weight[:, cut], preferred_element_type=F32
            ).astype(target.dtype)

    scatter.run(make)
    hat, _ = normalize(tokens[...].astype(F32))
    first = hat * gains[0:1, :] + offsets[0:1, :]
    middle[...] = residual_scale * first + (total[...] + output_offset[...])
    hat, _ = normalize(middle[...])
    own = pl.ds(pl.multiple_of(ring.me * rows, rows), rows)
    buffer[own, :] = (hat * gains[1:2, :] + offsets[1:2, :]).astype(BF16)
    ring.begin()

    def keep(device):
        part = pl.ds(pl.multiple_of(device * rows, rows), rows)
        return pltpu.make_async_copy(buffer.at[part, :], gathered.at[part, :], out_sem.at[device])

    def work(device):
        part = pl.ds(pl.multiple_of(device * rows, rows), rows)
        keep(device).start()

        @pl.loop(0, columns.shape[0] // UNITS)
        def _(step):
            own = pl.ds(pl.multiple_of(step * UNITS, UNITS), UNITS)
            gate = dot(gate_weight[own, :], buffer[part, :], ROWS) + columns[own, 0:1]
            up = dot(up_weight[own, :], buffer[part, :], ROWS) + columns[own, 1:2]
            up = up * columns[own, 2:3]
            normal = 0.5 * (1.0 + lax.erf(gate * (0.5**0.5)))
            density = jnp.exp(-0.5 * gate * gate) * (0.5 / jnp.pi) ** 0.5
            gelu = gate * normal
            hidden[own, part] = (gelu * up).astype(BF16)
            gate_factor[own, part] = (up * (normal + gate * density)).astype(BF16)
            up_factor[own, part] = (gelu * columns[own, 2:3]).astype(BF16)

    work(ring.me)
    ring.from_mate(0)
    work(ring.mate)
    for hop in range(1, ring.chips):
        ring.advance(hop)
        work(ring.origin(hop))
        ring.from_mate(hop)
        work(ring.mates_origin(hop))
    ring.finish()
    for device in range(count):
        keep(device).wait()


def attention_to_feed(
    count, mixed, weight, tokens, gains, offsets, output_offset, gate_weight, up_weight, columns
):
    rows, width = tokens.shape
    units = columns.shape[0]
    total = rows * count
    vmem = pl.BlockSpec(memory_space=pltpu.VMEM)
    return pl.pallas_call(
        functools.partial(middle_kernel, count),
        in_specs=[vmem] * 9,
        out_specs=[vmem] * 3 + [pl.BlockSpec(memory_space=pl.ANY), vmem],
        out_shape=[jax.ShapeDtypeStruct((units, total), BF16)] * 3
        + [jax.ShapeDtypeStruct((total, width), BF16), jax.ShapeDtypeStruct((rows, width), F32)],
        scratch_shapes=[pltpu.VMEM((total, width), BF16)]
        + scatter_space(count, rows, width)
        + ring_sems(count)
        + scatter_sems(count)
        + [pltpu.SemaphoreType.DMA((count,))],
        compiler_params=pltpu.CompilerParams(
            collective_id=1, has_side_effects=True, vmem_limit_bytes=58 << 20
        ),
        cost_estimate=pl.CostEstimate(
            flops=4 * total * width * units,
            bytes_accessed=total * width * 8,
            transcendentals=2 * total * units,
        ),
        name="attention_to_feed",
    )(
        mixed, weight, tokens, gains, offsets, output_offset[None], gate_weight, up_weight, columns
    )


class Stage:
    def __init__(self, slots, sem):
        self.slots, self.sem, self.copies, self.waited = slots, sem, [], set()

    def settle(self, index):
        if index not in self.waited:
            self.copies[index].wait()
            self.waited.add(index)

    def emit(self, work, size, target):
        index = len(self.copies)
        if index >= 2:
            self.settle(index - 2)
        slot = self.slots.at[index % 2, pl.ds(0, size), :]

        @pl.loop(0, slot.shape[1] // TILE)
        def _(tile):
            cut = pl.ds(pl.multiple_of(tile * TILE, TILE), TILE)
            slot[:, cut] = work(cut).astype(BF16)

        copy = pltpu.make_async_copy(slot, target, self.sem.at[index])
        copy.start()
        self.copies.append(copy)
        return index

    def finish(self):
        for index in range(len(self.copies)):
            self.settle(index)


def back_kernel(
    count,
    line_count,
    used,
    hidden,
    shrink,
    gate_weight,
    up_weight,
    output_weight,
    mixed,
    middle,
    cotangent,
    gains,
    cotangent_all,
    second_all,
    gate_factor,
    up_factor,
    grad_mixed,
    grad_middle,
    sums,
    shrink_part,
    expand_part,
    output_part,
    shrink_whole,
    expand_whole,
    grads_out,
    grads,
    buffer,
    factors,
    staged,
    flipped,
    turned_mixed,
    *rest,
):
    rows, width = middle.shape
    units = hidden.shape[0]
    tokens = buffer.shape[0]
    sems = rest[7:]
    big_sem, factor_sem, stage_sem = sems[19:22]
    residual_scale = (2.0 * LAYERS) ** 0.5
    ring = Ring(count, rows, buffer, sems[:4])
    scatter = Scatter(ring, *rest[:4], sems[4:9])
    stage = Stage(staged, stage_sem)
    parts = piece_rows(0, used)
    pieces = [
        (shrink_part.at[pl.ds(a, n), :], shrink_whole.at[pl.ds(a, n), :]) for a, n in parts
    ]
    pieces[-1:] = [
        (expand_part.at[pl.ds(a, n), :], expand_whole.at[pl.ds(a, n), :])
        for a, n in parts[:EARLY]
    ] + pieces[-1:]
    copy_of = lambda k: (
        k if k < len(parts) - 1 else len(parts) - 1 if k == len(pieces) - 1 else k + 1
    )
    line = Line(line_count, pieces, *rest[4:7], sems[9:19])
    barrier = ring.greet()
    line.greet(barrier)
    load = pltpu.make_async_copy(cotangent_all, buffer, big_sem.at[0])
    load.start()

    def factor(block, slot):
        cut = pl.ds(pl.multiple_of(block * BLOCK, BLOCK), BLOCK)
        return [
            pltpu.make_async_copy(from_.at[:, cut], factors.at[slot, c], factor_sem.at[slot, c])
            for c, from_ in enumerate((gate_factor, up_factor))
        ]

    for copy in factor(0, 0):
        copy.start()
    line.met(barrier, 3)
    load.wait()

    def shrink_work(a, n):
        return lambda cut: jnp.dot(
            hidden[a : a + n, :], buffer[:, cut], preferred_element_type=F32
        )

    shrinks = list(parts)

    def emit_shrinks(many):
        for a, n in shrinks[:many]:
            stage.emit(shrink_work(a, n), n, shrink_part.at[pl.ds(a, n), :])
        del shrinks[:many]

    begun = min(LANDINGS, len(parts) - 1)
    emit_shrinks(begun)
    for k in range(begun):
        stage.settle(k)
        if k == 0:
            line.ready(0)
        line.begin(k)

    @pl.loop(0, tokens // BLOCK)
    def _(block):
        slot = block % 2
        for copy in factor(block, slot):
            copy.wait()

        @pl.when(block + 1 < tokens // BLOCK)
        def _():
            for copy in factor(block + 1, 1 - slot):
                copy.start()

        cut = pl.ds(pl.multiple_of(block * BLOCK, BLOCK), BLOCK)

        @pl.loop(0, units // UNITS)
        def _(step):
            own = pl.ds(pl.multiple_of(step * UNITS, UNITS), UNITS)
            grad_hidden = dot(shrink[own, :], buffer[cut, :], ROWS)
            grads[0, own, cut] = (grad_hidden * factors[slot, 0, own, :].astype(F32)).astype(BF16)
            grads[1, own, cut] = (grad_hidden * factors[slot, 1, own, :].astype(F32)).astype(BF16)

    load = pltpu.make_async_copy(second_all, buffer, big_sem.at[1])
    out = pltpu.make_async_copy(grads, grads_out, big_sem.at[2])
    out.start()
    turns, following = list(range(len(pieces) + 1)), list(range(begun, len(pieces)))

    def turn():
        if not turns:
            return
        new = [k for k in following if k <= turns[0] + LANDINGS]
        if any(copy_of(k) >= len(stage.copies) for k in new):
            return
        t = turns.pop(0)
        if t < len(pieces):
            line.join(t)
            if t + 1 < len(pieces):
                stage.settle(copy_of(t + 1))
                line.ready(t + 1)
        if t > 0:
            line.close(t - 1)
        for k in new:
            stage.settle(copy_of(k))
            line.begin(k)
            following.remove(k)

    expands = [(0, a, n) for a, n in parts[:EARLY]]

    def expand_work(c, a, n):
        return lambda cut: jnp.dot(
            grads[c, a : a + n, :], buffer[:, cut], preferred_element_type=F32
        )

    def emit_expands(many):
        for _ in range(min(many, len(expands))):
            c, a, n = expands.pop(0)
            stage.emit(expand_work(c, a, n), n, expand_part.at[pl.ds(a, n), :])

    def make(device, target):
        part = pl.ds(pl.multiple_of(device * rows, rows), rows)
        for c in range(2):
            flipped[c] = grads[c, :, part].T

        @pl.loop(0, width // TILE)
        def _(tile):
            cut = pl.ds(pl.multiple_of(tile * TILE, TILE), TILE)
            target[:, cut] = (
                jnp.dot(flipped[0], gate_weight[:, cut], preferred_element_type=F32)
                + jnp.dot(flipped[1], up_weight[:, cut], preferred_element_type=F32)
            ).astype(target.dtype)

    def beside(far):
        step = ring.chips - 1 - far
        if step < 2:
            emit_shrinks(-(-(len(parts) - begun) // 2))
        if step == 1:
            emit_shrinks(len(shrinks))
            load.start()
        if step == 2:
            load.wait()
            emit_expands(len(expands))
        turn()

    scatter.run(make, beside)
    grad_output = cotangent[...].astype(F32)
    hat, scale = normalize(middle[...])
    grad_in, gain, offset = normalize_back(
        residual_scale * grad_output + scatter.total[...], gains[1:2, :], hat, scale
    )
    grad_middle[...] = grad_in
    scatter.release()
    own = pl.ds(pl.multiple_of(ring.me * rows, rows), rows)
    buffer[own, :] = grad_in.astype(BF16)
    ring.begin()
    sums[0:1, :] = gain[None]
    sums[1:2, :] = offset[None]
    sums[2:3, :] = jnp.sum(grad_middle[...].astype(BF16).astype(F32), axis=0, keepdims=True)
    sums[3:4, :] = jnp.sum(cotangent[...].astype(F32), axis=0, keepdims=True)
    sums[4:8, :] = jnp.zeros((4, width), F32)
    ones = jnp.ones((16, tokens), BF16)
    for c in range(2):
        sums[4 + c : 5 + c, :units] = dot(ones, grads[c], ROWS)[:1]

    summed = scatter.total.at[pl.ds(0, mixed.shape[1]), :]
    summed[...] = jnp.zeros(summed.shape, F32)

    def work(device):
        part = pl.ds(pl.multiple_of(device * rows, rows), rows)
        grad_mixed[part, :] = dot(buffer[part, :], output_weight[...], ROWS).astype(BF16)
        turned_mixed[...] = mixed[part, :].T

        @pl.loop(0, width // TILE)
        def _(tile):
            cut = pl.ds(pl.multiple_of(tile * TILE, TILE), TILE)
            summed[:, cut] += jnp.dot(
                turned_mixed[...], buffer[part, cut], preferred_element_type=F32
            )


    work(ring.me)
    ring.from_mate(0)
    work(ring.mate)
    turn()
    for hop in range(1, ring.chips):
        ring.advance(hop)
        work(ring.origin(hop))
        ring.from_mate(hop)
        work(ring.mates_origin(hop))
        turn()
        if hop > 1:
            turn()
    for a, n in piece_rows(0, mixed.shape[1]):
        stage.emit(
            lambda cut: summed[a : a + n, cut],
            n,
            output_part.at[pl.ds(a, n), :],
        )
    ring.finish()
    for _ in range(len(pieces) + 1):
        turn()
    for k in range(len(pieces)):
        line.spread(k)
    line.finish()
    stage.finish()
    out.wait()


def back(
    count,
    line_count,
    used,
    hidden,
    shrink,
    gate_weight,
    up_weight,
    output_weight,
    mixed,
    middle,
    cotangent,
    gains,
    cotangent_all,
    second_all,
    gate_factor,
    up_factor,
):
    rows, width = middle.shape
    units, total = hidden.shape
    heads = mixed.shape[1]
    vmem, any_ = pl.BlockSpec(memory_space=pltpu.VMEM), pl.BlockSpec(memory_space=pl.ANY)
    parts = piece_rows(0, used)
    pieces = len(parts) + len(parts[:EARLY])
    return pl.pallas_call(
        functools.partial(back_kernel, count, line_count, used),
        in_specs=[vmem] * 9 + [any_] * 4,
        out_specs=[vmem] * 3 + [any_] * 6,
        out_shape=[
            jax.ShapeDtypeStruct((total, heads), BF16),
            jax.ShapeDtypeStruct((rows, width), F32),
            jax.ShapeDtypeStruct((8, width), F32),
            jax.ShapeDtypeStruct((used, width), BF16),
            jax.ShapeDtypeStruct((sum(n for _, n in parts[:EARLY]), width), BF16),
            jax.ShapeDtypeStruct((heads, width), BF16),
            jax.ShapeDtypeStruct((used, width), BF16),
            jax.ShapeDtypeStruct((sum(n for _, n in parts[:EARLY]), width), BF16),
            jax.ShapeDtypeStruct((2, units, total), BF16),
        ],
        scratch_shapes=[
            pltpu.VMEM((2, units, total), BF16),
            pltpu.VMEM((total, width), BF16),
            pltpu.VMEM((2, 2, units, BLOCK), BF16),
            pltpu.VMEM((2, PIECE, width), BF16),
            pltpu.VMEM((2, rows, units), BF16),
            pltpu.VMEM((heads, rows), BF16),
        ]
        + scatter_space(count, rows, width)
        + line_space(width)
        + ring_sems(count)
        + scatter_sems(count)
        + line_sems(pieces)
        + [
            pltpu.SemaphoreType.DMA((3,)),
            pltpu.SemaphoreType.DMA((2, 2)),
            pltpu.SemaphoreType.DMA((pieces + heads // PIECE,)),
        ],
        compiler_params=pltpu.CompilerParams(
            collective_id=2, has_side_effects=True, vmem_limit_bytes=60 << 20
        ),
        cost_estimate=pl.CostEstimate(
            flops=18 * total * width * units, bytes_accessed=total * width * 8, transcendentals=0
        ),
        name="back",
    )(
        hidden,
        shrink,
        gate_weight,
        up_weight,
        output_weight,
        mixed,
        middle,
        cotangent,
        gains,
        cotangent_all,
        second_all,
        gate_factor,
        up_factor,
    )


def blocks_turned(values):
    side = values.shape[0]
    return jnp.concatenate(
        [values[:, at : at + side].T for at in range(0, values.shape[1], side)], axis=1
    )


def tail_kernel(
    count,
    line_count,
    used,
    packed,
    mixed,
    grad_mixed,
    peaks,
    cosine,
    sine,
    low,
    high,
    input_weight,
    hidden,
    shrink,
    middle,
    tokens,
    grad_middle,
    gains,
    offsets,
    shrink_offset,
    early_sums,
    first_all,
    second_all,
    grads,
    output_part,
    layer_out,
    tokens_grad,
    sums,
    expand_part,
    input_part,
    expand_whole,
    output_whole,
    input_whole,
    grad_projected,
    keys_t,
    inner,
    grad_keys,
    grad_values,
    buffer,
    lefts,
    staged,
    group_box,
    line_box,
    *rest,
):
    rows, width = middle.shape
    units = hidden.shape[0]
    seq_count, heads = peaks.shape[0], peaks.shape[1]
    sems = rest[7:]
    big_sem, left_sem, stage_sem = sems[15:18]
    residual_scale = (2.0 * LAYERS) ** 0.5
    ring = Ring(count, rows, None, [None] * 4)
    scatter = Scatter(ring, *rest[:4], sems[:5])
    stage = Stage(staged, stage_sem)
    expands = [(c, a, n) for c in range(2) for a, n in piece_rows(0, used)[EARLY if c == 0 else 0 :]]
    short = [e for e in expands if e[2] < PIECE]
    expands = [e for e in expands if e[2] == PIECE] + short
    lasts = piece_rows(0, grad_projected.shape[1])
    outs = piece_rows(0, output_part.shape[0])
    pieces = (
        [(output_part.at[pl.ds(a, n), :], output_whole.at[pl.ds(a, n), :]) for a, n in outs]
        + [
            (
                expand_part.at[pl.ds(c * units + a, n), :],
                expand_whole.at[pl.ds(c * units + a, n), :],
            )
            for c, a, n in expands
        ]
        + [(input_part.at[pl.ds(a, n), :], input_whole.at[pl.ds(a, n), :]) for a, n in lasts]
    )
    ahead = len(outs)
    full = ahead + len(expands) - len(short)
    tail_order = pieces[full : full + len(short)]
    pieces = pieces[:full] + pieces[full + len(short) :] + tail_order
    line = Line(line_count, pieces, *rest[4:7], sems[5:15])
    me, here = ring.me, lax.axis_index("dp")
    barrier = pltpu.get_barrier_semaphore()
    for axis, place, size in (("tp", me, count), ("dp", here, line_count)):
        for i in range(1, size):
            pl.semaphore_signal(
                barrier, inc=1, device_id={axis: (place + i) % size}, device_id_type=MESH
            )
    load = pltpu.make_async_copy(second_all, buffer, big_sem.at[0])
    load.start()

    def left(e):
        c, a, n = expands[e]
        return pltpu.make_async_copy(
            grads.at[c, pl.ds(a, n), :], lefts.at[e % 2, pl.ds(0, n), :], left_sem.at[e]
        )

    left(0).start()
    line.ready(0)
    pl.semaphore_wait(barrier, count + line_count - 2)
    done = [0]

    def copy_of(k):
        if k < full:
            return k - ahead
        if k < full + len(lasts):
            return k - full + len(expands)
        return k - len(lasts) - ahead


    def emit():
        e = done[0]
        if e == len(expands):
            return
        done[0] += 1
        left(e).wait()
        if e + 1 < len(expands):
            left(e + 1).start()
        n = expands[e][2]
        stage.emit(
            lambda cut: jnp.dot(
                lefts[e % 2, pl.ds(0, n), :], buffer[:, cut], preferred_element_type=F32
            ),
            n,
            expand_part.at[pl.ds(expands[e][0] * units + expands[e][1], n), :],
        )

    def there(k):
        if k >= ahead:
            while copy_of(k) >= len(stage.copies) and done[0] < len(expands):
                emit()
            stage.settle(copy_of(k))

    turns = list(range(len(pieces) + 1))

    def turn():
        if not turns:
            return
        new = [k for k in following if k <= turns[0] + LANDINGS]
        for k in new:
            late = full <= k < full + len(lasts)
            if k >= ahead and copy_of(k) >= len(stage.copies):
                if late or done[0] == len(expands):
                    return
        t = turns.pop(0)
        if t < len(pieces):
            line.join(t)
            if t + 1 < len(pieces):
                there(t + 1)
                line.ready(t + 1)
        if t > 0:
            line.close(t - 1)
        for k in new:
            there(k)
            line.begin(k)
            following.remove(k)

    following = list(range(LANDINGS, len(pieces)))
    for k in range(min(ahead, LANDINGS)):
        line.begin(k)
    load.wait()
    for k in range(ahead, LANDINGS):
        there(k)
        line.begin(k)

    for s in range(seq_count):
        for h in range(heads):
            span = pl.ds(s * SEQ_LEN, SEQ_LEN)
            head = pl.ds(h * HEAD_DIM, HEAD_DIM)
            three = pl.ds(h * 3 * HEAD_DIM, 3 * HEAD_DIM)
            attend_back(
                packed.at[span, three],
                mixed.at[span, head],
                grad_mixed.at[span, head],
                peaks.at[s, h],
                cosine.at[s],
                sine.at[s],
                low.at[s],
                high.at[s],
                grad_projected.at[span, three],
                keys_t,
                inner,
                grad_keys,
                grad_values,
            )
            emit()
            turn()
            emit()

    while done[0] < len(expands):
        emit()
    load = pltpu.make_async_copy(first_all, buffer, big_sem.at[1])
    load.start()
    load.wait()
    inputs = list(lasts)

    def emit_input():
        if inputs:
            a, n = inputs.pop(0)
            stage.emit(
                lambda cut: blocks_turned(dot(grad_projected[:, a : a + n], buffer[:, cut], COLS)),
                n,
                input_part.at[pl.ds(a, n), :],
            )

    def between(far):
        emit_input()
        turn()
        emit_input()

    def make(device, target):
        part = pl.ds(pl.multiple_of(device * rows, rows), rows)

        @pl.loop(0, width // TILE)
        def _(tile):
            cut = pl.ds(pl.multiple_of(tile * TILE, TILE), TILE)
            target[:, cut] = dot(grad_projected[part, :], input_weight[cut, :], ROWS).astype(
                target.dtype
            )

    scatter.run(make, between)
    while inputs:
        emit_input()
    hat, scale = normalize(tokens[...].astype(F32))
    grad_in, gain, offset = normalize_back(
        residual_scale * grad_middle[...] + scatter.total[...], gains[0:1, :], hat, scale
    )
    scatter.total[...] = grad_in
    keep = pltpu.make_async_copy(scatter.total, tokens_grad, big_sem.at[2])
    keep.start()
    small = group_box.at[me]
    small[0:1, :] = gain[None]
    small[1:2, :] = early_sums[0:1, :]
    small[2:3, :] = offset[None]
    small[3:4, :] = early_sums[1:2, :]
    small[4:6, :] = early_sums[2:4, :]
    small[6:8, :] = early_sums[4:6, :]
    scatter.release()
    turn()
    wide = grad_projected.shape[1]
    small[6:7, width - wide :] = jnp.dot(
        jnp.ones((16, grad_projected.shape[0]), BF16),
        grad_projected[...],
        preferred_element_type=F32,
    )[:1]

    def swaps(box, axis, place, size, send, recv):
        return [
            pltpu.make_async_remote_copy(
                src_ref=box.at[place],
                dst_ref=box.at[place],
                send_sem=send.at[i],
                recv_sem=recv.at[i],
                device_id={axis: (place + i) % size},
                device_id_type=MESH,
            )
            for i in range(1, size)
        ]

    group_swaps = swaps(group_box, "tp", me, count, *sems[18:20])
    line_swaps = swaps(line_box, "dp", here, line_count, *sems[20:22])
    for copy in group_swaps:
        copy.start()
    turn()

    def make_out(device, target):
        part = pl.ds(pl.multiple_of(device * rows, rows), rows)

        @pl.loop(0, width // TILE)
        def _(tile):
            cut = pl.ds(pl.multiple_of(tile * TILE, TILE), TILE)
            target[:, cut] = dot(hidden[:, part], shrink[:, cut], COLS).astype(target.dtype)

    keep.wait()
    scatter.run(make_out, lambda far: turn())
    hat, _ = normalize(middle[...])
    scatter.total[...] = (
        residual_scale * (hat * gains[1:2, :] + offsets[1:2, :])
        + scatter.total[...]
        + shrink_offset[...]
    )
    keep = pltpu.make_async_copy(scatter.total, layer_out, big_sem.at[3])
    keep.start()
    turn()
    for copy in group_swaps:
        copy.wait()
    line_box[here, 0:6, :] = sum(group_box[d, 0:6, :] for d in range(count))
    line_box[here, 6:8, :] = small[6:8, :]
    for copy in line_swaps:
        copy.start()
    for _ in range(len(pieces) + 1):
        turn()
    for copy in line_swaps:
        copy.wait()
    sums[...] = sum(line_box[d] for d in range(line_count))
    for k in range(len(pieces)):
        line.spread(k)
    line.finish()
    stage.finish()
    keep.wait()


def tail(
    count,
    line_count,
    used,
    packed,
    mixed,
    grad_mixed,
    peaks,
    cosine,
    sine,
    low,
    high,
    input_weight,
    hidden,
    shrink,
    middle,
    tokens,
    grad_middle,
    gains,
    offsets,
    shrink_offset,
    early_sums,
    first_all,
    second_all,
    grads,
    output_part,
):
    rows, width = middle.shape
    units, total = hidden.shape
    columns = packed.shape[1]
    heads = output_part.shape[0]
    vmem, any_ = pl.BlockSpec(memory_space=pltpu.VMEM), pl.BlockSpec(memory_space=pl.ANY)
    parts, lasts = piece_rows(0, used), len(piece_rows(0, columns))
    expands = len(parts[EARLY:]) + len(parts)
    pieces = expands + len(piece_rows(0, heads)) + lasts
    blocks = SEQ_LEN // BLOCK
    return pl.pallas_call(
        functools.partial(tail_kernel, count, line_count, used),
        in_specs=[vmem] * 18 + [any_] * 4,
        out_specs=[any_] * 2 + [vmem] + [any_] * 5,
        out_shape=[
            jax.ShapeDtypeStruct((rows, width), F32),
            jax.ShapeDtypeStruct((rows, width), F32),
            jax.ShapeDtypeStruct((8, width), F32),
            jax.ShapeDtypeStruct((2 * units, width), BF16),
            jax.ShapeDtypeStruct((columns, width), BF16),
            jax.ShapeDtypeStruct((2 * units, width), BF16),
            jax.ShapeDtypeStruct((heads, width), BF16),
            jax.ShapeDtypeStruct((columns, width), BF16),
        ],
        scratch_shapes=[
            pltpu.VMEM((total, columns), BF16),
            pltpu.VMEM((blocks, HEAD_DIM, BLOCK), BF16),
            pltpu.VMEM((blocks, 1, BLOCK), F32),
            pltpu.VMEM((SEQ_LEN, HEAD_DIM), F32),
            pltpu.VMEM((SEQ_LEN, HEAD_DIM), F32),
            pltpu.VMEM((total, width), BF16),
            pltpu.VMEM((2, PIECE, width), BF16),
            pltpu.VMEM((2, PIECE, width), BF16),
            pltpu.VMEM((count, 8, width), F32),
            pltpu.VMEM((line_count, 8, width), F32),
        ]
        + scatter_space(count, rows, width)
        + line_space(width)
        + scatter_sems(count)
        + line_sems(pieces)
        + [
            pltpu.SemaphoreType.DMA((4,)),
            pltpu.SemaphoreType.DMA((expands,)),
            pltpu.SemaphoreType.DMA((expands + lasts,)),
        ]
        + [pltpu.SemaphoreType.DMA((count,))] * 2
        + [pltpu.SemaphoreType.DMA((line_count,))] * 2,
        compiler_params=pltpu.CompilerParams(
            collective_id=3, has_side_effects=True, vmem_limit_bytes=60 << 20
        ),
        cost_estimate=pl.CostEstimate(
            flops=4 * total * width * (columns + units),
            bytes_accessed=total * width * 8,
            transcendentals=0,
        ),
        name="tail",
    )(
        packed,
        mixed,
        grad_mixed,
        peaks,
        cosine,
        sine,
        low[:, None],
        high[:, None],
        input_weight,
        hidden,
        shrink,
        middle,
        tokens,
        grad_middle,
        gains,
        offsets,
        shrink_offset[None],
        early_sums,
        first_all,
        second_all,
        grads,
        output_part,
    )


def finish_kernel(early, gate, up, shrink, output, inputs, expand_out, shrink_out, output_out, input_out):
    rows, ahead = expand_out.shape[0], early.shape[0]
    expand_out[:ahead, 0, :] = early[...].astype(F32)
    expand_out[ahead:, 0, :] = gate[ahead:rows, :].astype(F32)
    expand_out[:, 1, :] = up[:rows, :].astype(F32)
    shrink_out[...] = shrink[:rows, :].astype(F32)
    output_out[...] = output[...].astype(F32)
    for at in range(0, inputs.shape[0], PIECE):
        for cut in range(0, inputs.shape[1], PIECE):
            input_out[cut : cut + PIECE, at : at + PIECE] = inputs[
                at : at + PIECE, cut : cut + PIECE
            ].astype(F32)


def finish(early, both, shrink, output, inputs, rows):
    units, width = both.shape[0] // 2, both.shape[1]
    columns, heads = inputs.shape[0], output.shape[0]
    tile = 256
    part = lambda a: pl.BlockSpec((a.shape[0], tile), lambda j: (0, j))
    return pl.pallas_call(
        finish_kernel,
        grid=(width // tile,),
        in_specs=[
            part(early),
            pl.BlockSpec((units, tile), lambda j: (0, j)),
            pl.BlockSpec((units, tile), lambda j: (1, j)),
            part(shrink),
            part(output),
            part(inputs),
        ],
        out_specs=[
            pl.BlockSpec((rows, 2, tile), lambda j: (0, 0, j)),
            pl.BlockSpec((rows, tile), lambda j: (0, j)),
            pl.BlockSpec((heads, tile), lambda j: (0, j)),
            pl.BlockSpec((tile, columns), lambda j: (j, 0)),
        ],
        out_shape=[
            jax.ShapeDtypeStruct((rows, 2, width), F32),
            jax.ShapeDtypeStruct((rows, width), F32),
            jax.ShapeDtypeStruct((heads, width), F32),
            jax.ShapeDtypeStruct((width, columns), F32),
        ],
        compiler_params=pltpu.CompilerParams(vmem_limit_bytes=40 << 20),
        cost_estimate=pl.CostEstimate(
            flops=0, bytes_accessed=6 * width * (3 * rows + heads + columns), transcendentals=0
        ),
        name="finish",
    )(early, both, both, shrink, output, inputs)


def local(
    dp,
    tp,
    tokens,
    segment_ids,
    prefix_lengths,
    positions,
    norm_gains,
    norm_offsets,
    input_weight,
    input_offset,
    output_weight,
    output_offset,
    expand_weight,
    expand_offset,
    shrink_weight,
    shrink_offset,
    cotangent,
):
    seq_count = segment_ids.shape[0]
    units_used = expand_weight.shape[2]
    units = -(-units_used // UNITS) * UNITS
    used = -(-units_used // 16) * 16

    pad = ((0, units - units_used), (0, 0))
    turned_expand = jnp.transpose(expand_weight, (2, 1, 0))
    gate_weight, up_weight = jnp.pad(turned_expand[:, 0], pad), jnp.pad(turned_expand[:, 1], pad)
    shrink = jnp.pad(shrink_weight, pad)
    unit_index = lax.axis_index("tp") * units_used + lax.iota(jnp.int32, units_used)
    keep_units = (unit_index < FF_USED).astype(F32)
    columns = jnp.pad(jnp.stack([expand_offset[0], expand_offset[1], keep_units], axis=1), pad)

    row_at = lax.broadcasted_iota(jnp.int32, positions.shape, 1)
    low = row_at - positions
    matches = segment_ids[:, :, None] == lax.iota(jnp.int32, prefix_lengths.shape[1])
    own_prefix = jnp.sum(jnp.where(matches, prefix_lengths[:, None, :], 0), axis=2)
    high = jnp.maximum(row_at, low + own_prefix - 1)
    bounds = jnp.stack(
        [
            jnp.min(low.reshape(seq_count, -1, BLOCK), axis=2) // BLOCK,
            jnp.max(high.reshape(seq_count, -1, BLOCK), axis=2) // BLOCK + 1,
        ],
        axis=2,
    )
    cosine, sine = rotary_tables(positions)

    projected, first_all = project(
        tp, tokens, norm_gains[:1], norm_offsets[:1], input_weight, input_offset
    )
    waiting, first_all = lax.optimization_barrier((cotangent, first_all))
    cotangent_all = lax.all_gather(waiting, "tp", axis=0, tiled=True)
    packed, mixed, peaks = attend_forward(projected, cosine, sine, low, high, bounds)
    hidden, gate_factor, up_factor, second_all, middle = attention_to_feed(
        tp,
        mixed,
        output_weight,
        tokens,
        norm_gains,
        norm_offsets,
        output_offset,
        gate_weight,
        up_weight,
        columns,
    )

    grad_mixed, grad_middle, sums, _, _, output_part, shrink_whole, expand_early, grads = back(
        tp,
        dp,
        used,
        hidden,
        shrink,
        gate_weight,
        up_weight,
        output_weight,
        mixed,
        middle,
        cotangent,
        norm_gains,
        cotangent_all,
        second_all,
        gate_factor,
        up_factor,
    )
    layer_out, tokens_grad, small_sums, _, _, expand_whole, output_whole, input_whole = tail(
        tp,
        dp,
        used,
        packed,
        mixed,
        grad_mixed,
        peaks,
        cosine,
        sine,
        low,
        high,
        input_weight,
        hidden,
        shrink,
        middle,
        tokens,
        grad_middle,
        norm_gains,
        norm_offsets,
        shrink_offset,
        sums,
        first_all,
        second_all,
        grads,
        output_part,
    )

    expand_grad, shrink_grad, output_grad, input_grad = finish(
        expand_early, expand_whole, shrink_whole, output_whole, input_whole, units_used
    )
    return (
        layer_out,
        tokens_grad,
        input_grad,
        small_sums[6, small_sums.shape[1] - input_weight.shape[1] :],
        output_grad,
        small_sums[4],
        jnp.transpose(expand_grad, (2, 1, 0)),
        small_sums[6:8, :units_used],
        shrink_grad,
        small_sums[5],
        small_sums[0:2],
        small_sums[2:4],
    )


def solution(mesh):
    in_specs = (
        P(("dp", "tp"), None),
        P("dp", None),
        P("dp", None),
        P("dp", None),
        P(),
        P(),
        P(None, "tp"),
        P("tp"),
        P("tp", None),
        P(),
        P(None, None, "tp"),
        P(None, "tp"),
        P("tp", None),
        P(),
        P(("dp", "tp"), None),
    )
    out_specs = (
        P(("dp", "tp"), None),
        P(("dp", "tp"), None),
        P(None, "tp"),
        P("tp"),
        P("tp", None),
        P(),
        P(None, None, "tp"),
        P(None, "tp"),
        P("tp", None),
        P(),
        P(),
        P(),
    )
    return jax.shard_map(
        functools.partial(local, mesh.shape["dp"], mesh.shape["tp"]),
        mesh=mesh,
        in_specs=in_specs,
        out_specs=out_specs,
        check_vma=False,
    )
```

```python
import functools

import jax
import jax.numpy as jnp
from jax import lax
from jax.experimental import pallas as pl
from jax.experimental.pallas import tpu as pltpu
from jax.sharding import PartitionSpec as P

HEAD_DIM = 128
FF_USED = 5461
LAYERS = 24
SEQ_LEN = 1024
BLOCK = 256
TILE = 512
UNITS = 176

epsilon = 1e-05
rope_base = 10000.0
masked_score = -1e30
F32 = jnp.float32
BF16 = jnp.bfloat16
ROWS = (((1,), (1,)), ((), ()))
MESH = pl.DeviceIdType.MESH
COLS = (((0,), (0,)), ((), ()))


def dot(left, right, dims):
    return lax.dot_general(left, right, dims, preferred_element_type=F32)


def normalize(values):
    average = jnp.mean(values, axis=-1, keepdims=True)
    centred = values - average
    variance = jnp.mean(centred * centred, axis=-1, keepdims=True)
    scale = lax.rsqrt(variance + epsilon)
    return centred * scale, scale


def normalize_back(grad, gains, hat, scale):
    pulled = grad * gains
    grad_in = scale * (
        pulled
        - jnp.mean(pulled, axis=-1, keepdims=True)
        - hat * jnp.mean(pulled * hat, axis=-1, keepdims=True)
    )
    return grad_in, jnp.sum(grad * hat, axis=0), jnp.sum(grad, axis=0)


def rotary_tables(places):
    half_dim = HEAD_DIM // 2
    exponents = lax.iota(F32, half_dim) * (-2.0 / HEAD_DIM)
    rates = jnp.power(rope_base, exponents)
    angles = places.astype(F32)[..., None] * rates
    cosine, sine = jnp.cos(angles), jnp.sin(angles)
    return jnp.concatenate([cosine, cosine], -1), jnp.concatenate([-sine, sine], -1)


def turned(values, cosine, sine):
    return values * cosine + pltpu.roll(values, HEAD_DIM // 2, 1) * sine


def attend_forward_kernel(bounds, projected, cosine, sine, low, high, packed, mixed, peaks, values_t):
    seq = pl.program_id(0)
    score_scale = HEAD_DIM ** (-0.5)
    packed[:, :HEAD_DIM] = turned(projected[:, :HEAD_DIM], cosine[...], sine[...]).astype(BF16)
    packed[:, HEAD_DIM : 2 * HEAD_DIM] = turned(
        projected[:, HEAD_DIM : 2 * HEAD_DIM], cosine[...], sine[...]
    ).astype(BF16)
    packed[:, 2 * HEAD_DIM :] = projected[:, 2 * HEAD_DIM :].astype(BF16)
    for b in range(SEQ_LEN // BLOCK):
        values_t[b] = projected[b * BLOCK : (b + 1) * BLOCK, 2 * HEAD_DIM :].T.astype(BF16)

    def queries_block(b, _):
        start = pl.multiple_of(b * BLOCK, BLOCK)
        queries = packed[pl.ds(start, BLOCK), :HEAD_DIM]
        first = low[0, 0, pl.ds(start, BLOCK)][None, :]
        last = high[0, 0, pl.ds(start, BLOCK)][None, :]

        def keys_block(j, carry):
            peak, total, gathered = carry
            keys = packed[pl.ds(pl.multiple_of(j * BLOCK, BLOCK), BLOCK), HEAD_DIM : 2 * HEAD_DIM]
            scores = dot(keys, queries, ROWS) * score_scale
            place = lax.broadcasted_iota(jnp.int32, (BLOCK, BLOCK), 0) + j * BLOCK
            scores = jnp.where((place >= first) & (place <= last), scores, masked_score)
            new_peak = jnp.maximum(peak, jnp.max(scores, axis=0, keepdims=True))
            shifted = jnp.exp(scores - new_peak)
            fade = jnp.exp(peak - new_peak)
            total = total * fade + jnp.sum(shifted, axis=0, keepdims=True)
            gathered = gathered * fade + jnp.dot(
                values_t[j], shifted.astype(BF16), preferred_element_type=F32
            )
            return new_peak, total, gathered

        peak, total, gathered = lax.fori_loop(
            bounds[seq, b, 0],
            bounds[seq, b, 1],
            keys_block,
            (
                jnp.full((1, BLOCK), masked_score, F32),
                jnp.zeros((1, BLOCK), F32),
                jnp.zeros((HEAD_DIM, BLOCK), F32),
            ),
        )
        mixed[pl.ds(start, BLOCK), :] = (gathered / total).T.astype(BF16)
        peaks[0, 0, 0, pl.ds(start, BLOCK)] = (peak + jnp.log(total))[0]
        return 0

    lax.fori_loop(0, SEQ_LEN // BLOCK, queries_block, 0)


def attend_forward(projected, cosine, sine, low, high, bounds):
    seq_count, heads = cosine.shape[0], projected.shape[1] // (3 * HEAD_DIM)
    rows = seq_count * SEQ_LEN
    per_head = pl.BlockSpec((SEQ_LEN, 3 * HEAD_DIM), lambda s, h, *_: (s, h))
    table = pl.BlockSpec((None, SEQ_LEN, HEAD_DIM), lambda s, h, *_: (s, 0, 0))
    line = pl.BlockSpec((1, 1, SEQ_LEN), lambda s, h, *_: (s, 0, 0))
    return pl.pallas_call(
        attend_forward_kernel,
        grid_spec=pltpu.PrefetchScalarGridSpec(
            num_scalar_prefetch=1,
            grid=(seq_count, heads),
            in_specs=[per_head, table, table, line, line],
            out_specs=[
                per_head,
                pl.BlockSpec((SEQ_LEN, HEAD_DIM), lambda s, h, *_: (s, h)),
                pl.BlockSpec((1, 1, 1, SEQ_LEN), lambda s, h, *_: (s, h, 0, 0)),
            ],
            scratch_shapes=[pltpu.VMEM((SEQ_LEN // BLOCK, HEAD_DIM, BLOCK), BF16)],
        ),
        out_shape=[
            jax.ShapeDtypeStruct(projected.shape, BF16),
            jax.ShapeDtypeStruct((rows, heads * HEAD_DIM), BF16),
            jax.ShapeDtypeStruct((seq_count, heads, 1, SEQ_LEN), F32),
        ],
        compiler_params=pltpu.CompilerParams(vmem_limit_bytes=40 << 20),
        cost_estimate=pl.CostEstimate(
            flops=4 * rows * SEQ_LEN * HEAD_DIM * heads,
            bytes_accessed=rows * heads * HEAD_DIM * 20,
            transcendentals=rows * SEQ_LEN * heads,
        ),
        name="attend_forward",
    )(bounds, projected, cosine, sine, low[:, None], high[:, None])


def attend_back(
    packed, mixed, grad_mixed, peaks, cosine, sine, low, high, grad, keys_t, inner, grad_keys, grad_values
):
    score_scale = HEAD_DIM ** (-0.5)
    for b in range(SEQ_LEN // BLOCK):
        part = slice(b * BLOCK, (b + 1) * BLOCK)
        keys_t[b] = packed[part, HEAD_DIM : 2 * HEAD_DIM].astype(F32).T.astype(BF16)
        both = grad_mixed[part, :].astype(F32) * mixed[part, :].astype(F32)
        inner[b] = jnp.sum(both.T, axis=0, keepdims=True)
    grad_keys[...] = jnp.zeros_like(grad_keys)
    grad_values[...] = jnp.zeros_like(grad_values)

    @pl.loop(0, SEQ_LEN // BLOCK)
    def _(b):
        rows = pl.ds(pl.multiple_of(b * BLOCK, BLOCK), BLOCK)
        queries = packed[rows, :HEAD_DIM]
        pulled = grad_mixed[rows, :]
        first, last = low[:, rows], high[:, rows]
        peak = peaks[:, rows]
        inner_sum = inner[b]

        def keys_block(j, total):
            part = pl.ds(pl.multiple_of(j * BLOCK, BLOCK), BLOCK)
            keys = packed[part, HEAD_DIM : 2 * HEAD_DIM]
            values = packed[part, 2 * HEAD_DIM :]
            scores = dot(keys, queries, ROWS) * score_scale
            place = lax.broadcasted_iota(jnp.int32, (BLOCK, BLOCK), 0) + j * BLOCK
            scores = jnp.where((place >= first) & (place <= last), scores, masked_score)
            probs = jnp.exp(scores - peak)
            grad_probs = dot(values, pulled, ROWS)
            grad_scores = (probs * (grad_probs - inner_sum)).astype(BF16)
            grad_values[part, :] += jnp.dot(probs.astype(BF16), pulled, preferred_element_type=F32)
            grad_keys[part, :] += jnp.dot(grad_scores, queries, preferred_element_type=F32)
            return total + jnp.dot(keys_t[j], grad_scores, preferred_element_type=F32)

        total = lax.fori_loop(
            0, SEQ_LEN // BLOCK, keys_block, jnp.zeros((HEAD_DIM, BLOCK), F32)
        )
        grad_queries = total.T * score_scale
        grad[rows, :HEAD_DIM] = turned(grad_queries, cosine[rows, :], -sine[rows, :]).astype(BF16)

    grad[:, HEAD_DIM : 2 * HEAD_DIM] = turned(
        grad_keys[...] * score_scale, cosine[...], -sine[...]
    ).astype(BF16)
    grad[:, 2 * HEAD_DIM :] = grad_values[...].astype(BF16)


class Ring:
    def __init__(self, count, rows, buffer, sems):
        self.chips, self.rows, self.buffer = count // 2, rows, buffer
        self.ring_send, self.ring_recv, self.core_send, self.core_recv = sems
        me = lax.axis_index("tp")
        self.core, self.chip = me % 2, me // 2
        self.spot = self.place(self.chip)
        self.way = 1 - 2 * self.core
        self.next = self.place((self.spot + self.way + self.chips) % self.chips) * 2 + self.core
        self.last = self.place((self.spot - self.way + self.chips) % self.chips) * 2 + self.core
        self.me, self.mate = me, me + self.way

    def place(self, spot):
        turn = self.chips // 2
        return spot + (spot // turn) * (self.chips - 1 + turn - 2 * spot)

    def origin(self, hop):
        return self.place((self.spot - hop * self.way + hop * self.chips) % self.chips) * 2 + self.core

    def mates_origin(self, hop):
        spot = (self.spot + hop * self.way + hop * self.chips) % self.chips
        return self.place(spot) * 2 + 1 - self.core

    def part(self, device, half):
        size = self.rows // 2
        return pl.ds(pl.multiple_of(device * self.rows + half * size, size), size)

    def copy(self, device, half, send, recv, to):
        part = self.buffer.at[self.part(device, half), :]
        return pltpu.make_async_remote_copy(
            src_ref=part,
            dst_ref=part,
            send_sem=send,
            recv_sem=recv,
            device_id={"tp": to},
            device_id_type=MESH,
        )

    def greet(self):
        barrier = pltpu.get_barrier_semaphore()
        for other in (self.next, self.last, self.mate):
            pl.semaphore_signal(
                barrier, inc=1, device_id={"tp": other}, device_id_type=MESH
            )
        return barrier

    def along(self, hop, half, device):
        return self.copy(device, half, self.ring_send.at[hop, half], self.ring_recv.at[hop, half], self.next)

    def across(self, hop, half, device):
        return self.copy(device, half, self.core_send.at[hop, half], self.core_recv.at[hop, half], self.mate)

    def begin(self):
        for half in range(2):
            self.along(0, half, self.me).start()
            self.across(0, half, self.me).start()

    def advance(self, hop):
        device = self.origin(hop)
        for half in range(2):
            self.along(hop - 1, half, device).wait_recv()
            if hop < self.chips - 1:
                self.along(hop, half, device).start()
            self.across(hop, half, device).start()

    def from_mate(self, hop):
        device = self.mates_origin(hop)
        for half in range(2):
            self.across(hop, half, device).wait_recv()

    def finish(self):
        for half in range(2):
            for hop in range(self.chips):
                if hop < self.chips - 1:
                    self.along(hop, half, self.me).wait_send()
                self.across(hop, half, self.me).wait_send()


def ring_sems(count):
    chips = count // 2
    return [pltpu.SemaphoreType.DMA((chips, 2))] * 4


def project_kernel(
    count,
    tokens,
    gains,
    offsets,
    weight,
    bias,
    expand,
    projected,
    gate_weight,
    up_weight,
    gathered,
    buffer,
    woven,
    *rest,
):
    sems, out_sem, load_sem = rest[:4], rest[4], rest[5]
    load = pltpu.make_async_copy(expand, woven, load_sem)
    load.start()
    rows = tokens.shape[0]
    ring = Ring(count, rows, buffer, sems)
    barrier = ring.greet()
    hat, _ = normalize(tokens[...].astype(F32))
    own = pl.ds(pl.multiple_of(ring.me * rows, rows), rows)
    buffer[own, :] = (hat * gains[...] + offsets[...]).astype(BF16)
    pl.semaphore_wait(barrier, 3)
    ring.begin()

    def keep(device):
        part = pl.ds(pl.multiple_of(device * rows, rows), rows)
        return pltpu.make_async_copy(buffer.at[part, :], gathered.at[part, :], out_sem.at[device])

    def work(device):
        part = pl.ds(pl.multiple_of(device * rows, rows), rows)
        keep(device).start()
        projected[part, :] = (
            jnp.dot(buffer[part, :], weight[...], preferred_element_type=F32) + bias[...]
        )

    used, units = woven.shape[0], gate_weight.shape[0]
    tiles = woven.shape[2] // BLOCK
    share = -(-tiles // ring.chips)

    def part_ways(turn):
        @pl.loop(min(turn * share, tiles), min((turn + 1) * share, tiles))
        def _(tile):
            cut = pl.ds(pl.multiple_of(tile * BLOCK, BLOCK), BLOCK)
            for c, target in enumerate((gate_weight, up_weight)):
                target[used - used % 16 :, cut] = jnp.zeros(
                    (units - used + used % 16, BLOCK), BF16
                )
                target[:used, cut] = woven[:, c, cut]

    work(ring.me)
    ring.from_mate(0)
    work(ring.mate)
    load.wait()
    part_ways(0)
    for hop in range(1, ring.chips):
        ring.advance(hop)
        work(ring.origin(hop))
        ring.from_mate(hop)
        work(ring.mates_origin(hop))
        part_ways(hop)
    ring.finish()
    for device in range(count):
        keep(device).wait()


def project(count, tokens, gains, offsets, weight, bias, expand, units):
    rows, width = tokens.shape
    columns = weight.shape[1]
    total = rows * count
    vmem = pl.BlockSpec(memory_space=pltpu.VMEM)
    return pl.pallas_call(
        functools.partial(project_kernel, count),
        in_specs=[vmem] * 5 + [pl.BlockSpec(memory_space=pl.ANY)],
        out_specs=[vmem] * 3 + [pl.BlockSpec(memory_space=pl.ANY)],
        out_shape=[
            jax.ShapeDtypeStruct((total, columns), F32),
            jax.ShapeDtypeStruct((units, width), BF16),
            jax.ShapeDtypeStruct((units, width), BF16),
            jax.ShapeDtypeStruct((total, width), BF16),
        ],
        scratch_shapes=[pltpu.VMEM((total, width), BF16), pltpu.VMEM(expand.shape, BF16)]
        + ring_sems(count)
        + [pltpu.SemaphoreType.DMA((count,)), pltpu.SemaphoreType.DMA],
        compiler_params=pltpu.CompilerParams(
            collective_id=0, has_side_effects=True, vmem_limit_bytes=48 << 20
        ),
        cost_estimate=pl.CostEstimate(
            flops=2 * total * width * columns, bytes_accessed=total * width * 8, transcendentals=0
        ),
        name="project",
    )(tokens, gains, offsets, weight, bias[None], expand)


class Scatter:
    def __init__(self, ring, give, take, passing, total, sems):
        self.ring, self.give, self.take, self.passing, self.total = ring, give, take, passing, total
        self.give_send, self.give_recv, self.pass_send, self.pass_recv, self.again = sems

    def handed(self, far, half):
        size = self.ring.rows // 2
        part = pl.ds(half * size, size)
        return pltpu.make_async_remote_copy(
            src_ref=self.give.at[far % 2, part, :],
            dst_ref=self.take.at[far, part, :],
            send_sem=self.give_send.at[far, half],
            recv_sem=self.give_recv.at[far, half],
            device_id={"tp": self.ring.mate},
            device_id_type=MESH,
        )

    def passed(self, far, half):
        size = self.ring.rows // 2
        part = pl.ds(half * size, size)
        return pltpu.make_async_remote_copy(
            src_ref=self.passing.at[far, part, :],
            dst_ref=self.passing.at[far - 1, part, :],
            send_sem=self.pass_send.at[far, half],
            recv_sem=self.pass_recv.at[far - 1, half],
            device_id={"tp": self.ring.next},
            device_id_type=MESH,
        )

    def run(self, make, beside=lambda far: None):
        ring = self.ring
        chips, size = ring.chips, ring.rows // 2
        for far in reversed(range(chips)):
            if far < chips - 2:
                for half in range(2):
                    self.handed(far + 2, half).wait_send()
            make(ring.origin(far) + ring.way, self.give.at[far % 2])
            for half in range(2):
                self.handed(far, half).start()
            make(ring.origin(chips - far), self.total)
            beside(far)
            for half in range(2):
                self.handed(far, half).wait_recv()
                if far < chips - 1:
                    self.passed(far + 1, half).wait_recv()

                @pl.loop(0, size // 16)
                def _(row):
                    part = pl.ds(pl.multiple_of(half * size + row * 16, 16), 16)
                    value = self.total[part, :] + self.take[far, part, :].astype(F32)
                    if far < chips - 1:
                        value = value + self.passing[far, part, :].astype(F32)
                    if far > 0:
                        self.passing[far, part, :] = value.astype(BF16)
                    else:
                        self.total[part, :] = value

                if far > 0:
                    self.passed(far, half).start()
        for half in range(2):
            for far in range(chips):
                if far < 2:
                    self.handed(far, half).wait_send()
                if far > 0:
                    self.passed(far, half).wait_send()

    def release(self):
        for other in (self.ring.last, self.ring.mate):
            pl.semaphore_signal(self.again, inc=1, device_id={"tp": other}, device_id_type=MESH)
        pl.semaphore_wait(self.again, 2)


def scatter_space(count, rows, width):
    chips = count // 2
    return [
        pltpu.VMEM((2, rows, width), BF16),
        pltpu.VMEM((chips, rows, width), BF16),
        pltpu.VMEM((chips, rows, width), BF16),
        pltpu.VMEM((rows, width), F32),
    ]


def scatter_sems(count):
    return [pltpu.SemaphoreType.DMA((count // 2, 2))] * 4 + [pltpu.SemaphoreType.REGULAR]


SLOTS = 4
LANDINGS = 3
PIECE = 128
EARLY = 2


class Line:
    def __init__(self, count, pieces, held, came, crossed, sems):
        self.pieces, self.held, self.came, self.crossed = pieces, held, came, crossed
        (
            self.load_sem,
            self.keep_sem,
            self.in_send,
            self.in_recv,
            self.mid_send,
            self.mid_recv,
            self.out_send,
            self.out_recv,
            self.in_free,
            self.mid_free,
        ) = sems
        here = lax.axis_index("dp")
        half = count // 2
        side = here // half
        self.count, self.half = count, half
        self.inner, self.outer = here + 1 - 2 * side, here - 1 + 2 * side
        self.depth = here + side * (count - 1 - 2 * here)
        self.end, self.middle = self.depth == 0, self.depth == half - 1

    def greet(self, barrier):
        pl.semaphore_signal(barrier, inc=1, device_id={"dp": self.inner}, device_id_type=MESH)

        @pl.when(self.depth > 0)
        def _():
            pl.semaphore_signal(barrier, inc=1, device_id={"dp": self.outer}, device_id_type=MESH)

    def met(self, barrier, others):
        @pl.when(self.depth == 0)
        def _():
            pl.semaphore_wait(barrier, others + 1)

        @pl.when(self.depth > 0)
        def _():
            pl.semaphore_wait(barrier, others + 2)

    def rows(self, k):
        return self.pieces[k][0].shape[0]

    def sent(self, source, target, send, recv, to):
        return pltpu.make_async_remote_copy(
            src_ref=source,
            dst_ref=target,
            send_sem=send,
            recv_sem=recv,
            device_id={"dp": to},
            device_id_type=MESH,
        )

    def inward(self, k, source):
        landing = self.came.at[k % LANDINGS, pl.ds(0, self.rows(k)), :]
        return self.sent(source, landing, self.in_send.at[k], self.in_recv.at[k], self.inner)

    def across(self, k):
        part = pl.ds(0, self.rows(k))
        return self.sent(
            self.held.at[k % SLOTS, part, :],
            self.crossed.at[k % LANDINGS, part, :],
            self.mid_send.at[k],
            self.mid_recv.at[k],
            self.inner,
        )

    def outward(self, k, source):
        return self.sent(source, self.pieces[k][1], self.out_send.at[k], self.out_recv.at[k], self.outer)

    def slot(self, k):
        return self.held.at[k % SLOTS, pl.ds(0, self.rows(k)), :]

    def load(self, k):
        return pltpu.make_async_copy(self.pieces[k][0], self.slot(k), self.load_sem.at[k])

    def keep(self, k):
        return pltpu.make_async_copy(self.slot(k), self.pieces[k][1], self.keep_sem.at[k])

    def begin(self, k):
        @pl.when(self.end)
        def _():
            if k >= LANDINGS:
                pl.semaphore_wait(self.in_free, 1)
            self.inward(k, self.pieces[k][0]).start()

    def free(self, k):
        @pl.when(self.middle)
        def _():
            self.outward(k, self.slot(k)).wait_send()
            self.keep(k).wait()

        if self.half > 2:

            @pl.when((self.depth > 0) & (self.depth < self.half - 1))
            def _():
                self.inward(k, self.slot(k)).wait_send()

    def ready(self, k):
        if k >= SLOTS:
            self.free(k - SLOTS)

        @pl.when(self.depth > 0)
        def _():
            self.load(k).start()

    def add(self, k, other):
        slot = self.held.at[k % SLOTS]

        @pl.loop(0, self.rows(k) // 16)
        def _(row):
            part = pl.ds(pl.multiple_of(row * 16, 16), 16)
            slot[part, :] = (
                slot[part, :].astype(F32) + other[k % LANDINGS, part, :].astype(F32)
            ).astype(BF16)

    def join(self, k):
        @pl.when(self.depth > 0)
        def _():
            self.load(k).wait()
            self.inward(k, self.slot(k)).wait_recv()
            self.add(k, self.came)
            if k + LANDINGS < len(self.pieces):
                pl.semaphore_signal(
                    self.in_free, inc=1, device_id={"dp": self.outer}, device_id_type=MESH
                )

        @pl.when(self.middle)
        def _():
            if k >= LANDINGS:
                pl.semaphore_wait(self.mid_free, 1)
            self.across(k).start()

        if self.half > 2:

            @pl.when((self.depth > 0) & (self.depth < self.half - 1))
            def _():
                if k >= LANDINGS:
                    pl.semaphore_wait(self.in_free, 1)
                self.inward(k, self.slot(k)).start()

    def close(self, k):
        @pl.when(self.middle)
        def _():
            self.across(k).wait_recv()
            self.across(k).wait_send()
            self.add(k, self.crossed)
            if k + LANDINGS < len(self.pieces):
                pl.semaphore_signal(
                    self.mid_free, inc=1, device_id={"dp": self.inner}, device_id_type=MESH
                )
            self.outward(k, self.slot(k)).start()
            self.keep(k).start()

    def spread(self, k):
        @pl.when(self.depth < self.half - 1)
        def _():
            self.outward(k, self.pieces[k][1]).wait_recv()

        if self.half > 2:

            @pl.when((self.depth > 0) & (self.depth < self.half - 1))
            def _():
                self.outward(k, self.pieces[k][1]).start()

    def finish(self):
        total = len(self.pieces)
        for k in range(max(0, total - SLOTS), total):
            self.free(k)
        for k in range(total):

            @pl.when(self.end)
            def _():
                self.inward(k, self.pieces[k][0]).wait_send()

            if self.half > 2:

                @pl.when((self.depth > 0) & (self.depth < self.half - 1))
                def _():
                    self.outward(k, self.pieces[k][1]).wait_send()


def line_space(width):
    return [
        pltpu.VMEM((SLOTS, PIECE, width), BF16),
        pltpu.VMEM((LANDINGS, PIECE, width), BF16),
        pltpu.VMEM((LANDINGS, PIECE, width), BF16),
    ]


def line_sems(pieces):
    return [pltpu.SemaphoreType.DMA((pieces,))] * 8 + [pltpu.SemaphoreType.REGULAR] * 2


def piece_rows(start, total):
    return [(start + at, min(PIECE, total - at)) for at in range(0, total, PIECE)]


def middle_kernel(
    count,
    mixed,
    weight,
    tokens,
    gains,
    offsets,
    output_offset,
    gate_weight,
    up_weight,
    columns,
    hidden,
    gate_factor,
    up_factor,
    gathered,
    middle,
    buffer,
    give,
    take,
    passing,
    total,
    *rest,
):
    rows = tokens.shape[0]
    residual_scale = (2.0 * LAYERS) ** 0.5
    ring = Ring(count, rows, buffer, rest[:4])
    scatter = Scatter(ring, give, take, passing, total, rest[4:9])
    out_sem = rest[9]
    pl.semaphore_wait(ring.greet(), 3)

    def make(device, target):
        part = pl.ds(pl.multiple_of(device * rows, rows), rows)

        @pl.loop(0, weight.shape[1] // TILE)
        def _(tile):
            cut = pl.ds(pl.multiple_of(tile * TILE, TILE), TILE)
            target[:, cut] = jnp.dot(
                mixed[part, :], weight[:, cut], preferred_element_type=F32
            ).astype(target.dtype)

    scatter.run(make)
    hat, _ = normalize(tokens[...].astype(F32))
    first = hat * gains[0:1, :] + offsets[0:1, :]
    middle[...] = residual_scale * first + (total[...] + output_offset[...])
    hat, _ = normalize(middle[...])
    own = pl.ds(pl.multiple_of(ring.me * rows, rows), rows)
    buffer[own, :] = (hat * gains[1:2, :] + offsets[1:2, :]).astype(BF16)
    ring.begin()

    def keep(device):
        part = pl.ds(pl.multiple_of(device * rows, rows), rows)
        return pltpu.make_async_copy(buffer.at[part, :], gathered.at[part, :], out_sem.at[device])

    def work(device):
        part = pl.ds(pl.multiple_of(device * rows, rows), rows)
        keep(device).start()

        @pl.loop(0, columns.shape[0] // UNITS)
        def _(step):
            own = pl.ds(pl.multiple_of(step * UNITS, UNITS), UNITS)
            gate = dot(gate_weight[own, :], buffer[part, :], ROWS) + columns[own, 0:1]
            up = dot(up_weight[own, :], buffer[part, :], ROWS) + columns[own, 1:2]
            up = up * columns[own, 2:3]
            normal = 0.5 * (1.0 + lax.erf(gate * (0.5**0.5)))
            density = jnp.exp(-0.5 * gate * gate) * (0.5 / jnp.pi) ** 0.5
            gelu = gate * normal
            hidden[own, part] = (gelu * up).astype(BF16)
            gate_factor[own, part] = (up * (normal + gate * density)).astype(BF16)
            up_factor[own, part] = (gelu * columns[own, 2:3]).astype(BF16)

    work(ring.me)
    ring.from_mate(0)
    work(ring.mate)
    for hop in range(1, ring.chips):
        ring.advance(hop)
        work(ring.origin(hop))
        ring.from_mate(hop)
        work(ring.mates_origin(hop))
    ring.finish()
    for device in range(count):
        keep(device).wait()


def attention_to_feed(
    count, mixed, weight, tokens, gains, offsets, output_offset, gate_weight, up_weight, columns
):
    rows, width = tokens.shape
    units = columns.shape[0]
    total = rows * count
    vmem = pl.BlockSpec(memory_space=pltpu.VMEM)
    return pl.pallas_call(
        functools.partial(middle_kernel, count),
        in_specs=[vmem] * 9,
        out_specs=[vmem] * 3 + [pl.BlockSpec(memory_space=pl.ANY), vmem],
        out_shape=[jax.ShapeDtypeStruct((units, total), BF16)] * 3
        + [jax.ShapeDtypeStruct((total, width), BF16), jax.ShapeDtypeStruct((rows, width), F32)],
        scratch_shapes=[pltpu.VMEM((total, width), BF16)]
        + scatter_space(count, rows, width)
        + ring_sems(count)
        + scatter_sems(count)
        + [pltpu.SemaphoreType.DMA((count,))],
        compiler_params=pltpu.CompilerParams(
            collective_id=1, has_side_effects=True, vmem_limit_bytes=58 << 20
        ),
        cost_estimate=pl.CostEstimate(
            flops=4 * total * width * units,
            bytes_accessed=total * width * 8,
            transcendentals=2 * total * units,
        ),
        name="attention_to_feed",
    )(
        mixed, weight, tokens, gains, offsets, output_offset[None], gate_weight, up_weight, columns
    )


class Stage:
    def __init__(self, slots, sem):
        self.slots, self.sem, self.copies, self.waited = slots, sem, [], set()

    def settle(self, index):
        if index not in self.waited:
            self.copies[index].wait()
            self.waited.add(index)

    def emit(self, work, size, target):
        index = len(self.copies)
        if index >= 2:
            self.settle(index - 2)
        slot = self.slots.at[index % 2, pl.ds(0, size), :]

        @pl.loop(0, slot.shape[1] // TILE)
        def _(tile):
            cut = pl.ds(pl.multiple_of(tile * TILE, TILE), TILE)
            slot[:, cut] = work(cut).astype(BF16)

        copy = pltpu.make_async_copy(slot, target, self.sem.at[index])
        copy.start()
        self.copies.append(copy)
        return index

    def finish(self):
        for index in range(len(self.copies)):
            self.settle(index)


def back_kernel(
    count,
    line_count,
    used,
    hidden,
    shrink,
    gate_weight,
    up_weight,
    output_weight,
    mixed,
    middle,
    cotangent,
    gains,
    cotangent_all,
    second_all,
    gate_factor,
    up_factor,
    grad_mixed,
    grad_middle,
    sums,
    shrink_part,
    expand_part,
    output_part,
    shrink_whole,
    expand_whole,
    grads_out,
    grads,
    buffer,
    factors,
    staged,
    flipped,
    turned_mixed,
    *rest,
):
    rows, width = middle.shape
    units = hidden.shape[0]
    tokens = buffer.shape[0]
    sems = rest[7:]
    big_sem, factor_sem, stage_sem = sems[19:22]
    residual_scale = (2.0 * LAYERS) ** 0.5
    ring = Ring(count, rows, buffer, sems[:4])
    scatter = Scatter(ring, *rest[:4], sems[4:9])
    stage = Stage(staged, stage_sem)
    parts = piece_rows(0, used)
    pieces = [
        (shrink_part.at[pl.ds(a, n), :], shrink_whole.at[pl.ds(a, n), :]) for a, n in parts
    ]
    pieces[-1:] = [
        (expand_part.at[pl.ds(a, n), :], expand_whole.at[pl.ds(a, n), :])
        for a, n in parts[:EARLY]
    ] + pieces[-1:]
    copy_of = lambda k: (
        k if k < len(parts) - 1 else len(parts) - 1 if k == len(pieces) - 1 else k + 1
    )
    line = Line(line_count, pieces, *rest[4:7], sems[9:19])
    barrier = ring.greet()
    line.greet(barrier)
    load = pltpu.make_async_copy(cotangent_all, buffer, big_sem.at[0])
    load.start()

    def factor(block, slot):
        cut = pl.ds(pl.multiple_of(block * BLOCK, BLOCK), BLOCK)
        return [
            pltpu.make_async_copy(from_.at[:, cut], factors.at[slot, c], factor_sem.at[slot, c])
            for c, from_ in enumerate((gate_factor, up_factor))
        ]

    for copy in factor(0, 0):
        copy.start()
    line.met(barrier, 3)
    load.wait()

    def shrink_work(a, n):
        return lambda cut: jnp.dot(
            hidden[a : a + n, :], buffer[:, cut], preferred_element_type=F32
        )

    shrinks = list(parts)

    def emit_shrinks(many):
        for a, n in shrinks[:many]:
            stage.emit(shrink_work(a, n), n, shrink_part.at[pl.ds(a, n), :])
        del shrinks[:many]

    begun = min(LANDINGS, len(parts) - 1)
    emit_shrinks(begun)
    for k in range(begun):
        stage.settle(k)
        if k == 0:
            line.ready(0)
        line.begin(k)

    @pl.loop(0, tokens // BLOCK)
    def _(block):
        slot = block % 2
        for copy in factor(block, slot):
            copy.wait()

        @pl.when(block + 1 < tokens // BLOCK)
        def _():
            for copy in factor(block + 1, 1 - slot):
                copy.start()

        cut = pl.ds(pl.multiple_of(block * BLOCK, BLOCK), BLOCK)

        @pl.loop(0, units // UNITS)
        def _(step):
            own = pl.ds(pl.multiple_of(step * UNITS, UNITS), UNITS)
            grad_hidden = dot(shrink[own, :], buffer[cut, :], ROWS)
            grads[0, own, cut] = (grad_hidden * factors[slot, 0, own, :].astype(F32)).astype(BF16)
            grads[1, own, cut] = (grad_hidden * factors[slot, 1, own, :].astype(F32)).astype(BF16)

    load = pltpu.make_async_copy(second_all, buffer, big_sem.at[1])
    out = pltpu.make_async_copy(grads, grads_out, big_sem.at[2])
    out.start()
    turns, following = list(range(len(pieces) + 1)), list(range(begun, len(pieces)))

    def turn():
        if not turns:
            return
        new = [k for k in following if k <= turns[0] + LANDINGS]
        if any(copy_of(k) >= len(stage.copies) for k in new):
            return
        t = turns.pop(0)
        if t < len(pieces):
            line.join(t)
            if t + 1 < len(pieces):
                stage.settle(copy_of(t + 1))
                line.ready(t + 1)
        if t > 0:
            line.close(t - 1)
        for k in new:
            stage.settle(copy_of(k))
            line.begin(k)
            following.remove(k)

    expands = [(0, a, n) for a, n in parts[:EARLY]]

    def expand_work(c, a, n):
        return lambda cut: jnp.dot(
            grads[c, a : a + n, :], buffer[:, cut], preferred_element_type=F32
        )

    def emit_expands(many):
        for _ in range(min(many, len(expands))):
            c, a, n = expands.pop(0)
            stage.emit(expand_work(c, a, n), n, expand_part.at[pl.ds(a, n), :])

    def make(device, target):
        part = pl.ds(pl.multiple_of(device * rows, rows), rows)
        for c in range(2):
            flipped[c] = grads[c, :, part].T

        @pl.loop(0, width // TILE)
        def _(tile):
            cut = pl.ds(pl.multiple_of(tile * TILE, TILE), TILE)
            target[:, cut] = (
                jnp.dot(flipped[0], gate_weight[:, cut], preferred_element_type=F32)
                + jnp.dot(flipped[1], up_weight[:, cut], preferred_element_type=F32)
            ).astype(target.dtype)

    def beside(far):
        step = ring.chips - 1 - far
        if step < 2:
            emit_shrinks(-(-(len(parts) - begun) // 2))
        if step == 1:
            emit_shrinks(len(shrinks))
            load.start()
        if step == 2:
            load.wait()
            emit_expands(len(expands))
        turn()

    scatter.run(make, beside)
    grad_output = cotangent[...].astype(F32)
    hat, scale = normalize(middle[...])
    grad_in, gain, offset = normalize_back(
        residual_scale * grad_output + scatter.total[...], gains[1:2, :], hat, scale
    )
    grad_middle[...] = grad_in
    scatter.release()
    own = pl.ds(pl.multiple_of(ring.me * rows, rows), rows)
    buffer[own, :] = grad_in.astype(BF16)
    ring.begin()
    sums[0:1, :] = gain[None]
    sums[1:2, :] = offset[None]
    sums[2:3, :] = jnp.sum(grad_middle[...].astype(BF16).astype(F32), axis=0, keepdims=True)
    sums[3:4, :] = jnp.sum(cotangent[...].astype(F32), axis=0, keepdims=True)
    sums[4:8, :] = jnp.zeros((4, width), F32)
    ones = jnp.ones((16, tokens), BF16)
    for c in range(2):
        sums[4 + c : 5 + c, :units] = dot(ones, grads[c], ROWS)[:1]

    summed = scatter.total.at[pl.ds(0, mixed.shape[1]), :]
    summed[...] = jnp.zeros(summed.shape, F32)

    def work(device):
        part = pl.ds(pl.multiple_of(device * rows, rows), rows)
        grad_mixed[part, :] = dot(buffer[part, :], output_weight[...], ROWS).astype(BF16)
        turned_mixed[...] = mixed[part, :].T

        @pl.loop(0, width // TILE)
        def _(tile):
            cut = pl.ds(pl.multiple_of(tile * TILE, TILE), TILE)
            summed[:, cut] += jnp.dot(
                turned_mixed[...], buffer[part, cut], preferred_element_type=F32
            )


    work(ring.me)
    ring.from_mate(0)
    work(ring.mate)
    turn()
    for hop in range(1, ring.chips):
        ring.advance(hop)
        work(ring.origin(hop))
        ring.from_mate(hop)
        work(ring.mates_origin(hop))
        turn()
        if hop > 1:
            turn()
    for a, n in piece_rows(0, mixed.shape[1]):
        stage.emit(
            lambda cut: summed[a : a + n, cut],
            n,
            output_part.at[pl.ds(a, n), :],
        )
    ring.finish()
    for _ in range(len(pieces) + 1):
        turn()
    for k in range(len(pieces)):
        line.spread(k)
    line.finish()
    stage.finish()
    out.wait()


def back(
    count,
    line_count,
    used,
    hidden,
    shrink,
    gate_weight,
    up_weight,
    output_weight,
    mixed,
    middle,
    cotangent,
    gains,
    cotangent_all,
    second_all,
    gate_factor,
    up_factor,
):
    rows, width = middle.shape
    units, total = hidden.shape
    heads = mixed.shape[1]
    vmem, any_ = pl.BlockSpec(memory_space=pltpu.VMEM), pl.BlockSpec(memory_space=pl.ANY)
    parts = piece_rows(0, used)
    pieces = len(parts) + len(parts[:EARLY])
    return pl.pallas_call(
        functools.partial(back_kernel, count, line_count, used),
        in_specs=[vmem] * 9 + [any_] * 4,
        out_specs=[vmem] * 3 + [any_] * 6,
        out_shape=[
            jax.ShapeDtypeStruct((total, heads), BF16),
            jax.ShapeDtypeStruct((rows, width), F32),
            jax.ShapeDtypeStruct((8, width), F32),
            jax.ShapeDtypeStruct((used, width), BF16),
            jax.ShapeDtypeStruct((sum(n for _, n in parts[:EARLY]), width), BF16),
            jax.ShapeDtypeStruct((heads, width), BF16),
            jax.ShapeDtypeStruct((used, width), BF16),
            jax.ShapeDtypeStruct((sum(n for _, n in parts[:EARLY]), width), BF16),
            jax.ShapeDtypeStruct((2, units, total), BF16),
        ],
        scratch_shapes=[
            pltpu.VMEM((2, units, total), BF16),
            pltpu.VMEM((total, width), BF16),
            pltpu.VMEM((2, 2, units, BLOCK), BF16),
            pltpu.VMEM((2, PIECE, width), BF16),
            pltpu.VMEM((2, rows, units), BF16),
            pltpu.VMEM((heads, rows), BF16),
        ]
        + scatter_space(count, rows, width)
        + line_space(width)
        + ring_sems(count)
        + scatter_sems(count)
        + line_sems(pieces)
        + [
            pltpu.SemaphoreType.DMA((3,)),
            pltpu.SemaphoreType.DMA((2, 2)),
            pltpu.SemaphoreType.DMA((pieces + heads // PIECE,)),
        ],
        compiler_params=pltpu.CompilerParams(
            collective_id=2, has_side_effects=True, vmem_limit_bytes=60 << 20
        ),
        cost_estimate=pl.CostEstimate(
            flops=18 * total * width * units, bytes_accessed=total * width * 8, transcendentals=0
        ),
        name="back",
    )(
        hidden,
        shrink,
        gate_weight,
        up_weight,
        output_weight,
        mixed,
        middle,
        cotangent,
        gains,
        cotangent_all,
        second_all,
        gate_factor,
        up_factor,
    )


def blocks_turned(values):
    side = values.shape[0]
    return jnp.concatenate(
        [values[:, at : at + side].T for at in range(0, values.shape[1], side)], axis=1
    )


def tail_kernel(
    count,
    line_count,
    used,
    packed,
    mixed,
    grad_mixed,
    peaks,
    cosine,
    sine,
    low,
    high,
    input_weight,
    hidden,
    shrink,
    middle,
    tokens,
    grad_middle,
    gains,
    offsets,
    shrink_offset,
    early_sums,
    first_all,
    second_all,
    grads,
    output_part,
    layer_out,
    tokens_grad,
    sums,
    expand_part,
    input_part,
    expand_whole,
    output_whole,
    input_whole,
    grad_projected,
    keys_t,
    inner,
    grad_keys,
    grad_values,
    buffer,
    lefts,
    staged,
    group_box,
    line_box,
    *rest,
):
    rows, width = middle.shape
    units = hidden.shape[0]
    seq_count, heads = peaks.shape[0], peaks.shape[1]
    sems = rest[7:]
    big_sem, left_sem, stage_sem = sems[15:18]
    residual_scale = (2.0 * LAYERS) ** 0.5
    ring = Ring(count, rows, None, [None] * 4)
    scatter = Scatter(ring, *rest[:4], sems[:5])
    stage = Stage(staged, stage_sem)
    expands = [(c, a, n) for c in range(2) for a, n in piece_rows(0, used)[EARLY if c == 0 else 0 :]]
    short = [e for e in expands if e[2] < PIECE]
    expands = [e for e in expands if e[2] == PIECE] + short
    lasts = piece_rows(0, grad_projected.shape[1])
    outs = piece_rows(0, output_part.shape[0])
    pieces = (
        [(output_part.at[pl.ds(a, n), :], output_whole.at[pl.ds(a, n), :]) for a, n in outs]
        + [
            (
                expand_part.at[pl.ds(c * units + a, n), :],
                expand_whole.at[pl.ds(c * units + a, n), :],
            )
            for c, a, n in expands
        ]
        + [(input_part.at[pl.ds(a, n), :], input_whole.at[pl.ds(a, n), :]) for a, n in lasts]
    )
    ahead = len(outs)
    full = ahead + len(expands) - len(short)
    tail_order = pieces[full : full + len(short)]
    pieces = pieces[:full] + pieces[full + len(short) :] + tail_order
    line = Line(line_count, pieces, *rest[4:7], sems[5:15])
    me, here = ring.me, lax.axis_index("dp")
    barrier = pltpu.get_barrier_semaphore()
    for axis, place, size in (("tp", me, count), ("dp", here, line_count)):
        for i in range(1, size):
            pl.semaphore_signal(
                barrier, inc=1, device_id={axis: (place + i) % size}, device_id_type=MESH
            )
    load = pltpu.make_async_copy(second_all, buffer, big_sem.at[0])
    load.start()

    def left(e):
        c, a, n = expands[e]
        return pltpu.make_async_copy(
            grads.at[c, pl.ds(a, n), :], lefts.at[e % 2, pl.ds(0, n), :], left_sem.at[e]
        )

    left(0).start()
    line.ready(0)
    pl.semaphore_wait(barrier, count + line_count - 2)
    done = [0]

    def copy_of(k):
        if k < full:
            return k - ahead
        if k < full + len(lasts):
            return k - full + len(expands)
        return k - len(lasts) - ahead


    def emit():
        e = done[0]
        if e == len(expands):
            return
        done[0] += 1
        left(e).wait()
        if e + 1 < len(expands):
            left(e + 1).start()
        n = expands[e][2]
        stage.emit(
            lambda cut: jnp.dot(
                lefts[e % 2, pl.ds(0, n), :], buffer[:, cut], preferred_element_type=F32
            ),
            n,
            expand_part.at[pl.ds(expands[e][0] * units + expands[e][1], n), :],
        )

    def there(k):
        if k >= ahead:
            while copy_of(k) >= len(stage.copies) and done[0] < len(expands):
                emit()
            stage.settle(copy_of(k))

    turns = list(range(len(pieces) + 1))

    def turn():
        if not turns:
            return
        new = [k for k in following if k <= turns[0] + LANDINGS]
        for k in new:
            late = full <= k < full + len(lasts)
            if k >= ahead and copy_of(k) >= len(stage.copies):
                if late or done[0] == len(expands):
                    return
        t = turns.pop(0)
        if t < len(pieces):
            line.join(t)
            if t + 1 < len(pieces):
                there(t + 1)
                line.ready(t + 1)
        if t > 0:
            line.close(t - 1)
        for k in new:
            there(k)
            line.begin(k)
            following.remove(k)

    following = list(range(LANDINGS, len(pieces)))
    for k in range(min(ahead, LANDINGS)):
        line.begin(k)
    load.wait()
    for k in range(ahead, LANDINGS):
        there(k)
        line.begin(k)

    for s in range(seq_count):
        for h in range(heads):
            span = pl.ds(s * SEQ_LEN, SEQ_LEN)
            head = pl.ds(h * HEAD_DIM, HEAD_DIM)
            three = pl.ds(h * 3 * HEAD_DIM, 3 * HEAD_DIM)
            attend_back(
                packed.at[span, three],
                mixed.at[span, head],
                grad_mixed.at[span, head],
                peaks.at[s, h],
                cosine.at[s],
                sine.at[s],
                low.at[s],
                high.at[s],
                grad_projected.at[span, three],
                keys_t,
                inner,
                grad_keys,
                grad_values,
            )
            emit()
            turn()
            emit()

    while done[0] < len(expands):
        emit()
    load = pltpu.make_async_copy(first_all, buffer, big_sem.at[1])
    load.start()
    load.wait()
    inputs = list(lasts)

    def emit_input():
        if inputs:
            a, n = inputs.pop(0)
            stage.emit(
                lambda cut: blocks_turned(dot(grad_projected[:, a : a + n], buffer[:, cut], COLS)),
                n,
                input_part.at[pl.ds(a, n), :],
            )

    def between(far):
        emit_input()
        turn()
        emit_input()

    def make(device, target):
        part = pl.ds(pl.multiple_of(device * rows, rows), rows)

        @pl.loop(0, width // TILE)
        def _(tile):
            cut = pl.ds(pl.multiple_of(tile * TILE, TILE), TILE)
            target[:, cut] = dot(grad_projected[part, :], input_weight[cut, :], ROWS).astype(
                target.dtype
            )

    scatter.run(make, between)
    while inputs:
        emit_input()
    hat, scale = normalize(tokens[...].astype(F32))
    grad_in, gain, offset = normalize_back(
        residual_scale * grad_middle[...] + scatter.total[...], gains[0:1, :], hat, scale
    )
    scatter.total[...] = grad_in
    keep = pltpu.make_async_copy(scatter.total, tokens_grad, big_sem.at[2])
    keep.start()
    small = group_box.at[me]
    small[0:1, :] = gain[None]
    small[1:2, :] = early_sums[0:1, :]
    small[2:3, :] = offset[None]
    small[3:4, :] = early_sums[1:2, :]
    small[4:6, :] = early_sums[2:4, :]
    small[6:8, :] = early_sums[4:6, :]
    scatter.release()
    turn()
    wide = grad_projected.shape[1]
    small[6:7, width - wide :] = jnp.dot(
        jnp.ones((16, grad_projected.shape[0]), BF16),
        grad_projected[...],
        preferred_element_type=F32,
    )[:1]

    def swaps(box, axis, place, size, send, recv):
        return [
            pltpu.make_async_remote_copy(
                src_ref=box.at[place],
                dst_ref=box.at[place],
                send_sem=send.at[i],
                recv_sem=recv.at[i],
                device_id={axis: (place + i) % size},
                device_id_type=MESH,
            )
            for i in range(1, size)
        ]

    group_swaps = swaps(group_box, "tp", me, count, *sems[18:20])
    line_swaps = swaps(line_box, "dp", here, line_count, *sems[20:22])
    for copy in group_swaps:
        copy.start()
    turn()

    def make_out(device, target):
        part = pl.ds(pl.multiple_of(device * rows, rows), rows)

        @pl.loop(0, width // TILE)
        def _(tile):
            cut = pl.ds(pl.multiple_of(tile * TILE, TILE), TILE)
            target[:, cut] = dot(hidden[:, part], shrink[:, cut], COLS).astype(target.dtype)

    keep.wait()
    scatter.run(make_out, lambda far: turn())
    hat, _ = normalize(middle[...])
    scatter.total[...] = (
        residual_scale * (hat * gains[1:2, :] + offsets[1:2, :])
        + scatter.total[...]
        + shrink_offset[...]
    )
    keep = pltpu.make_async_copy(scatter.total, layer_out, big_sem.at[3])
    keep.start()
    turn()
    for copy in group_swaps:
        copy.wait()
    line_box[here, 0:6, :] = sum(group_box[d, 0:6, :] for d in range(count))
    line_box[here, 6:8, :] = small[6:8, :]
    for copy in line_swaps:
        copy.start()
    for _ in range(len(pieces) + 1):
        turn()
    for copy in line_swaps:
        copy.wait()
    sums[...] = sum(line_box[d] for d in range(line_count))
    for k in range(len(pieces)):
        line.spread(k)
    line.finish()
    stage.finish()
    keep.wait()


def tail(
    count,
    line_count,
    used,
    packed,
    mixed,
    grad_mixed,
    peaks,
    cosine,
    sine,
    low,
    high,
    input_weight,
    hidden,
    shrink,
    middle,
    tokens,
    grad_middle,
    gains,
    offsets,
    shrink_offset,
    early_sums,
    first_all,
    second_all,
    grads,
    output_part,
):
    rows, width = middle.shape
    units, total = hidden.shape
    columns = packed.shape[1]
    heads = output_part.shape[0]
    vmem, any_ = pl.BlockSpec(memory_space=pltpu.VMEM), pl.BlockSpec(memory_space=pl.ANY)
    parts, lasts = piece_rows(0, used), len(piece_rows(0, columns))
    expands = len(parts[EARLY:]) + len(parts)
    pieces = expands + len(piece_rows(0, heads)) + lasts
    blocks = SEQ_LEN // BLOCK
    return pl.pallas_call(
        functools.partial(tail_kernel, count, line_count, used),
        in_specs=[vmem] * 18 + [any_] * 4,
        out_specs=[any_] * 2 + [vmem] + [any_] * 5,
        out_shape=[
            jax.ShapeDtypeStruct((rows, width), F32),
            jax.ShapeDtypeStruct((rows, width), F32),
            jax.ShapeDtypeStruct((8, width), F32),
            jax.ShapeDtypeStruct((2 * units, width), BF16),
            jax.ShapeDtypeStruct((columns, width), BF16),
            jax.ShapeDtypeStruct((2 * units, width), BF16),
            jax.ShapeDtypeStruct((heads, width), BF16),
            jax.ShapeDtypeStruct((columns, width), BF16),
        ],
        scratch_shapes=[
            pltpu.VMEM((total, columns), BF16),
            pltpu.VMEM((blocks, HEAD_DIM, BLOCK), BF16),
            pltpu.VMEM((blocks, 1, BLOCK), F32),
            pltpu.VMEM((SEQ_LEN, HEAD_DIM), F32),
            pltpu.VMEM((SEQ_LEN, HEAD_DIM), F32),
            pltpu.VMEM((total, width), BF16),
            pltpu.VMEM((2, PIECE, width), BF16),
            pltpu.VMEM((2, PIECE, width), BF16),
            pltpu.VMEM((count, 8, width), F32),
            pltpu.VMEM((line_count, 8, width), F32),
        ]
        + scatter_space(count, rows, width)
        + line_space(width)
        + scatter_sems(count)
        + line_sems(pieces)
        + [
            pltpu.SemaphoreType.DMA((4,)),
            pltpu.SemaphoreType.DMA((expands,)),
            pltpu.SemaphoreType.DMA((expands + lasts,)),
        ]
        + [pltpu.SemaphoreType.DMA((count,))] * 2
        + [pltpu.SemaphoreType.DMA((line_count,))] * 2,
        compiler_params=pltpu.CompilerParams(
            collective_id=3, has_side_effects=True, vmem_limit_bytes=60 << 20
        ),
        cost_estimate=pl.CostEstimate(
            flops=4 * total * width * (columns + units),
            bytes_accessed=total * width * 8,
            transcendentals=0,
        ),
        name="tail",
    )(
        packed,
        mixed,
        grad_mixed,
        peaks,
        cosine,
        sine,
        low[:, None],
        high[:, None],
        input_weight,
        hidden,
        shrink,
        middle,
        tokens,
        grad_middle,
        gains,
        offsets,
        shrink_offset[None],
        early_sums,
        first_all,
        second_all,
        grads,
        output_part,
    )


def finish_kernel(early, gate, up, shrink, output, inputs, expand_out, shrink_out, output_out, input_out):
    rows, ahead = expand_out.shape[0], early.shape[0]
    expand_out[:ahead, 0, :] = early[...].astype(F32)
    expand_out[ahead:, 0, :] = gate[ahead:rows, :].astype(F32)
    expand_out[:, 1, :] = up[:rows, :].astype(F32)
    shrink_out[...] = shrink[:rows, :].astype(F32)
    output_out[...] = output[...].astype(F32)
    for at in range(0, inputs.shape[0], PIECE):
        for cut in range(0, inputs.shape[1], PIECE):
            input_out[cut : cut + PIECE, at : at + PIECE] = inputs[
                at : at + PIECE, cut : cut + PIECE
            ].astype(F32)


def finish(early, both, shrink, output, inputs, rows):
    units, width = both.shape[0] // 2, both.shape[1]
    columns, heads = inputs.shape[0], output.shape[0]
    tile = 256
    part = lambda a: pl.BlockSpec((a.shape[0], tile), lambda j: (0, j))
    return pl.pallas_call(
        finish_kernel,
        grid=(width // tile,),
        in_specs=[
            part(early),
            pl.BlockSpec((units, tile), lambda j: (0, j)),
            pl.BlockSpec((units, tile), lambda j: (1, j)),
            part(shrink),
            part(output),
            part(inputs),
        ],
        out_specs=[
            pl.BlockSpec((rows, 2, tile), lambda j: (0, 0, j)),
            pl.BlockSpec((rows, tile), lambda j: (0, j)),
            pl.BlockSpec((heads, tile), lambda j: (0, j)),
            pl.BlockSpec((tile, columns), lambda j: (j, 0)),
        ],
        out_shape=[
            jax.ShapeDtypeStruct((rows, 2, width), F32),
            jax.ShapeDtypeStruct((rows, width), F32),
            jax.ShapeDtypeStruct((heads, width), F32),
            jax.ShapeDtypeStruct((width, columns), F32),
        ],
        compiler_params=pltpu.CompilerParams(vmem_limit_bytes=40 << 20),
        cost_estimate=pl.CostEstimate(
            flops=0, bytes_accessed=6 * width * (3 * rows + heads + columns), transcendentals=0
        ),
        name="finish",
    )(early, both, both, shrink, output, inputs)


def local(
    dp,
    tp,
    tokens,
    segment_ids,
    prefix_lengths,
    positions,
    norm_gains,
    norm_offsets,
    input_weight,
    input_offset,
    output_weight,
    output_offset,
    expand_weight,
    expand_offset,
    shrink_weight,
    shrink_offset,
    cotangent,
):
    seq_count = segment_ids.shape[0]
    units_used = expand_weight.shape[2]
    units = -(-units_used // UNITS) * UNITS
    used = -(-units_used // 16) * 16

    pad = ((0, units - units_used), (0, 0))
    turned_expand = jnp.transpose(expand_weight, (2, 1, 0))
    shrink = jnp.pad(shrink_weight, pad)
    unit_index = lax.axis_index("tp") * units_used + lax.iota(jnp.int32, units_used)
    keep_units = (unit_index < FF_USED).astype(F32)
    columns = jnp.pad(jnp.stack([expand_offset[0], expand_offset[1], keep_units], axis=1), pad)

    row_at = lax.broadcasted_iota(jnp.int32, positions.shape, 1)
    low = row_at - positions
    matches = segment_ids[:, :, None] == lax.iota(jnp.int32, prefix_lengths.shape[1])
    own_prefix = jnp.sum(jnp.where(matches, prefix_lengths[:, None, :], 0), axis=2)
    high = jnp.maximum(row_at, low + own_prefix - 1)
    bounds = jnp.stack(
        [
            jnp.min(low.reshape(seq_count, -1, BLOCK), axis=2) // BLOCK,
            jnp.max(high.reshape(seq_count, -1, BLOCK), axis=2) // BLOCK + 1,
        ],
        axis=2,
    )
    cosine, sine = rotary_tables(positions)

    projected, gate_weight, up_weight, first_all = project(
        tp,
        tokens,
        norm_gains[:1],
        norm_offsets[:1],
        input_weight,
        input_offset,
        turned_expand,
        units,
    )
    waiting, first_all = lax.optimization_barrier((cotangent, first_all))
    cotangent_all = lax.all_gather(waiting, "tp", axis=0, tiled=True)
    packed, mixed, peaks = attend_forward(projected, cosine, sine, low, high, bounds)
    hidden, gate_factor, up_factor, second_all, middle = attention_to_feed(
        tp,
        mixed,
        output_weight,
        tokens,
        norm_gains,
        norm_offsets,
        output_offset,
        gate_weight,
        up_weight,
        columns,
    )

    grad_mixed, grad_middle, sums, _, _, output_part, shrink_whole, expand_early, grads = back(
        tp,
        dp,
        used,
        hidden,
        shrink,
        gate_weight,
        up_weight,
        output_weight,
        mixed,
        middle,
        cotangent,
        norm_gains,
        cotangent_all,
        second_all,
        gate_factor,
        up_factor,
    )
    layer_out, tokens_grad, small_sums, _, _, expand_whole, output_whole, input_whole = tail(
        tp,
        dp,
        used,
        packed,
        mixed,
        grad_mixed,
        peaks,
        cosine,
        sine,
        low,
        high,
        input_weight,
        hidden,
        shrink,
        middle,
        tokens,
        grad_middle,
        norm_gains,
        norm_offsets,
        shrink_offset,
        sums,
        first_all,
        second_all,
        grads,
        output_part,
    )

    expand_grad, shrink_grad, output_grad, input_grad = finish(
        expand_early, expand_whole, shrink_whole, output_whole, input_whole, units_used
    )
    return (
        layer_out,
        tokens_grad,
        input_grad,
        small_sums[6, small_sums.shape[1] - input_weight.shape[1] :],
        output_grad,
        small_sums[4],
        jnp.transpose(expand_grad, (2, 1, 0)),
        small_sums[6:8, :units_used],
        shrink_grad,
        small_sums[5],
        small_sums[0:2],
        small_sums[2:4],
    )


def solution(mesh):
    in_specs = (
        P(("dp", "tp"), None),
        P("dp", None),
        P("dp", None),
        P("dp", None),
        P(),
        P(),
        P(None, "tp"),
        P("tp"),
        P("tp", None),
        P(),
        P(None, None, "tp"),
        P(None, "tp"),
        P("tp", None),
        P(),
        P(("dp", "tp"), None),
    )
    out_specs = (
        P(("dp", "tp"), None),
        P(("dp", "tp"), None),
        P(None, "tp"),
        P("tp"),
        P("tp", None),
        P(),
        P(None, None, "tp"),
        P(None, "tp"),
        P("tp", None),
        P(),
        P(),
        P(),
    )
    return jax.shard_map(
        functools.partial(local, mesh.shape["dp"], mesh.shape["tp"]),
        mesh=mesh,
        in_specs=in_specs,
        out_specs=out_specs,
        check_vma=False,
    )
```
